32 devices in a mesh: dom: 32 (over z, y, x, core).
Axes of the slice: x: 2, y: 2, z: 4, core: 2. Of those that a mesh axis runs over, the one named last changes fastest.
Arguments:
- hidden: bfloat16 [49152, 1024], P('dom'), may hold values from -6 to 6
- bases: bfloat16 [1024, 1224], replicated, may hold values from -0.1875 to 0.1875
- self_weight: bfloat16 [1024, 153], replicated, may hold values from -0.1875 to 0.1875
- coef: float32 [5, 8], replicated, may hold values from -3 to 3
- bias: float32 [153], replicated, may hold values from -3 to 3
- edge_src: int32 [196608], P('dom'), may hold values from 0 to 1535
- edge_dst: int32 [196608], P('dom'), may hold values from 0 to 1535
- edge_rel: int32 [196608], P('dom'), may hold values from 0 to 4
- send_rows: int32 [32, 32, 72], P('dom'), may hold values from 0 to 1536, as said below
- recv_rows: int32 [32, 32, 72], P('dom'), may hold values from 0 to 1536, as said below
- labels: int32 [49152], P('dom'), may hold values from 0 to 152
- train_mask: int32 [49152], P('dom'), may hold values from 0 to 1, as said below
- bnd_rows: int32 [32, 32, 8], P('dom'), may hold values from 0 to 1536, as said below
- tiles: float32 [1536, 128, 128], P('dom'), may hold values from 0 to 0.003515625
- tile_cols: int32 [1536], P('dom'), may hold values from 0 to 13, as said below
Outputs:
- smoothed: float32 [49152, 153], P('dom')
The draws below stay inside these ranges and needn't reach their ends.
Inputs may be any that keep to these rules, and one draw needn't show every extreme that they name: `send_rows`: entries below 1536 are rows of the sending partition and come first in each block; 1536 marks an empty slot. Every row of a partition is sent exactly once over all peers, and one peer of every partition receives a full block of 72. The slot k of recv_rows[d, s] receives the row in slot k of send_rows[s, d]; its entries below 1536 are rows of d, each row of d named exactly once over all s; 1536 marks an empty slot, exactly where the matching send slot is empty. `bnd_rows`: entries below 1536 are rows of the sending partition; 1536 marks an empty slot. Every partition fills all 8 slots for one peer. `train_mask`: every partition holds at least one known label. `tile_cols`: A partition's tiles come in order of row blocks, 4 to a block; the first 2 of a block name local column blocks (below 12), the others halo column blocks; every halo column block is named in every partition.
All inputs are finite; a program needn't handle non-finite values. Where the reference program divides by a largest or mean magnitude, that divisor is 1e-20 or more.
Results may differ from the reference program's by a relative error of at most 0.0003.
Values sent between devices are 32-bit elements; how exact they have to be, the bound alone decides.
No kernel may reach another device: no remote copies, remote signals or barrier semaphores. Data moves between devices by JAX's collectives and lax.ppermute only.
A program may use at most 128 MiB of HBM per device.

```python
import jax
import jax.numpy as jnp
from jax import lax

H = 1024
C = 153
NB = 8
REL = 5
ND = 1536
TB = 128
BND = 8
TILES_ROW = 4
LOC_ROW = 2
ITERS = 3
NPART = 32
NTOT = 49152
EDGES = 6144
SLOT = 72
NT = 48


def relay_plan(key):
    keys = jax.random.split(jax.random.fold_in(key, 101), 5)
    per = ND // NPART
    spread = per // 2
    order = jnp.arange(NPART, dtype=jnp.int32)
    lifts = jax.random.randint(keys[0], (NPART,), 0, spread - 1)
    shift = jax.random.randint(keys[1], (), 0, NPART)
    lifts = lifts.at[shift].set(spread - 2).at[(shift + 1) % NPART].set(0)
    swing = lifts - jnp.roll(lifts, -1)
    offset = (order[None, :] - order[:, None]) % NPART
    cycle = jax.random.permutation(keys[2], NPART).astype(jnp.int32)
    place = jnp.zeros((NPART,), jnp.int32).at[cycle].set(order)
    first = (order + shift) % NPART
    second = cycle[(place[first] + 1) % NPART]
    sizes = per + swing[offset] + 2 * (order[None, :] == first[:, None]).astype(jnp.int32) - 2 * (order[None, :] == second[:, None]).astype(jnp.int32)
    slot = jnp.arange(SLOT, dtype=jnp.int32)
    send_perm = jax.vmap(lambda k: jax.random.permutation(k, ND))(jax.random.split(keys[3], NPART)).astype(jnp.int32)
    start = jnp.cumsum(sizes, axis=1) - sizes
    spots = jnp.clip(start[:, :, None] + slot, 0, ND - 1).reshape(NPART, NPART * SLOT)
    picked = jnp.take_along_axis(send_perm, spots, axis=1).reshape(NPART, NPART, SLOT)
    send = jnp.where(slot < sizes[:, :, None], picked, ND)
    flipped = sizes.T
    recv_perm = jax.vmap(lambda k: jax.random.permutation(k, ND))(jax.random.split(keys[4], NPART)).astype(jnp.int32)
    rstart = jnp.cumsum(flipped, axis=1) - flipped
    rspots = jnp.clip(rstart[:, :, None] + slot, 0, ND - 1).reshape(NPART, NPART * SLOT)
    landed = jnp.take_along_axis(recv_perm, rspots, axis=1).reshape(NPART, NPART, SLOT)
    recv = jnp.where(slot < flipped[:, :, None], landed, ND)
    return (send.astype(jnp.int32), recv.astype(jnp.int32))


def draw_send_rows(key, part):
    return relay_plan(key)[0]


def draw_recv_rows(key, part):
    return relay_plan(key)[1]


def draw_train_mask(key, part):
    keys = jax.random.split(jax.random.fold_in(key, 303), 2)
    rows = jnp.arange(NPART * ND, dtype=jnp.int32)
    owner = rows // ND
    chance = jax.random.randint(keys[0], (NPART * ND,), 0, 8 * (NPART - 1)) < NPART - 1 + 2 * owner
    forced = jax.random.randint(keys[1], (NPART,), 0, ND)
    hit = rows % ND == forced[owner]
    return (chance | hit).astype(jnp.int32)


def draw_bnd_rows(key, part):
    keys = jax.random.split(jax.random.fold_in(key, 202), 3)
    rows = jax.random.randint(keys[0], (NPART, NPART, BND), 0, ND)
    live = jax.random.randint(keys[1], (NPART, NPART, BND), 0, 3) > 0
    pick = jax.random.randint(keys[2], (), 0, NPART)
    order = jnp.arange(NPART, dtype=jnp.int32)
    full = (order[None, :] == (order[:, None] + pick) % NPART)[:, :, None]
    return jnp.where(live | full, rows, ND).astype(jnp.int32)


def draw_tile_cols(key, part):
    keys = jax.random.split(jax.random.fold_in(key, 404), 3)
    local_blocks = ND // TB
    halo_blocks = NPART * BND // TB
    near = jax.random.randint(keys[0], (NPART, local_blocks, LOC_ROW), 0, local_blocks)
    far = local_blocks + jax.random.randint(keys[1], (NPART, local_blocks, TILES_ROW - LOC_ROW - 1), 0, halo_blocks)
    lead = jax.random.randint(keys[2], (NPART, 1), 0, halo_blocks)
    cover = local_blocks + (jnp.arange(local_blocks, dtype=jnp.int32)[None, :] + lead) % halo_blocks
    return jnp.concatenate([near, far, cover[:, :, None]], 2).reshape(-1).astype(jnp.int32)


def plant(result, stream_key, low, largest):
    spot = [jax.random.randint(jax.random.fold_in(stream_key, axis), (), 0, length) for axis, length in enumerate(result.shape)]
    longest = result.shape.index(max(result.shape))
    beside = spot[:longest] + [(spot[longest] + 1) % result.shape[longest]] + spot[longest + 1:]
    return result.at[tuple(spot)].set(low).at[tuple(beside)].set(largest)


def level_of(rng, shape, pieces, least, high):
    def one(position, parts):
        steps = jax.random.uniform(jax.random.fold_in(jax.random.fold_in(rng, 6), position), (parts,), jnp.float32, least / len(pieces), high / len(pieces))
        return jnp.repeat(jnp.exp(steps), shape[position] // parts).reshape((-1,) + (1,) * (len(shape) - position - 1))

    level = one(*pieces[0])
    for cut in pieces[1:]:
        level = level * one(*cut)
    return level


def scatter_about(key, extent, scale, bound, cuts=(), held_as=jnp.bfloat16):
    result = scale * jax.random.normal(key, extent, jnp.float32)
    if cuts:
        result = result * level_of(key, extent, cuts, -0.22, 0.18)
    return jnp.clip(result, -bound, bound).astype(held_as)


def setup_inputs(seed: int = 0) -> dict:
    seeds = jax.random.split(jax.random.key(seed), 16)
    return {
        "hidden": scatter_about(seeds[0], (NTOT, H), 1.0, 6.0, ((0, 32),)),
        "bases": scatter_about(seeds[1], (H, NB * C), H ** -0.5, 0.1875),
        "self_weight": scatter_about(seeds[2], (H, C), H ** -0.5, 0.1875),
        "coef": scatter_about(seeds[3], (REL, NB), 0.5, 3.0, (), jnp.float32),
        "bias": scatter_about(seeds[4], (C,), 0.5, 3.0, (), jnp.float32),
        "edge_src": plant(jax.random.randint(seeds[5], (NPART * EDGES,), 0, ND), jax.random.fold_in(seeds[5], 1), 0, ND - 1).astype(jnp.int32),
        "edge_dst": plant(jax.random.randint(seeds[6], (NPART * EDGES,), 0, ND), jax.random.fold_in(seeds[6], 1), 0, ND - 1).astype(jnp.int32),
        "edge_rel": plant(jax.random.randint(seeds[7], (NPART * EDGES,), 0, REL), jax.random.fold_in(seeds[7], 1), 0, REL - 1).astype(jnp.int32),
        "send_rows": draw_send_rows(jax.random.fold_in(seeds[15], 71), 0),
        "recv_rows": draw_recv_rows(jax.random.fold_in(seeds[15], 71), 0),
        "labels": plant(jax.random.randint(seeds[10], (NTOT,), 0, C), jax.random.fold_in(seeds[10], 1), 0, C - 1).astype(jnp.int32),
        "train_mask": draw_train_mask(jax.random.fold_in(seeds[15], 71), 0),
        "bnd_rows": draw_bnd_rows(jax.random.fold_in(seeds[15], 71), 0),
        "tiles": jnp.clip(0.003515625 * jax.random.uniform(seeds[13], (NPART * NT, TB, TB), jnp.float32) ** level_of(seeds[13], (NPART * NT, TB, TB), ((0, 32),), -0.2, 0.2), 0.0, 0.003515625),
        "tile_cols": draw_tile_cols(jax.random.fold_in(seeds[15], 71), 0),
    }


correct_rate = 0.8
smooth_rate = 0.75
tiny = 1e-6


def device_scores(hid, src, dst, rel, bases, self_weight, coef, bias):
    nrow = hid.shape[0]
    proj = jnp.dot(hid, bases, preferred_element_type=jnp.float32).reshape(nrow, NB, C)
    mixed = jnp.einsum("nbc,rb->rnc", proj, coef.astype(jnp.float32), precision=lax.Precision.HIGHEST)
    msgs = mixed[rel, src]
    segment = dst * REL + rel
    counts = jax.ops.segment_sum(jnp.ones(src.shape, jnp.float32), segment, num_segments=nrow * REL)
    weight = 1.0 / counts[segment]
    agg = jax.ops.segment_sum(msgs * weight[:, None], dst, num_segments=nrow)
    return jnp.dot(hid, self_weight, preferred_element_type=jnp.float32) + agg + bias


def tile_product(state_d, halo_d, tiles_d, cols_d):
    whole = jnp.concatenate([state_d, halo_d], 0).reshape(-1, TB, C)
    picked = whole[cols_d]
    prod = jnp.einsum("tij,tjc->tic", tiles_d, picked, precision=lax.Precision.HIGHEST)
    return prod.reshape(ND // TB, TILES_ROW, TB, C).sum(1).reshape(ND, C)


def propagate(state, bnd_rows, tiles_all, cols_all):
    ids = jnp.arange(NPART, dtype=jnp.int32)
    padded = jnp.concatenate([state, jnp.zeros((NPART, 1, C), jnp.float32)], 1)
    sent = padded[ids[:, None, None], bnd_rows]
    halo = jnp.transpose(sent, (1, 0, 2, 3)).reshape(NPART, NPART * BND, C)
    return lax.map(lambda xs: tile_product(xs[0], xs[1], xs[2], xs[3]), (state, halo, tiles_all, cols_all))


def reference(hidden, bases, self_weight, coef, bias, edge_src, edge_dst, edge_rel, send_rows, recv_rows, labels, train_mask, bnd_rows, tiles, tile_cols):
    ids = jnp.arange(NPART, dtype=jnp.int32)
    scores = lax.map(lambda xs: device_scores(xs[0], xs[1], xs[2], xs[3], bases, self_weight, coef, bias),
                     (hidden.reshape(NPART, ND, H), edge_src.reshape(NPART, EDGES),
                      edge_dst.reshape(NPART, EDGES), edge_rel.reshape(NPART, EDGES)))
    padded = jnp.concatenate([scores, jnp.zeros((NPART, 1, C), jnp.float32)], 1)
    sent = padded[ids[:, None, None], send_rows]
    moved = jnp.transpose(sent, (1, 0, 2, 3))
    base = jnp.zeros((NPART, ND + 1, C), jnp.float32).at[ids[:, None, None], recv_rows].set(moved)[:, :ND]
    tiles_all = tiles.reshape(NPART, NT, TB, TB)
    cols_all = tile_cols.reshape(NPART, NT)
    onehot = (labels.reshape(NPART, ND)[..., None] == jnp.arange(C, dtype=jnp.int32)).astype(jnp.float32)
    known = train_mask.reshape(NPART, ND)[..., None].astype(jnp.float32)
    error0 = known * (onehot - base)
    sigma = jnp.sum(jnp.mean(jnp.abs(error0), -1)) / jnp.sum(known)
    carried = error0
    for step in range(ITERS):
        carried = (1.0 - correct_rate) * error0 + correct_rate * propagate(carried, bnd_rows, tiles_all, cols_all)
    magnitude = jnp.mean(jnp.abs(carried), -1, keepdims=True) + tiny
    corrected = base + sigma * carried / magnitude
    start = known * onehot + (1.0 - known) * corrected
    smoothed = start
    for step in range(ITERS):
        smoothed = (1.0 - smooth_rate) * start + smooth_rate * propagate(smoothed, bnd_rows, tiles_all, cols_all)
    return smoothed.reshape(NTOT, C)
```

```python
import functools

import jax
import jax.numpy as jnp
from jax import lax
from jax.experimental import pallas as pl
from jax.experimental.pallas import tpu as pltpu
from jax.sharding import PartitionSpec as P

TILES_ROW = 4
LOC_ROW = 2
ITERS = 3
L = 128

correct_rate = 0.8
smooth_rate = 0.75
tiny = 1e-06

F32 = jnp.float32
BF16 = jnp.bfloat16
VM = pl.BlockSpec(memory_space=pltpu.VMEM)
SM = pl.BlockSpec(memory_space=pltpu.SMEM)
MIB = 1 << 20


def up(a, b):
    return -(-a // b)


def split(x):
    hi = x.astype(BF16)
    return hi, (x - hi.astype(F32)).astype(BF16)


def dot(a, b):
    return jnp.dot(a, b, preferred_element_type=F32)


def lanes(rows):
    return lax.broadcasted_iota(jnp.int32, (rows, L), 1)


def pair(ref, row):
    return ref.at[pl.ds(pl.multiple_of(2 * row, 2), 2), :]


def gather_rows(idx_ref, src, stg, peers, slots):
    def body(p, _):
        for k in range(slots):
            row = idx_ref[0, p, k]
            pair(stg, p * slots + k)[...] = pair(src, row)[...]
        return 0

    lax.fori_loop(0, peers, body, 0)


def scores_kernel(
    hid, bases, self_w, bias, coef, es, ed, er, send, out,
    whi, wlo, m2, s0, s1, sc2, stg, kv, ks, sem, *, classes, slots, per, blk,
):
    n, hdim = hid.shape
    rest = classes - L
    nrel, nb = coef.shape
    peers = out.shape[0]
    erows = es.shape[0]
    kv[0] = (er[...] * n + es[...]) * 2
    kv[1] = (er[...] * n + ed[...]) * 2
    copy = pltpu.make_async_copy(kv, ks, sem)
    copy.start()

    step = 32

    def mix(i, _):
        rows = pl.ds(pl.multiple_of(i * step, step), step)
        parts = [bases[rows, b * classes : (b + 1) * classes].astype(F32) for b in range(nb)]
        for r in range(nrel):
            w = coef[r, 0] * parts[0]
            for b in range(1, nb):
                w = w + coef[r, b] * parts[b]
            hi, lo = split(w)
            whi[rows, r * 2 * L : r * 2 * L + classes] = hi
            wlo[rows, r * 2 * L : r * 2 * L + classes] = lo
        whi[rows, nrel * 2 * L : nrel * 2 * L + classes] = self_w[rows, :]
        return 0

    lax.fori_loop(0, hdim // step, mix, 0)

    s0[...] = jnp.zeros_like(s0)
    s1[...] = jnp.zeros_like(s1)
    sc2[pl.ds(2 * n, 16), :] = jnp.zeros((16, L), F32)

    chunk = 256
    lane = lanes(chunk)

    def project(i, _):
        row = pl.multiple_of(i * chunk, chunk)
        h = hid[pl.ds(row, chunk), :]
        for r in range(nrel):
            cols = pl.ds(r * 2 * L, 2 * L)
            a = dot(h, whi[:, cols]) + dot(h, wlo[:, cols])
            at = 2 * (r * n + row)
            m2[pl.ds(at, chunk, stride=2), :] = a[:, :L]
            tail = jnp.where(lane < rest, a[:, L:], jnp.where(lane == rest, 1.0, 0.0))
            m2[pl.ds(at + 1, chunk, stride=2), :] = tail
        a = dot(h, whi[:, pl.ds(nrel * 2 * L, 2 * L)])
        sc2[pl.ds(2 * row, chunk, stride=2), :] = a[:, :L] + bias[0:1, :]
        tail = jnp.where(lane < rest, a[:, L:] + bias[1:2, :], 0.0)
        sc2[pl.ds(2 * row + 1, chunk, stride=2), :] = tail
        return 0

    lax.fori_loop(0, n // chunk, project, 0)
    copy.wait()

    half = erows // 2

    def edges(t, _):
        for l in range(L):
            for c, s in enumerate((s0, s1)):
                j = ks[0, t + c * half, l]
                d = ks[1, t + c * half, l]
                src = m2[pl.ds(pl.multiple_of(j, 2), 2), :]
                at = pl.ds(pl.multiple_of(d, 2), 2)
                s[at, :] = s[at, :] + src
        return 0

    lax.fori_loop(0, half, edges, 0)

    fin = 64
    flane = lanes(fin)

    def finish(i, _):
        row = i * fin
        a0 = sc2[pl.ds(2 * row, fin, stride=2), :]
        a1 = sc2[pl.ds(2 * row + 1, fin, stride=2), :]
        for r in range(nrel):
            at = 2 * (r * n + row)
            m = s0[pl.ds(at, fin, stride=2), :] + s1[pl.ds(at, fin, stride=2), :]
            t = s0[pl.ds(at + 1, fin, stride=2), :] + s1[pl.ds(at + 1, fin, stride=2), :]
            inv = 1.0 / jnp.maximum(t[:, rest : rest + 1], 1.0)
            a0 = a0 + m * inv
            a1 = a1 + t * inv
        sc2[pl.ds(2 * row, fin, stride=2), :] = a0
        sc2[pl.ds(2 * row + 1, fin, stride=2), :] = jnp.where(flane < rest, a1, 0.0)
        return 0

    lax.fori_loop(0, n // fin, finish, 0)

    gather_rows(send, sc2, stg, peers, slots)
    ntail = up(slots, per)

    def put(p, _):
        at = p * 2 * slots
        out[p, 0:slots, :] = stg[pl.ds(at, slots, stride=2), :]
        tail = stg[pl.ds(at + 1, ntail, stride=2 * per), :]
        for q in range(1, per):
            x = stg[pl.ds(at + 2 * q + 1, ntail, stride=2 * per), :]
            tail = tail + pltpu.roll(x, q * rest, axis=1)
        out[p, slots : slots + ntail, :] = tail
        return 0

    lax.fori_loop(0, peers, put, 0)


def pack(bnd, v2, stg, out, extra, *, peers, slots, per, rest):
    gather_rows(bnd, v2, stg, peers, slots)
    ntail = up(slots, per)
    blk = slots + ntail
    for k in range(slots):
        out[pl.ds(k, peers, stride=blk), :] = stg[pl.ds(2 * k, peers, stride=2 * slots), :]
    for j in range(ntail):
        tail = None
        for q in range(min(per, slots - j * per)):
            x = stg[pl.ds(2 * (j * per + q) + 1, peers, stride=2 * slots), :]
            x = pltpu.roll(x, q * rest, axis=1) if q else x
            tail = x if tail is None else tail + x
        if j == 0 and extra is not None:
            tail = tail + extra
        out[pl.ds(slots + j, peers, stride=blk), :] = tail


def errors_kernel(arr, recv, bnd, labk, base, e0, eh, el, out, stg, base2, v2, stgb, *, classes, per):
    n = base.shape[0]
    rest = classes - L
    peers, blk, _ = arr.shape
    slots = recv.shape[2]
    ntail = up(slots, per)
    tlane = lanes(ntail)

    def unpack(p, _):
        at = p * 2 * slots
        tail = arr[p, slots : slots + ntail, :]
        for q in range(per):
            x = pltpu.roll(tail, (L - q * rest) % L, axis=1) if q else tail
            x = jnp.where(tlane < rest, x, 0.0)
            stg[pl.ds(at + 2 * q + 1, ntail, stride=2 * per), :] = x
        stg[pl.ds(at, slots, stride=2), :] = arr[p, 0:slots, :]
        return 0

    lax.fori_loop(0, peers, unpack, 0)

    def spread(p, _):
        for k in range(slots):
            row = recv[0, p, k]
            pair(base2, row)[...] = pair(stg, p * slots + k)[...]
        return 0

    lax.fori_loop(0, peers, spread, 0)

    chunk = 128
    lane = lanes(chunk)

    def error(i, _):
        row = pl.multiple_of(i * chunk, chunk)
        rows = pl.ds(row, chunk)
        lab = labk[rows, :]
        known = lab >= 0.0
        for h in range(2):
            cols = slice(h * L, (h + 1) * L)
            b = base2[pl.ds(2 * row + h, chunk, stride=2), :]
            onehot = jnp.where(lab == (lane + h * L).astype(F32), 1.0, 0.0)
            e = jnp.where(known, onehot - b, 0.0)
            base[rows, cols] = b
            e0[rows, cols] = e
            hi, lo = split(e)
            eh[rows, cols] = hi
            el[rows, cols] = lo
            v2[pl.ds(2 * row + h, chunk, stride=2), :] = e
        return 0

    lax.fori_loop(0, n // chunk, error, 0)
    v2[pl.ds(2 * n, 16), :] = jnp.zeros((16, L), F32)
    pack(bnd, v2, stgb, out, None, peers=peers, slots=bnd.shape[2], per=per, rest=rest)


def tiles_kernel(tiles, cols, labels, mask, nh, nl, fh, fl, labk, cnt):
    blocks = labels.shape[0]
    halo = fh.shape[1] // L

    def body(b, _):
        rows = pl.ds(pl.multiple_of(b * L, L), L)
        for j in range(LOC_ROW):
            hi, lo = split(tiles[b * TILES_ROW + j])
            nh[rows, j * L : (j + 1) * L] = hi
            nl[rows, j * L : (j + 1) * L] = lo
        for q in range(halo):
            acc = jnp.zeros((L, L), F32)
            for j in range(LOC_ROW, TILES_ROW):
                hit = cols[b * TILES_ROW + j] == blocks + q
                acc = acc + jnp.where(hit, tiles[b * TILES_ROW + j], 0.0)
            hi, lo = split(acc)
            fh[rows, q * L : (q + 1) * L] = hi
            fl[rows, q * L : (q + 1) * L] = lo
        lab = jnp.where(mask[pl.ds(b, 1), :] > 0, labels[pl.ds(b, 1), :], -1).astype(F32)
        labk[rows, :] = jnp.broadcast_to(lab, (L, L)).T
        return 0

    lax.fori_loop(0, blocks, body, 0)
    cnt[...] = jnp.zeros(cnt.shape, F32) + jnp.sum(mask[...].astype(F32))


def near_kernel(vh, vl, e, nh, nl, cols, *rest_refs, rate, classes, sums):
    if sums:
        cnt, part, tot = rest_refs
    else:
        (part,) = rest_refs
    blocks = vh.shape[0] // L

    def body(b, acc):
        rows = pl.ds(pl.multiple_of(b * L, L), L)
        at = [pl.ds(pl.multiple_of(cols[b * TILES_ROW + j] * L, L), L) for j in range(LOC_ROW)]
        bh = jnp.concatenate([vh[a, :] for a in at], 0)
        bl = jnp.concatenate([vl[a, :] for a in at], 0)
        a2 = dot(jnp.concatenate([nh[rows, :], nl[rows, :]], 0), bh)
        near = a2[:L] + a2[L:] + dot(nh[rows, :], bl)
        ev = e[rows, :]
        part[rows, :] = (1.0 - rate) * ev + rate * near
        if sums:
            mag = jnp.abs(ev)
            mag = mag[:, :L] + mag[:, L:]
            acc = acc + jnp.sum(mag.reshape(L // 8, 8, L), 0)
        return acc

    acc = lax.fori_loop(0, blocks, body, jnp.zeros((8, L), F32))
    if sums:
        total = jnp.sum(acc) * (1.0 / classes)
        lane = lanes(8)
        tot[...] = jnp.where(lane == L - 2, total, jnp.where(lane == L - 1, cnt[...], 0.0))


def far_kernel(*refs, rate, classes, per, mode, peers, slots, n):
    rest = classes - L
    refs = list(refs)
    arr, fh, fl, part = refs[:4]
    refs = refs[4:]
    if mode != "last":
        bnd = refs.pop(0)
    if mode == "sums":
        tot = refs.pop(0)
    if mode == "turn":
        base, labk, start = refs.pop(0), refs.pop(0), refs.pop(2)
    if mode == "last":
        out, hm, hr = refs
    else:
        vh, vl, out, hm, hr, v2, stgb = refs
    ntail = up(slots, per)
    blk = slots + ntail
    tlane = lanes(peers)
    for k in range(slots):
        hm[pl.ds(k, peers, stride=slots), :] = arr[pl.ds(k, peers, stride=blk), :]
    for j in range(ntail):
        tail = arr[pl.ds(slots + j, peers, stride=blk), :]
        if j == 0 and mode == "turn":
            sums = jnp.sum(tail, axis=0, keepdims=True)
            sigma = sums[:, L - 2 : L - 1] / sums[:, L - 1 : L]
        for q in range(min(per, slots - j * per)):
            x = pltpu.roll(tail, (L - q * rest) % L, axis=1) if q else tail
            x = jnp.where(tlane < rest, x, 0.0)
            hr[pl.ds(j * per + q, peers, stride=slots), :] = x
    hh, hl = split(jnp.concatenate([hm[...], hr[...]], 1))

    chunk = 256
    lane = lanes(chunk)

    def body(i, _):
        row = pl.multiple_of(i * chunk, chunk)
        rows = pl.ds(row, chunk)
        a2 = dot(jnp.concatenate([fh[rows, :], fl[rows, :]], 0), hh)
        far = a2[:chunk] + a2[chunk:] + dot(fh[rows, :], hl)
        v = part[rows, :] + rate * far
        if mode == "last":
            out[rows, :] = v[:, :classes]
            return 0
        if mode == "turn":
            mag = jnp.abs(v)
            mag = jnp.sum(mag[:, :L] + mag[:, L:], -1, keepdims=True) * (1.0 / classes) + tiny
            scale = sigma / mag
            lab = labk[rows, :]
        for h in range(2):
            cols = slice(h * L, (h + 1) * L)
            x = v[:, cols]
            if mode == "turn":
                onehot = jnp.where(lab == (lane + h * L).astype(F32), 1.0, 0.0)
                x = jnp.where(lab >= 0.0, onehot, base[rows, cols] + scale * x)
                start[rows, cols] = x
            hi, lo = split(x)
            vh[rows, cols] = hi
            vl[rows, cols] = lo
            v2[pl.ds(2 * row + h, chunk, stride=2), :] = x
        return 0

    lax.fori_loop(0, n // chunk, body, 0)
    if mode != "last":
        v2[pl.ds(2 * n, 16), :] = jnp.zeros((16, L), F32)
        extra = tot[0:1, :] if mode == "sums" else None
        pack(bnd, v2, stgb, out, extra, peers=peers, slots=slots, per=per, rest=rest)


def call(kernel, outs, ins, args, scratch=(), vmem=0, flops=0, size=0, name=None):
    return pl.pallas_call(
        kernel,
        out_shape=outs,
        in_specs=ins,
        out_specs=jax.tree.map(lambda _: VM, outs),
        scratch_shapes=list(scratch),
        compiler_params=pltpu.CompilerParams(vmem_limit_bytes=vmem),
        cost_estimate=pl.CostEstimate(flops=flops, bytes_accessed=size, transcendentals=0),
        name=name,
    )(*args)


def swap(x):
    return lax.all_to_all(x, "dom", split_axis=0, concat_axis=0, tiled=True)


def on_device(
    peers, hidden, bases, self_weight, coef, bias, edge_src, edge_dst, edge_rel, send_rows, recv_rows, labels,
    train_mask, bnd_rows, tiles, tile_cols,
):
    n, hdim = hidden.shape
    classes = self_weight.shape[1]
    nrel, nb = coef.shape
    rest = classes - L
    per = (L - 2) // rest
    slots = send_rows.shape[2]
    bnd = bnd_rows.shape[2]
    ne = edge_src.shape[0]
    halo = peers * bnd
    sds = jax.ShapeDtypeStruct
    state = sds((n, 2 * L), F32)
    half = sds((n, 2 * L), BF16)
    blocks = n // L

    blk = up(slots + up(slots, per), 8) * 8
    bias2 = jnp.pad(bias, (0, 2 * L - classes)).reshape(2, L)
    square = lambda x: x.reshape(-1, L)
    stage = pltpu.VMEM((2 * (peers * slots + 16), L), F32)
    rows2 = pltpu.VMEM((2 * n + 16, L), F32)
    sent = call(
        functools.partial(scores_kernel, classes=classes, slots=slots, per=per, blk=blk),
        sds((peers, blk, L), F32),
        [VM, VM, VM, VM, SM, VM, VM, VM, SM],
        (hidden, bases, self_weight, bias2, coef, square(edge_src), square(edge_dst), square(edge_rel), send_rows),
        [
            pltpu.VMEM((hdim, (nrel + 1) * 2 * L), BF16),
            pltpu.VMEM((hdim, nrel * 2 * L), BF16),
            pltpu.VMEM((2 * nrel * n, L), F32),
            pltpu.VMEM((2 * nrel * n, L), F32),
            pltpu.VMEM((2 * nrel * n, L), F32),
            rows2,
            stage,
            pltpu.VMEM((2, ne // L, L), jnp.int32),
            pltpu.SMEM((2, ne // L, L), jnp.int32),
            pltpu.SemaphoreType.DMA,
        ],
        vmem=56 * MIB,
        name="scores",
    )
    arrived = swap(sent)
    nh, nl, fh, fl, labk, cnt = call(
        tiles_kernel,
        (half, half, sds((n, halo), BF16), sds((n, halo), BF16), sds((n, L), F32), sds((8, L), F32)),
        [VM, SM, VM, VM],
        (tiles, tile_cols, square(labels), square(train_mask)),
        vmem=28 * MIB,
        flops=10**7,
        size=8 * 10**6,
        name="tiles",
    )
    lines = peers * (bnd + up(bnd, per))
    packed = sds((lines, L), F32)
    stageb = pltpu.VMEM((2 * halo, L), F32)
    base, e, vh, vl, out = call(
        functools.partial(errors_kernel, classes=classes, per=per),
        (state, state, half, half, packed),
        [VM, SM, SM, VM],
        (arrived, recv_rows, bnd_rows, labk),
        [stage, rows2, rows2, stageb],
        vmem=28 * MIB,
        name="errors",
    )
    hscr = [pltpu.VMEM((halo, L), F32)] * 2
    for step in range(2 * ITERS):
        rate = correct_rate if step < ITERS else smooth_rate
        halos = swap(out.reshape(peers, 1, -1)).reshape(lines, L)
        sums = step == 0
        mode = "last" if step == 2 * ITERS - 1 else "turn" if step == ITERS - 1 else "sums" if step == ITERS - 2 else "step"
        got = call(
            functools.partial(near_kernel, rate=rate, classes=classes, sums=sums),
            (state, sds((8, L), F32)) if sums else (state,),
            [VM, VM, VM, VM, VM, SM] + [VM] * sums,
            (vh, vl, e, nh, nl, tile_cols) + ((cnt,) if sums else ()),
            vmem=16 * MIB,
            flops=10**9,
            size=8 * 10**6,
            name="near",
        )
        part = got[0]
        if sums:
            tot = got[1]
        far = functools.partial(
            far_kernel, rate=rate, classes=classes, per=per, mode=mode, peers=peers, slots=bnd, n=n
        )
        args, ins = (halos, fh, fl, part), [VM] * 4
        if mode == "last":
            return call(far, sds((n, classes), F32), ins, args, hscr, vmem=24 * MIB, name="far_last")
        args, ins = args + (bnd_rows,), ins + [SM]
        outs = (half, half, packed)
        if mode == "sums":
            args, ins = args + (tot,), ins + [VM]
        if mode == "turn":
            args, ins = args + (base, labk), ins + [VM, VM]
            outs = (half, half, state, packed)
        got = call(far, outs, ins, args, hscr + [rows2, stageb], vmem=24 * MIB, name="far_" + mode)
        if mode == "turn":
            vh, vl, e, out = got
        else:
            vh, vl, out = got


def solution(mesh):
    row = P("dom")
    in_specs = (
        P("dom", None), P(), P(), P(), P(), row, row, row, P("dom", None, None), P("dom", None, None), row, row,
        P("dom", None, None), P("dom", None, None), row,
    )
    return jax.shard_map(
        functools.partial(on_device, mesh.shape["dom"]),
        mesh=mesh,
        in_specs=in_specs,
        out_specs=P("dom", None),
        check_vma=False,
    )
```

```python
import functools

import jax
import jax.numpy as jnp
from jax import lax
from jax.experimental import pallas as pl
from jax.experimental.pallas import tpu as pltpu
from jax.sharding import PartitionSpec as P

TILES_ROW = 4
LOC_ROW = 2
ITERS = 3
L = 128

correct_rate = 0.8
smooth_rate = 0.75
tiny = 1e-06

F32 = jnp.float32
BF16 = jnp.bfloat16
VM = pl.BlockSpec(memory_space=pltpu.VMEM)
SM = pl.BlockSpec(memory_space=pltpu.SMEM)
HB = pl.BlockSpec(memory_space=pltpu.HBM)
MIB = 1 << 20


def up(a, b):
    return -(-a // b)


def split(x):
    hi = x.astype(BF16)
    return hi, (x - hi.astype(F32)).astype(BF16)


def dot(a, b):
    return jnp.dot(a, b, preferred_element_type=F32)


def lanes(rows):
    return lax.broadcasted_iota(jnp.int32, (rows, L), 1)


def pair(ref, row):
    return ref.at[pl.ds(pl.multiple_of(2 * row, 2), 2), :]


def gather_rows(idx_ref, src, stg, peers, slots):
    def body(p, _):
        for k in range(slots):
            row = idx_ref[0, p, k]
            pair(stg, p * slots + k)[...] = pair(src, row)[...]
        return 0

    lax.fori_loop(0, peers, body, 0)


def scores_kernel(
    hid, bases, self_w, bias, coef, es, ed, er, send, out,
    whi, wlo, m2, s0, s1, sc2, stg, kv, ks, sem, *, classes, slots, per, blk,
):
    n, hdim = hid.shape
    rest = classes - L
    nrel, nb = coef.shape
    peers = out.shape[0]
    erows = es.shape[0]
    kv[0] = (er[...] * n + es[...]) * 2
    kv[1] = (er[...] * n + ed[...]) * 2
    copy = pltpu.make_async_copy(kv, ks, sem)
    copy.start()

    step = 32

    def mix(i, _):
        rows = pl.ds(pl.multiple_of(i * step, step), step)
        parts = [bases[rows, b * classes : (b + 1) * classes].astype(F32) for b in range(nb)]
        for r in range(nrel):
            w = coef[r, 0] * parts[0]
            for b in range(1, nb):
                w = w + coef[r, b] * parts[b]
            hi, lo = split(w)
            whi[rows, r * 2 * L : r * 2 * L + classes] = hi
            wlo[rows, r * 2 * L : r * 2 * L + classes] = lo
        whi[rows, nrel * 2 * L : nrel * 2 * L + classes] = self_w[rows, :]
        return 0

    lax.fori_loop(0, hdim // step, mix, 0)

    s0[...] = jnp.zeros_like(s0)
    s1[...] = jnp.zeros_like(s1)
    sc2[pl.ds(2 * n, 16), :] = jnp.zeros((16, L), F32)

    chunk = 256
    lane = lanes(chunk)

    def project(i, _):
        row = pl.multiple_of(i * chunk, chunk)
        h = hid[pl.ds(row, chunk), :]
        for r in range(nrel):
            cols = pl.ds(r * 2 * L, 2 * L)
            a = dot(h, whi[:, cols]) + dot(h, wlo[:, cols])
            at = 2 * (r * n + row)
            m2[pl.ds(at, chunk, stride=2), :] = a[:, :L]
            tail = jnp.where(lane < rest, a[:, L:], jnp.where(lane == rest, 1.0, 0.0))
            m2[pl.ds(at + 1, chunk, stride=2), :] = tail
        a = dot(h, whi[:, pl.ds(nrel * 2 * L, 2 * L)])
        sc2[pl.ds(2 * row, chunk, stride=2), :] = a[:, :L] + bias[0:1, :]
        tail = jnp.where(lane < rest, a[:, L:] + bias[1:2, :], 0.0)
        sc2[pl.ds(2 * row + 1, chunk, stride=2), :] = tail
        return 0

    lax.fori_loop(0, n // chunk, project, 0)
    copy.wait()

    half = erows // 2

    def edges(t, _):
        for l in range(L):
            for c, s in enumerate((s0, s1)):
                j = ks[0, t + c * half, l]
                d = ks[1, t + c * half, l]
                src = m2[pl.ds(pl.multiple_of(j, 2), 2), :]
                at = pl.ds(pl.multiple_of(d, 2), 2)
                s[at, :] = s[at, :] + src
        return 0

    lax.fori_loop(0, half, edges, 0)

    fin = 64
    flane = lanes(fin)

    def finish(i, _):
        row = i * fin
        a0 = sc2[pl.ds(2 * row, fin, stride=2), :]
        a1 = sc2[pl.ds(2 * row + 1, fin, stride=2), :]
        for r in range(nrel):
            at = 2 * (r * n + row)
            m = s0[pl.ds(at, fin, stride=2), :] + s1[pl.ds(at, fin, stride=2), :]
            t = s0[pl.ds(at + 1, fin, stride=2), :] + s1[pl.ds(at + 1, fin, stride=2), :]
            inv = 1.0 / jnp.maximum(t[:, rest : rest + 1], 1.0)
            a0 = a0 + m * inv
            a1 = a1 + t * inv
        sc2[pl.ds(2 * row, fin, stride=2), :] = a0
        sc2[pl.ds(2 * row + 1, fin, stride=2), :] = jnp.where(flane < rest, a1, 0.0)
        return 0

    lax.fori_loop(0, n // fin, finish, 0)

    gather_rows(send, sc2, stg, peers, slots)
    ntail = up(slots, per)

    def put(p, _):
        at = p * 2 * slots
        out[p, 0:slots, :] = stg[pl.ds(at, slots, stride=2), :]
        tail = stg[pl.ds(at + 1, ntail, stride=2 * per), :]
        for q in range(1, per):
            x = stg[pl.ds(at + 2 * q + 1, ntail, stride=2 * per), :]
            tail = tail + pltpu.roll(x, q * rest, axis=1)
        out[p, slots : slots + ntail, :] = tail
        return 0

    lax.fori_loop(0, peers, put, 0)


def pack(bnd, v2, stg, out, extra, *, peers, slots, per, rest):
    gather_rows(bnd, v2, stg, peers, slots)
    ntail = up(slots, per)
    blk = slots + ntail
    for k in range(slots):
        out[pl.ds(k, peers, stride=blk), :] = stg[pl.ds(2 * k, peers, stride=2 * slots), :]
    for j in range(ntail):
        tail = None
        for q in range(min(per, slots - j * per)):
            x = stg[pl.ds(2 * (j * per + q) + 1, peers, stride=2 * slots), :]
            x = pltpu.roll(x, q * rest, axis=1) if q else x
            tail = x if tail is None else tail + x
        if j == 0 and extra is not None:
            tail = tail + extra
        out[pl.ds(slots + j, peers, stride=blk), :] = tail


def errors_kernel(
    arr, recv, bnd, labk_hbm, base_hbm, e_hbm, out, stg, base2, v2, stgb, labk, sems, *, classes, per, n
):
    rest = classes - L
    peers, blk, _ = arr.shape
    slots = recv.shape[2]
    ntail = up(slots, per)
    tlane = lanes(ntail)
    load = pltpu.make_async_copy(labk_hbm, labk, sems.at[0])
    load.start()

    def unpack(p, _):
        at = p * 2 * slots
        tail = arr[p, slots : slots + ntail, :]
        for q in range(per):
            x = pltpu.roll(tail, (L - q * rest) % L, axis=1) if q else tail
            x = jnp.where(tlane < rest, x, 0.0)
            stg[pl.ds(at + 2 * q + 1, ntail, stride=2 * per), :] = x
        stg[pl.ds(at, slots, stride=2), :] = arr[p, 0:slots, :]
        return 0

    lax.fori_loop(0, peers, unpack, 0)

    def spread(p, _):
        for k in range(slots):
            row = recv[0, p, k]
            pair(base2, row)[...] = pair(stg, p * slots + k)[...]
        return 0

    lax.fori_loop(0, peers, spread, 0)
    keep = pltpu.make_async_copy(base2, base_hbm, sems.at[1])
    keep.start()
    load.wait()

    chunk = 128
    lane = lanes(chunk)

    def error(i, _):
        row = pl.multiple_of(i * chunk, chunk)
        lab = labk[pl.ds(row, chunk), :]
        known = lab >= 0.0
        for h in range(2):
            rows = pl.ds(2 * row + h, chunk, stride=2)
            onehot = jnp.where(lab == (lane + h * L).astype(F32), 1.0, 0.0)
            v2[rows, :] = jnp.where(known, onehot - base2[rows, :], 0.0)
        return 0

    lax.fori_loop(0, n // chunk, error, 0)
    v2[pl.ds(2 * n, 16), :] = jnp.zeros((16, L), F32)
    save = pltpu.make_async_copy(v2, e_hbm, sems.at[2])
    save.start()
    pack(bnd, v2, stgb, out, None, peers=peers, slots=bnd.shape[2], per=per, rest=rest)
    keep.wait()
    save.wait()


def tiles_kernel(tiles, cols, labels, mask, nh_hbm, nl_hbm, fh, fl, lab_hbm, cnt, nh, nl, labk, sems):
    blocks = labels.shape[0]
    halo = fh.shape[1] // L

    def body(b, _):
        rows = pl.ds(pl.multiple_of(b * L, L), L)
        for j in range(LOC_ROW):
            hi, lo = split(tiles[b * TILES_ROW + j])
            nh[rows, j * L : (j + 1) * L] = hi
            nl[rows, j * L : (j + 1) * L] = lo
        for q in range(halo):
            acc = jnp.zeros((L, L), F32)
            for j in range(LOC_ROW, TILES_ROW):
                hit = cols[b * TILES_ROW + j] == blocks + q
                acc = acc + jnp.where(hit, tiles[b * TILES_ROW + j], 0.0)
            hi, lo = split(acc)
            fh[rows, q * L : (q + 1) * L] = hi
            fl[rows, q * L : (q + 1) * L] = lo
        lab = jnp.where(mask[pl.ds(b, 1), :] > 0, labels[pl.ds(b, 1), :], -1).astype(F32)
        labk[rows, :] = jnp.broadcast_to(lab, (L, L)).T
        return 0

    lax.fori_loop(0, blocks, body, 0)
    pairs = ((nh, nh_hbm), (nl, nl_hbm), (labk, lab_hbm))
    saves = [pltpu.make_async_copy(a, b, sems.at[i]) for i, (a, b) in enumerate(pairs)]
    for c in saves:
        c.start()
    cnt[...] = jnp.zeros(cnt.shape, F32) + jnp.sum(mask[...].astype(F32))
    for c in saves:
        c.wait()


def near_kernel(v_hbm, e_hbm, nh_hbm, nl_hbm, cols, *refs, rate, classes, sums):
    if sums:
        cnt, part, tot, v2, e2, nh, nl, vh, vl, sems = refs
    else:
        part, v2, e2, nh, nl, vh, vl, sems = refs
    pairs = ((v_hbm, v2), (nh_hbm, nh), (nl_hbm, nl), (e_hbm, e2))
    loads = [pltpu.make_async_copy(a, b, sems.at[i]) for i, (a, b) in enumerate(pairs)]
    for c in loads:
        c.start()
    blocks = part.shape[0] // L
    loads[0].wait()

    def halve(b, _):
        rows = pl.ds(pl.multiple_of(b * L, L), L)
        for h in range(2):
            hi, lo = split(v2[pl.ds(b * 2 * L + h, L, stride=2), :])
            vh[rows, h * L : (h + 1) * L] = hi
            vl[rows, h * L : (h + 1) * L] = lo
        return 0

    lax.fori_loop(0, blocks, halve, 0)
    for c in loads[1:]:
        c.wait()

    def body(b, acc):
        rows = pl.ds(pl.multiple_of(b * L, L), L)
        at = [pl.ds(pl.multiple_of(cols[b * TILES_ROW + j] * L, L), L) for j in range(LOC_ROW)]
        bh = jnp.concatenate([vh[a, :] for a in at], 0)
        bl = jnp.concatenate([vl[a, :] for a in at], 0)
        a2 = dot(jnp.concatenate([nh[rows, :], nl[rows, :]], 0), bh)
        near = a2[:L] + a2[L:] + dot(nh[rows, :], bl)
        for h in range(2):
            ev = e2[pl.ds(b * 2 * L + h, L, stride=2), :]
            part[rows, h * L : (h + 1) * L] = (1.0 - rate) * ev + rate * near[:, h * L : (h + 1) * L]
            if sums:
                acc = acc + jnp.sum(jnp.abs(ev).reshape(L // 8, 8, L), 0)
        return acc

    acc = lax.fori_loop(0, blocks, body, jnp.zeros((8, L), F32))
    if sums:
        total = jnp.sum(acc) * (1.0 / classes)
        lane = lanes(8)
        tot[...] = jnp.where(lane == L - 2, total, jnp.where(lane == L - 1, cnt[...], 0.0))


def far_kernel(*refs, rate, classes, per, mode, peers, slots, n):
    rest = classes - L
    refs = list(refs)
    arr, fh, fl, part = refs[:4]
    refs = refs[4:]
    if mode != "last":
        bnd = refs.pop(0)
    if mode == "sums":
        tot = refs.pop(0)
    if mode == "turn":
        base_hbm, lab_hbm, base2, labk, sems = refs.pop(0), refs.pop(0), refs.pop(), refs.pop(), refs.pop()
        loads = [
            pltpu.make_async_copy(base_hbm, base2, sems.at[0]),
            pltpu.make_async_copy(lab_hbm, labk, sems.at[1]),
        ]
        for c in loads:
            c.start()
    if mode == "last":
        out, hm, hr = refs
    else:
        v_hbm, out, hm, hr, v2, stgb, vsem = refs
    ntail = up(slots, per)
    blk = slots + ntail
    tlane = lanes(peers)
    for k in range(slots):
        hm[pl.ds(k, peers, stride=slots), :] = arr[pl.ds(k, peers, stride=blk), :]
    for j in range(ntail):
        tail = arr[pl.ds(slots + j, peers, stride=blk), :]
        if j == 0 and mode == "turn":
            sums = jnp.sum(tail, axis=0, keepdims=True)
            sigma = sums[:, L - 2 : L - 1] / sums[:, L - 1 : L]
        for q in range(min(per, slots - j * per)):
            x = pltpu.roll(tail, (L - q * rest) % L, axis=1) if q else tail
            x = jnp.where(tlane < rest, x, 0.0)
            hr[pl.ds(j * per + q, peers, stride=slots), :] = x
    hh, hl = split(jnp.concatenate([hm[...], hr[...]], 1))
    if mode == "turn":
        for c in loads:
            c.wait()

    chunk = 256
    lane = lanes(chunk)

    def body(i, _):
        row = pl.multiple_of(i * chunk, chunk)
        rows = pl.ds(row, chunk)
        a2 = dot(jnp.concatenate([fh[rows, :], fl[rows, :]], 0), hh)
        far = a2[:chunk] + a2[chunk:] + dot(fh[rows, :], hl)
        v = part[rows, :] + rate * far
        if mode == "last":
            out[0:L, rows] = v[:, :L].T
            out[L:classes, rows] = v[:, L:].T[:rest]
            return 0
        if mode == "turn":
            mag = jnp.abs(v)
            mag = jnp.sum(mag[:, :L] + mag[:, L:], -1, keepdims=True) * (1.0 / classes) + tiny
            scale = sigma / mag
            lab = labk[rows, :]
        for h in range(2):
            x = v[:, h * L : (h + 1) * L]
            rows2 = pl.ds(2 * row + h, chunk, stride=2)
            if mode == "turn":
                onehot = jnp.where(lab == (lane + h * L).astype(F32), 1.0, 0.0)
                x = jnp.where(lab >= 0.0, onehot, base2[rows2, :] + scale * x)
            v2[rows2, :] = x
        return 0

    lax.fori_loop(0, n // chunk, body, 0)
    if mode != "last":
        v2[pl.ds(2 * n, 16), :] = jnp.zeros((16, L), F32)
        save = pltpu.make_async_copy(v2, v_hbm, vsem)
        save.start()
        extra = tot[0:1, :] if mode == "sums" else None
        pack(bnd, v2, stgb, out, extra, peers=peers, slots=slots, per=per, rest=rest)
        save.wait()


def call(kernel, outs, ins, args, scratch=(), vmem=0, flops=0, size=0, name=None, specs=None):
    if specs:
        outs = tuple(pltpu.HBM(o.shape, o.dtype) if p is HB else o for o, p in zip(outs, specs))
    args = [pltpu.with_memory_space_constraint(a, pltpu.HBM) if p is HB else a for a, p in zip(args, ins)]
    return pl.pallas_call(
        kernel,
        out_shape=outs,
        in_specs=ins,
        out_specs=specs or jax.tree.map(lambda _: VM, outs),
        scratch_shapes=list(scratch),
        compiler_params=pltpu.CompilerParams(vmem_limit_bytes=vmem),
        cost_estimate=pl.CostEstimate(flops=flops, bytes_accessed=size, transcendentals=0),
        name=name,
    )(*args)


def swap(x):
    return lax.all_to_all(x, "dom", split_axis=0, concat_axis=0, tiled=True)


def on_device(
    peers, hidden, bases, self_weight, coef, bias, edge_src, edge_dst, edge_rel, send_rows, recv_rows, labels,
    train_mask, bnd_rows, tiles, tile_cols,
):
    n, hdim = hidden.shape
    classes = self_weight.shape[1]
    nrel, nb = coef.shape
    rest = classes - L
    per = (L - 2) // rest
    slots = send_rows.shape[2]
    bnd = bnd_rows.shape[2]
    ne = edge_src.shape[0]
    halo = peers * bnd
    sds = jax.ShapeDtypeStruct
    state = sds((n, 2 * L), F32)
    half = sds((n, 2 * L), BF16)
    blocks = n // L

    blk = up(slots + up(slots, per), 8) * 8
    bias2 = jnp.pad(bias, (0, 2 * L - classes)).reshape(2, L)
    square = lambda x: x.reshape(-1, L)
    stage = pltpu.VMEM((2 * (peers * slots + 16), L), F32)
    rows2 = pltpu.VMEM((2 * n + 16, L), F32)
    sent = call(
        functools.partial(scores_kernel, classes=classes, slots=slots, per=per, blk=blk),
        sds((peers, blk, L), F32),
        [VM, VM, VM, VM, SM, VM, VM, VM, SM],
        (hidden, bases, self_weight, bias2, coef, square(edge_src), square(edge_dst), square(edge_rel), send_rows),
        [
            pltpu.VMEM((hdim, (nrel + 1) * 2 * L), BF16),
            pltpu.VMEM((hdim, nrel * 2 * L), BF16),
            pltpu.VMEM((2 * nrel * n, L), F32),
            pltpu.VMEM((2 * nrel * n, L), F32),
            pltpu.VMEM((2 * nrel * n, L), F32),
            rows2,
            stage,
            pltpu.VMEM((2, ne // L, L), jnp.int32),
            pltpu.SMEM((2, ne // L, L), jnp.int32),
            pltpu.SemaphoreType.DMA,
        ],
        vmem=56 * MIB,
        name="scores",
    )
    arrived = swap(sent)
    dma = lambda k: pltpu.SemaphoreType.DMA((k,))
    spread = sds((2 * n + 16, L), F32)
    labv = pltpu.VMEM((n, L), F32)
    halfv = pltpu.VMEM((n, 2 * L), BF16)
    nh, nl, fh, fl, labk, cnt = call(
        tiles_kernel,
        (half, half, sds((n, halo), BF16), sds((n, halo), BF16), sds((n, L), F32), sds((8, L), F32)),
        [VM, SM, VM, VM],
        (tiles, tile_cols, square(labels), square(train_mask)),
        [halfv, halfv, labv, dma(3)],
        vmem=28 * MIB,
        flops=10**7,
        size=8 * 10**6,
        name="tiles",
        specs=(HB, HB, VM, VM, HB, VM),
    )
    lines = peers * (bnd + up(bnd, per))
    packed = sds((lines, L), F32)
    stageb = pltpu.VMEM((2 * halo, L), F32)
    base, v, out = call(
        functools.partial(errors_kernel, classes=classes, per=per, n=n),
        (spread, spread, packed),
        [VM, SM, SM, HB],
        (arrived, recv_rows, bnd_rows, labk),
        [stage, rows2, rows2, stageb, labv, dma(3)],
        vmem=28 * MIB,
        name="errors",
        specs=(HB, HB, VM),
    )
    e = v
    hscr = [pltpu.VMEM((halo, L), F32)] * 2
    for step in range(2 * ITERS):
        rate = correct_rate if step < ITERS else smooth_rate
        halos = swap(out.reshape(peers, 1, -1)).reshape(lines, L)
        sums = step == 0
        mode = "last" if step == 2 * ITERS - 1 else "turn" if step == ITERS - 1 else "sums" if step == ITERS - 2 else "step"
        got = call(
            functools.partial(near_kernel, rate=rate, classes=classes, sums=sums),
            (state, sds((8, L), F32)) if sums else (state,),
            [HB, HB, HB, HB, SM] + [VM] * sums,
            (v, e, nh, nl, tile_cols) + ((cnt,) if sums else ()),
            [rows2, rows2, halfv, halfv, halfv, halfv, dma(4)],
            vmem=24 * MIB,
            flops=10**9,
            size=8 * 10**6,
            name="near",
        )
        part = got[0]
        if sums:
            tot = got[1]
        far = functools.partial(
            far_kernel, rate=rate, classes=classes, per=per, mode=mode, peers=peers, slots=bnd, n=n
        )
        args, ins = (halos, fh, fl, part), [VM] * 4
        if mode == "last":
            return call(far, sds((classes, n), F32), ins, args, hscr, vmem=24 * MIB, name="far_last").T
        args, ins = args + (bnd_rows,), ins + [SM]
        scratch = hscr + [rows2, stageb, pltpu.SemaphoreType.DMA]
        if mode == "sums":
            args, ins = args + (tot,), ins + [VM]
        if mode == "turn":
            args, ins = args + (base, labk), ins + [HB, HB]
            scratch = scratch + [dma(2), labv, rows2]
        v, out = call(
            far, (spread, packed), ins, args, scratch, vmem=24 * MIB, name="far_" + mode, specs=(HB, VM)
        )
        if mode == "turn":
            e = v


def solution(mesh):
    row = P("dom")
    in_specs = (
        P("dom", None), P(), P(), P(), P(), row, row, row, P("dom", None, None), P("dom", None, None), row, row,
        P("dom", None, None), P("dom", None, None), row,
    )
    return jax.shard_map(
        functools.partial(on_device, mesh.shape["dom"]),
        mesh=mesh,
        in_specs=in_specs,
        out_specs=P("dom", None),
        check_vma=False,
    )
```

```python
import functools

import jax
import jax.numpy as jnp
from jax import lax
from jax.experimental import pallas as pl
from jax.experimental.pallas import tpu as pltpu
from jax.sharding import PartitionSpec as P

TILES_ROW = 4
LOC_ROW = 2
ITERS = 3
L = 128

correct_rate = 0.8
smooth_rate = 0.75
tiny = 1e-06

F32 = jnp.float32
BF16 = jnp.bfloat16
VM = pl.BlockSpec(memory_space=pltpu.VMEM)
SM = pl.BlockSpec(memory_space=pltpu.SMEM)
HB = pl.BlockSpec(memory_space=pltpu.HBM)
MIB = 1 << 20


def up(a, b):
    return -(-a // b)


def split(x):
    hi = x.astype(BF16)
    return hi, (x - hi.astype(F32)).astype(BF16)


def dot(a, b):
    return jnp.dot(a, b, preferred_element_type=F32)


def lanes(rows):
    return lax.broadcasted_iota(jnp.int32, (rows, L), 1)


def pair(ref, row):
    return ref.at[pl.ds(pl.multiple_of(2 * row, 2), 2), :]


def gather_rows(idx_ref, src, stg, peers, slots):
    for p in range(peers):
        for k in range(slots):
            at = pl.ds(pl.multiple_of(idx_ref[0, p, k], 2), 2)
            stg[pl.ds(2 * (p * slots + k), 2), :] = src[at, :]


def fetch(src, rows, refs, sems):
    copies = [pltpu.make_async_copy(src.at[pl.ds(i, 1), :], r, sems.at[i]) for i, r in zip(rows, refs)]
    for c in copies:
        c.start()
    return copies


def scores_kernel(
    hid, bt, st, bias, coef, es, ed, er, send, out,
    pt, p0, p1, m2, s0, s1, s2, s3, sc2, stg, kj, kd, kp, sj, sd, sp, *ks, classes, slots, per,
):
    n, hdim = hid.shape
    rest = classes - L
    nrel, nb = coef.shape
    peers = out.shape[0]
    erows = es.shape[0]
    acc = (s0, s1, s2, s3)
    ksj, ksd, ksp = ks[:erows], ks[erows : 2 * erows], ks[2 * erows :]
    kj[...] = (er[...] * n + es[...]) * 2
    kd[...] = (er[...] * n + ed[...]) * 2
    kp[:, 0:slots] = send[0] * 2
    copies = fetch(kj, range(erows), ksj, sj) + fetch(kd, range(erows), ksd, sd) + fetch(kp, range(peers), ksp, sp)

    base_r = nb * L
    base_s = base_r + 2 * L
    gap = 2 * L // nb
    step = 2 * L

    def arrange(i, _):
        cols = pl.ds(pl.multiple_of(i * step, step), step)
        for b in range(nb):
            x = bt[b * classes : (b + 1) * classes, cols].astype(F32)
            pt[b * L : (b + 1) * L, cols] = x[:L].astype(BF16)
            tail = jnp.concatenate([x[L:], jnp.zeros((gap - rest, step), F32)], 0)
            pt[base_r + b * gap : base_r + (b + 1) * gap, cols] = tail.astype(BF16)
        x = st[:, cols].astype(F32)
        pt[base_s : base_s + L, cols] = x[:L].astype(BF16)
        tail = jnp.concatenate([x[L:], jnp.zeros((L - rest, step), F32)], 0)
        pt[base_s + L : base_s + 2 * L, cols] = tail.astype(BF16)
        return 0

    lax.fori_loop(0, hdim // step, arrange, 0)

    chunk = 256
    sub = 32
    zrows = 2 * nrel * chunk
    lane = lanes(sub)
    one = jnp.where(lane == rest, 1.0, 0.0)
    lane8 = lanes(8)
    gains = []
    for r in range(nrel):
        for h in range(2):
            g = jnp.zeros((8, L), F32)
            for b in range(nb // 2):
                g = jnp.where(lane8 // gap == b, coef[r, h * (nb // 2) + b], g)
            gains.append(g[0:1])
    bias0 = bias[0:1, 0:L]
    bias1 = jnp.concatenate([bias[0:1, L:classes], jnp.zeros((1, L - rest), F32)], 1)

    def project(i, dst):
        h = hid[pl.ds(pl.multiple_of(i * chunk, chunk), chunk), :]
        for j in range(0, base_s + 2 * L, 2 * L):
            dst[:, j : j + 2 * L] = lax.dot_general(
                h, pt[j : j + 2 * L, :], (((1,), (1,)), ((), ())), preferred_element_type=F32
            )
            yield

    def mix(i, src):
        row0 = i * chunk
        for u in range(0, chunk, sub):
            for z in acc:
                piece = zrows * sub // chunk
                at = pl.multiple_of(i * zrows + u * piece // sub, piece)
                z[pl.ds(at, piece), :] = jnp.zeros((piece, L), F32)
            rows = slice(u, u + sub)
            mains = [src[rows, b * L : (b + 1) * L] for b in range(nb)]
            q = [src[rows, base_r + h * L : base_r + (h + 1) * L] for h in range(2)]
            for r in range(nrel):
                x = coef[r, 0] * mains[0]
                for b in range(1, nb):
                    x = x + coef[r, b] * mains[b]
                t = gains[2 * r] * q[0] + gains[2 * r + 1] * q[1]
                turn = L // 2
                while turn >= gap:
                    t = t + pltpu.roll(t, turn, axis=1)
                    turn //= 2
                at = 2 * (r * n + row0 + u)
                m2[pl.ds(at, sub, stride=2), :] = x
                m2[pl.ds(at + 1, sub, stride=2), :] = jnp.where(lane < rest, t, one)
            at = 2 * (row0 + u)
            sc2[pl.ds(at, sub, stride=2), :] = src[rows, base_s : base_s + L] + bias0
            sc2[pl.ds(at + 1, sub, stride=2), :] = src[rows, base_s + L : base_s + 2 * L] + bias1
            yield

    def weave(*works):
        works = list(works)
        while works:
            for w in list(works):
                if next(w, 0) == 0:
                    works.remove(w)

    sc2[pl.ds(2 * n, 16), :] = jnp.zeros((16, L), F32)
    count = n // chunk
    weave(project(0, p0))

    def pipe(t, _):
        weave(project(2 * t + 1, p1), mix(2 * t, p0))
        weave(project(2 * t + 2, p0), mix(2 * t + 1, p1))
        return 0

    lax.fori_loop(0, count // 2 - 1, pipe, 0)
    weave(project(count - 1, p1), mix(count - 2, p0))
    weave(mix(count - 1, p1))
    for c in copies:
        c.wait()

    def edges(t, _):
        for v in range(2):
            for e in range(erows):
                s = acc[e % 4]
                j = ksj[e][0, 2 * t + v]
                d = ksd[e][0, 2 * t + v]
                src = m2[pl.ds(pl.multiple_of(j, 2), 2), :]
                at = pl.ds(pl.multiple_of(d, 2), 2)
                s[at, :] = s[at, :] + src
        return 0

    lax.fori_loop(0, L // 2, edges, 0)

    fin = 64
    flane = lanes(fin)

    def finish(i, _):
        row = i * fin
        a0 = sc2[pl.ds(2 * row, fin, stride=2), :]
        a1 = sc2[pl.ds(2 * row + 1, fin, stride=2), :]
        for r in range(nrel):
            rows = [pl.ds(2 * (r * n + row) + h, fin, stride=2) for h in range(2)]
            m, t = [(s0[w, :] + s1[w, :]) + (s2[w, :] + s3[w, :]) for w in rows]
            inv = 1.0 / jnp.maximum(t[:, rest : rest + 1], 1.0)
            a0 = a0 + m * inv
            a1 = a1 + t * inv
        sc2[pl.ds(2 * row, fin, stride=2), :] = a0
        sc2[pl.ds(2 * row + 1, fin, stride=2), :] = jnp.where(flane < rest, a1, 0.0)
        return 0

    lax.fori_loop(0, n // fin, finish, 0)

    def collect(k, _):
        for p in range(peers):
            at = pl.ds(pl.multiple_of(ksp[p][0, k], 2), 2)
            pair(stg, p * slots + k)[...] = sc2[at, :]
        return 0

    lax.fori_loop(0, slots, collect, 0)
    ntail = up(slots, per)

    def put(p, _):
        at = p * 2 * slots
        out[p, 0:slots, :] = stg[pl.ds(at, slots, stride=2), :]
        tail = stg[pl.ds(at + 1, ntail, stride=2 * per), :]
        for q in range(1, per):
            x = stg[pl.ds(at + 2 * q + 1, ntail, stride=2 * per), :]
            tail = tail + pltpu.roll(x, q * rest, axis=1)
        out[p, slots : slots + ntail, :] = tail
        return 0

    lax.fori_loop(0, peers, put, 0)


def pack(bnd, v2, stg, out, extra, *, peers, slots, per, rest):
    gather_rows(bnd, v2, stg, peers, slots)
    ntail = up(slots, per)
    blk = slots + ntail
    for k in range(slots):
        out[pl.ds(k, peers, stride=blk), :] = stg[pl.ds(2 * k, peers, stride=2 * slots), :]
    for j in range(ntail):
        tail = None
        for q in range(min(per, slots - j * per)):
            x = stg[pl.ds(2 * (j * per + q) + 1, peers, stride=2 * slots), :]
            x = pltpu.roll(x, q * rest, axis=1) if q else x
            tail = x if tail is None else tail + x
        if j == 0 and extra is not None:
            tail = tail + extra
        out[pl.ds(slots + j, peers, stride=blk), :] = tail


def errors_kernel(
    arr, recv, bnd, labk_hbm, base_hbm, e_hbm, out, stg, base2, v2, stgb, labk, sems, *, classes, per, n
):
    rest = classes - L
    peers, blk, _ = arr.shape
    slots = recv.shape[2]
    ntail = up(slots, per)
    tlane = lanes(ntail)
    load = pltpu.make_async_copy(labk_hbm, labk, sems.at[0])
    load.start()

    def unpack(p, _):
        at = p * 2 * slots
        tail = arr[p, slots : slots + ntail, :]
        for q in range(per):
            x = pltpu.roll(tail, (L - q * rest) % L, axis=1) if q else tail
            x = jnp.where(tlane < rest, x, 0.0)
            stg[pl.ds(at + 2 * q + 1, ntail, stride=2 * per), :] = x
        stg[pl.ds(at, slots, stride=2), :] = arr[p, 0:slots, :]
        return 0

    lax.fori_loop(0, peers, unpack, 0)

    def spread(p, _):
        for k in range(slots):
            row = recv[0, p, k]
            pair(base2, row)[...] = pair(stg, p * slots + k)[...]
        return 0

    lax.fori_loop(0, peers, spread, 0)
    keep = pltpu.make_async_copy(base2, base_hbm, sems.at[1])
    keep.start()
    load.wait()

    chunk = 128
    lane = lanes(chunk)

    def error(i, _):
        row = pl.multiple_of(i * chunk, chunk)
        lab = labk[pl.ds(row, chunk), :]
        known = lab >= 0.0
        for h in range(2):
            rows = pl.ds(2 * row + h, chunk, stride=2)
            onehot = jnp.where(lab == (lane + h * L).astype(F32), 1.0, 0.0)
            v2[rows, :] = jnp.where(known, onehot - base2[rows, :], 0.0)
        return 0

    lax.fori_loop(0, n // chunk, error, 0)
    v2[pl.ds(2 * n, 16), :] = jnp.zeros((16, L), F32)
    save = pltpu.make_async_copy(v2, e_hbm, sems.at[2])
    save.start()
    pack(bnd, v2, stgb, out, None, peers=peers, slots=bnd.shape[2], per=per, rest=rest)
    keep.wait()
    save.wait()


def tiles_kernel(tiles, cols, labels, mask, nh_hbm, nl_hbm, fh, fl, lab_hbm, cnt, nh, nl, labk, sems):
    blocks = labels.shape[0]
    halo = fh.shape[1] // L

    def body(b, _):
        rows = pl.ds(pl.multiple_of(b * L, L), L)
        for j in range(LOC_ROW):
            hi, lo = split(tiles[b * TILES_ROW + j])
            nh[rows, j * L : (j + 1) * L] = hi
            nl[rows, j * L : (j + 1) * L] = lo
        for q in range(halo):
            acc = jnp.zeros((L, L), F32)
            for j in range(LOC_ROW, TILES_ROW):
                hit = cols[b * TILES_ROW + j] == blocks + q
                acc = acc + jnp.where(hit, tiles[b * TILES_ROW + j], 0.0)
            hi, lo = split(acc)
            fh[rows, q * L : (q + 1) * L] = hi
            fl[rows, q * L : (q + 1) * L] = lo
        lab = jnp.where(mask[pl.ds(b, 1), :] > 0, labels[pl.ds(b, 1), :], -1).astype(F32)
        labk[rows, :] = jnp.broadcast_to(lab, (L, L)).T
        return 0

    lax.fori_loop(0, blocks, body, 0)
    pairs = ((nh, nh_hbm), (nl, nl_hbm), (labk, lab_hbm))
    saves = [pltpu.make_async_copy(a, b, sems.at[i]) for i, (a, b) in enumerate(pairs)]
    for c in saves:
        c.start()
    cnt[...] = jnp.zeros(cnt.shape, F32) + jnp.sum(mask[...].astype(F32))
    for c in saves:
        c.wait()


def near_kernel(v_hbm, e_hbm, nh_hbm, nl_hbm, cols, *refs, rate, classes, sums):
    if sums:
        cnt, part, tot, v2, e2, nh, nl, vh, vl, sems = refs
    else:
        part, v2, e2, nh, nl, vh, vl, sems = refs
    pairs = ((v_hbm, v2), (nh_hbm, nh), (nl_hbm, nl), (e_hbm, e2))
    loads = [pltpu.make_async_copy(a, b, sems.at[i]) for i, (a, b) in enumerate(pairs)]
    for c in loads:
        c.start()
    blocks = part.shape[0] // L
    loads[0].wait()

    def halve(b, _):
        rows = pl.ds(pl.multiple_of(b * L, L), L)
        for h in range(2):
            hi, lo = split(v2[pl.ds(b * 2 * L + h, L, stride=2), :])
            vh[rows, h * L : (h + 1) * L] = hi
            vl[rows, h * L : (h + 1) * L] = lo
        return 0

    lax.fori_loop(0, blocks, halve, 0)
    for c in loads[1:]:
        c.wait()

    def body(b, acc):
        rows = pl.ds(pl.multiple_of(b * L, L), L)
        at = [pl.ds(pl.multiple_of(cols[b * TILES_ROW + j] * L, L), L) for j in range(LOC_ROW)]
        bh = jnp.concatenate([vh[a, :] for a in at], 0)
        bl = jnp.concatenate([vl[a, :] for a in at], 0)
        a2 = dot(jnp.concatenate([nh[rows, :], nl[rows, :]], 0), bh)
        near = a2[:L] + a2[L:] + dot(nh[rows, :], bl)
        for h in range(2):
            ev = e2[pl.ds(b * 2 * L + h, L, stride=2), :]
            part[rows, h * L : (h + 1) * L] = (1.0 - rate) * ev + rate * near[:, h * L : (h + 1) * L]
            if sums:
                acc = acc + jnp.sum(jnp.abs(ev).reshape(L // 8, 8, L), 0)
        return acc

    acc = lax.fori_loop(0, blocks, body, jnp.zeros((8, L), F32))
    if sums:
        total = jnp.sum(acc) * (1.0 / classes)
        lane = lanes(8)
        tot[...] = jnp.where(lane == L - 2, total, jnp.where(lane == L - 1, cnt[...], 0.0))


def far_kernel(*refs, rate, classes, per, mode, peers, slots, n):
    rest = classes - L
    refs = list(refs)
    arr, fh, fl, part = refs[:4]
    refs = refs[4:]
    if mode != "last":
        bnd = refs.pop(0)
    if mode == "sums":
        tot = refs.pop(0)
    if mode == "turn":
        base_hbm, lab_hbm, base2, labk, sems = refs.pop(0), refs.pop(0), refs.pop(), refs.pop(), refs.pop()
        loads = [
            pltpu.make_async_copy(base_hbm, base2, sems.at[0]),
            pltpu.make_async_copy(lab_hbm, labk, sems.at[1]),
        ]
        for c in loads:
            c.start()
    if mode == "last":
        out, hm, hr = refs
    else:
        v_hbm, out, hm, hr, v2, stgb, vsem = refs
    ntail = up(slots, per)
    blk = slots + ntail
    tlane = lanes(peers)
    for k in range(slots):
        hm[pl.ds(k, peers, stride=slots), :] = arr[pl.ds(k, peers, stride=blk), :]
    for j in range(ntail):
        tail = arr[pl.ds(slots + j, peers, stride=blk), :]
        if j == 0 and mode == "turn":
            sums = jnp.sum(tail, axis=0, keepdims=True)
            sigma = sums[:, L - 2 : L - 1] / sums[:, L - 1 : L]
        for q in range(min(per, slots - j * per)):
            x = pltpu.roll(tail, (L - q * rest) % L, axis=1) if q else tail
            x = jnp.where(tlane < rest, x, 0.0)
            hr[pl.ds(j * per + q, peers, stride=slots), :] = x
    hh, hl = split(jnp.concatenate([hm[...], hr[...]], 1))
    if mode == "turn":
        for c in loads:
            c.wait()

    chunk = 256
    lane = lanes(chunk)

    def body(i, _):
        row = pl.multiple_of(i * chunk, chunk)
        rows = pl.ds(row, chunk)
        a2 = dot(jnp.concatenate([fh[rows, :], fl[rows, :]], 0), hh)
        far = a2[:chunk] + a2[chunk:] + dot(fh[rows, :], hl)
        v = part[rows, :] + rate * far
        if mode == "last":
            out[0:L, rows] = v[:, :L].T
            out[L:classes, rows] = v[:, L:].T[:rest]
            return 0
        if mode == "turn":
            mag = jnp.abs(v)
            mag = jnp.sum(mag[:, :L] + mag[:, L:], -1, keepdims=True) * (1.0 / classes) + tiny
            scale = sigma / mag
            lab = labk[rows, :]
        for h in range(2):
            x = v[:, h * L : (h + 1) * L]
            rows2 = pl.ds(2 * row + h, chunk, stride=2)
            if mode == "turn":
                onehot = jnp.where(lab == (lane + h * L).astype(F32), 1.0, 0.0)
                x = jnp.where(lab >= 0.0, onehot, base2[rows2, :] + scale * x)
            v2[rows2, :] = x
        return 0

    lax.fori_loop(0, n // chunk, body, 0)
    if mode != "last":
        v2[pl.ds(2 * n, 16), :] = jnp.zeros((16, L), F32)
        save = pltpu.make_async_copy(v2, v_hbm, vsem)
        save.start()
        extra = tot[0:1, :] if mode == "sums" else None
        pack(bnd, v2, stgb, out, extra, peers=peers, slots=slots, per=per, rest=rest)
        save.wait()


def call(kernel, outs, ins, args, scratch=(), vmem=0, flops=0, size=0, name=None, specs=None):
    if specs:
        outs = tuple(pltpu.HBM(o.shape, o.dtype) if p is HB else o for o, p in zip(outs, specs))
    args = [pltpu.with_memory_space_constraint(a, pltpu.HBM) if p is HB else a for a, p in zip(args, ins)]
    return pl.pallas_call(
        kernel,
        out_shape=outs,
        in_specs=ins,
        out_specs=specs or jax.tree.map(lambda _: VM, outs),
        scratch_shapes=list(scratch),
        compiler_params=pltpu.CompilerParams(vmem_limit_bytes=vmem),
        cost_estimate=pl.CostEstimate(flops=flops, bytes_accessed=size, transcendentals=0),
        name=name,
    )(*args)


def swap(x):
    return lax.all_to_all(x, "dom", split_axis=0, concat_axis=0, tiled=True)


def on_device(
    peers, hidden, bases, self_weight, coef, bias, edge_src, edge_dst, edge_rel, send_rows, recv_rows, labels,
    train_mask, bnd_rows, tiles, tile_cols,
):
    n, hdim = hidden.shape
    classes = self_weight.shape[1]
    nrel, nb = coef.shape
    rest = classes - L
    per = (L - 2) // rest
    slots = send_rows.shape[2]
    bnd = bnd_rows.shape[2]
    ne = edge_src.shape[0]
    halo = peers * bnd
    sds = jax.ShapeDtypeStruct
    state = sds((n, 2 * L), F32)
    half = sds((n, 2 * L), BF16)
    blocks = n // L

    dma = lambda k: pltpu.SemaphoreType.DMA((k,))
    blk = up(slots + up(slots, per), 8) * 8
    square = lambda x: x.reshape(-1, L)
    stage = pltpu.VMEM((2 * (peers * slots + 16), L), F32)
    rows2 = pltpu.VMEM((2 * n + 16, L), F32)
    sums = pltpu.VMEM((2 * nrel * n, L), F32)
    wide = (nb + 4) * L
    erows = ne // L
    bnd_rows = 2 * bnd_rows
    sent = call(
        functools.partial(scores_kernel, classes=classes, slots=slots, per=per),
        sds((peers, blk, L), F32),
        [VM, VM, VM, VM, SM, VM, VM, VM, VM],
        (hidden, bases.T, self_weight.T, bias.reshape(1, -1), coef)
        + (square(edge_src), square(edge_dst), square(edge_rel), send_rows),
        [pltpu.VMEM((wide, hdim), BF16)]
        + [pltpu.VMEM((256, wide), F32)] * 2
        + [sums] * 5
        + [rows2, stage]
        + [pltpu.VMEM((erows, L), jnp.int32)] * 2
        + [pltpu.VMEM((peers, L), jnp.int32), dma(erows), dma(erows), dma(peers)]
        + [pltpu.SMEM((1, L), jnp.int32)] * (2 * erows + peers),
        vmem=60 * MIB,
        name="scores",
    )
    arrived = swap(sent)
    spread = sds((2 * n + 16, L), F32)
    labv = pltpu.VMEM((n, L), F32)
    halfv = pltpu.VMEM((n, 2 * L), BF16)
    nh, nl, fh, fl, labk, cnt = call(
        tiles_kernel,
        (half, half, sds((n, halo), BF16), sds((n, halo), BF16), sds((n, L), F32), sds((8, L), F32)),
        [VM, SM, VM, VM],
        (tiles, tile_cols, square(labels), square(train_mask)),
        [halfv, halfv, labv, dma(3)],
        vmem=28 * MIB,
        flops=10**7,
        size=8 * 10**6,
        name="tiles",
        specs=(HB, HB, VM, VM, HB, VM),
    )
    lines = peers * (bnd + up(bnd, per))
    packed = sds((lines, L), F32)
    stageb = pltpu.VMEM((2 * halo, L), F32)
    base, v, out = call(
        functools.partial(errors_kernel, classes=classes, per=per, n=n),
        (spread, spread, packed),
        [VM, SM, SM, HB],
        (arrived, recv_rows, bnd_rows, labk),
        [stage, rows2, rows2, stageb, labv, dma(3)],
        vmem=28 * MIB,
        name="errors",
        specs=(HB, HB, VM),
    )
    e = v
    hscr = [pltpu.VMEM((halo, L), F32)] * 2
    for step in range(2 * ITERS):
        rate = correct_rate if step < ITERS else smooth_rate
        halos = swap(out.reshape(peers, 1, -1)).reshape(lines, L)
        sums = step == 0
        mode = "last" if step == 2 * ITERS - 1 else "turn" if step == ITERS - 1 else "sums" if step == ITERS - 2 else "step"
        got = call(
            functools.partial(near_kernel, rate=rate, classes=classes, sums=sums),
            (state, sds((8, L), F32)) if sums else (state,),
            [HB, HB, HB, HB, SM] + [VM] * sums,
            (v, e, nh, nl, tile_cols) + ((cnt,) if sums else ()),
            [rows2, rows2, halfv, halfv, halfv, halfv, dma(4)],
            vmem=24 * MIB,
            flops=10**9,
            size=8 * 10**6,
            name="near",
        )
        part = got[0]
        if sums:
            tot = got[1]
        far = functools.partial(
            far_kernel, rate=rate, classes=classes, per=per, mode=mode, peers=peers, slots=bnd, n=n
        )
        args, ins = (halos, fh, fl, part), [VM] * 4
        if mode == "last":
            return call(far, sds((classes, n), F32), ins, args, hscr, vmem=24 * MIB, name="far_last").T
        args, ins = args + (bnd_rows,), ins + [SM]
        scratch = hscr + [rows2, stageb, pltpu.SemaphoreType.DMA]
        if mode == "sums":
            args, ins = args + (tot,), ins + [VM]
        if mode == "turn":
            args, ins = args + (base, labk), ins + [HB, HB]
            scratch = scratch + [dma(2), labv, rows2]
        v, out = call(
            far, (spread, packed), ins, args, scratch, vmem=24 * MIB, name="far_" + mode, specs=(HB, VM)
        )
        if mode == "turn":
            e = v


def solution(mesh):
    row = P("dom")
    in_specs = (
        P("dom", None), P(), P(), P(), P(), row, row, row, P("dom", None, None), P("dom", None, None), row, row,
        P("dom", None, None), P("dom", None, None), row,
    )
    return jax.shard_map(
        functools.partial(on_device, mesh.shape["dom"]),
        mesh=mesh,
        in_specs=in_specs,
        out_specs=P("dom", None),
        check_vma=False,
    )
```

```python
import functools

import jax
import jax.numpy as jnp
from jax import lax
from jax.experimental import pallas as pl
from jax.experimental.pallas import tpu as pltpu
from jax.sharding import PartitionSpec as P

TILES_ROW = 4
LOC_ROW = 2
ITERS = 3
L = 128

correct_rate = 0.8
smooth_rate = 0.75
tiny = 1e-06

F32 = jnp.float32
BF16 = jnp.bfloat16
VM = pl.BlockSpec(memory_space=pltpu.VMEM)
SM = pl.BlockSpec(memory_space=pltpu.SMEM)
HB = pl.BlockSpec(memory_space=pltpu.HBM)
MIB = 1 << 20


def up(a, b):
    return -(-a // b)


def split(x):
    hi = x.astype(BF16)
    return hi, (x - hi.astype(F32)).astype(BF16)


def dot(a, b):
    return jnp.dot(a, b, preferred_element_type=F32)


def lanes(rows):
    return lax.broadcasted_iota(jnp.int32, (rows, L), 1)


def pair(ref, row):
    return ref.at[pl.ds(pl.multiple_of(2 * row, 2), 2), :]


def gather_rows(idx_ref, src, stg, peers, slots):
    group = 4

    def body(g, _):
        for p in range(group):
            for k in range(slots):
                at = pl.ds(pl.multiple_of(idx_ref[0, g * group + p, k], 2), 2)
                pair(stg, g * (group * slots) + (p * slots + k))[...] = src[at, :]
        return 0

    lax.fori_loop(0, peers // group, body, 0)


def fetch(src, rows, refs, sems):
    copies = [pltpu.make_async_copy(src.at[pl.ds(i, 1), :], r, sems.at[i]) for i, r in zip(rows, refs)]
    for c in copies:
        c.start()
    return copies


def scores_kernel(
    hid, bt, st, bias, coef, es, ed, er, send, out, blank,
    pt, p0, m2, s0, s1, s2, s3, sc2, stg, kj, kd, kp, zero, sj, sd, sp, sz, *ks, classes, slots, per,
):
    n, hdim = hid.shape
    rest = classes - L
    nrel, nb = coef.shape
    peers = out.shape[0]
    erows = es.shape[0]
    acc = (s0, s1, s2, s3)
    ksj, ksd, ksp = ks[:erows], ks[erows : 2 * erows], ks[2 * erows :]
    kj[...] = (er[...] * n + es[...]) * 2
    kd[...] = (er[...] * n + ed[...]) * 2
    kp[:, 0:slots] = send[0] * 2
    copies = fetch(kj, range(erows), ksj, sj) + fetch(kd, range(erows), ksd, sd) + fetch(kp, range(peers), ksp, sp)
    zero[...] = jnp.zeros_like(zero)
    wipe = pltpu.make_async_copy(zero, blank, sz.at[0])
    wipe.start()

    base_r = nb * L
    base_s = base_r + 2 * L
    gap = 2 * L // nb
    step = 2 * L

    def arrange(i, _):
        cols = pl.ds(pl.multiple_of(i * step, step), step)
        for b in range(nb):
            x = bt[b * classes : (b + 1) * classes, cols].astype(F32)
            pt[b * L : (b + 1) * L, cols] = x[:L].astype(BF16)
            tail = jnp.concatenate([x[L:], jnp.zeros((gap - rest, step), F32)], 0)
            pt[base_r + b * gap : base_r + (b + 1) * gap, cols] = tail.astype(BF16)
        x = st[:, cols].astype(F32)
        pt[base_s : base_s + L, cols] = x[:L].astype(BF16)
        tail = jnp.concatenate([x[L:], jnp.zeros((L - rest, step), F32)], 0)
        pt[base_s + L : base_s + 2 * L, cols] = tail.astype(BF16)
        return 0

    lax.fori_loop(0, hdim // step, arrange, 0)
    wipe.wait()
    zrows = blank.shape[0]
    for c, s in enumerate(acc):
        for i in range(nrel):
            copies.append(pltpu.make_async_copy(blank, s.at[pl.ds(i * zrows, zrows), :], sz.at[1 + c * nrel + i]))
            copies[-1].start()

    chunk = p0.shape[0]
    sub = 32
    lane = lanes(sub)
    one = jnp.where(lane == rest, 1.0, 0.0)
    lane8 = lanes(8)
    gains = []
    for r in range(nrel):
        for h in range(2):
            g = jnp.zeros((8, L), F32)
            for b in range(nb // 2):
                g = jnp.where(lane8 // gap == b, coef[r, h * (nb // 2) + b], g)
            gains.append(g[0:1])
    bias0 = bias[0:1, 0:L]
    bias1 = jnp.concatenate([bias[0:1, L:classes], jnp.zeros((1, L - rest), F32)], 1)

    def project(i, _):
        row0 = pl.multiple_of(i * chunk, chunk)
        h = hid[pl.ds(row0, chunk), :]
        for j in range(0, base_s + 2 * L, 2 * L):
            p0[:, j : j + 2 * L] = lax.dot_general(
                h, pt[j : j + 2 * L, :], (((1,), (1,)), ((), ())), preferred_element_type=F32
            )

        def mix(u, _):
            rows = pl.ds(pl.multiple_of(u * sub, sub), sub)
            row = row0 + u * sub
            mains = [p0[rows, b * L : (b + 1) * L] for b in range(nb)]
            q = [p0[rows, base_r + h * L : base_r + (h + 1) * L] for h in range(2)]
            for r in range(nrel):
                x = coef[r, 0] * mains[0]
                for b in range(1, nb):
                    x = x + coef[r, b] * mains[b]
                t = gains[2 * r] * q[0] + gains[2 * r + 1] * q[1]
                turn = L // 2
                while turn >= gap:
                    t = t + pltpu.roll(t, turn, axis=1)
                    turn //= 2
                at = 2 * (r * n + row)
                m2[pl.ds(at, sub, stride=2), :] = x
                m2[pl.ds(at + 1, sub, stride=2), :] = jnp.where(lane < rest, t, one)
            at = 2 * row
            sc2[pl.ds(at, sub, stride=2), :] = p0[rows, base_s : base_s + L] + bias0
            sc2[pl.ds(at + 1, sub, stride=2), :] = p0[rows, base_s + L : base_s + 2 * L] + bias1
            return 0

        lax.fori_loop(0, chunk // sub, mix, 0)
        return 0

    sc2[pl.ds(2 * n, 16), :] = jnp.zeros((16, L), F32)
    lax.fori_loop(0, n // chunk, project, 0)
    for c in copies:
        c.wait()

    def edges(t, _):
        for v in range(2):
            for e in range(erows):
                s = acc[e % 4]
                j = ksj[e][0, 2 * t + v]
                d = ksd[e][0, 2 * t + v]
                src = m2[pl.ds(pl.multiple_of(j, 2), 2), :]
                at = pl.ds(pl.multiple_of(d, 2), 2)
                s[at, :] = s[at, :] + src
        return 0

    lax.fori_loop(0, L // 2, edges, 0)

    fin = 128
    flane = lanes(fin)

    def finish(i, _):
        row = i * fin
        a0 = sc2[pl.ds(2 * row, fin, stride=2), :]
        a1 = sc2[pl.ds(2 * row + 1, fin, stride=2), :]
        for r in range(nrel):
            rows = [pl.ds(2 * (r * n + row) + h, fin, stride=2) for h in range(2)]
            m, t = [(s0[w, :] + s1[w, :]) + (s2[w, :] + s3[w, :]) for w in rows]
            inv = 1.0 / jnp.maximum(t[:, rest : rest + 1], 1.0)
            a0 = a0 + m * inv
            a1 = a1 + t * inv
        sc2[pl.ds(2 * row, fin, stride=2), :] = a0
        sc2[pl.ds(2 * row + 1, fin, stride=2), :] = jnp.where(flane < rest, a1, 0.0)
        return 0

    lax.fori_loop(0, n // fin, finish, 0)

    def collect(k, _):
        for p in range(peers):
            at = pl.ds(pl.multiple_of(ksp[p][0, k], 2), 2)
            pair(stg, p * slots + k)[...] = sc2[at, :]
        return 0

    lax.fori_loop(0, slots, collect, 0)
    ntail = up(slots, per)

    def put(p, _):
        at = p * 2 * slots
        out[p, 0:slots, :] = stg[pl.ds(at, slots, stride=2), :]
        tail = stg[pl.ds(at + 1, ntail, stride=2 * per), :]
        for q in range(1, per):
            x = stg[pl.ds(at + 2 * q + 1, ntail, stride=2 * per), :]
            tail = tail + pltpu.roll(x, q * rest, axis=1)
        out[p, slots : slots + ntail, :] = tail
        return 0

    lax.fori_loop(0, peers, put, 0)


def pack(bnd, v2, stg, out, extra, *, peers, slots, per, rest):
    gather_rows(bnd, v2, stg, peers, slots)
    ntail = up(slots, per)
    blk = slots + ntail
    for k in range(slots):
        out[pl.ds(k, peers, stride=blk), :] = stg[pl.ds(2 * k, peers, stride=2 * slots), :]
    for j in range(ntail):
        tail = None
        for q in range(min(per, slots - j * per)):
            x = stg[pl.ds(2 * (j * per + q) + 1, peers, stride=2 * slots), :]
            x = pltpu.roll(x, q * rest, axis=1) if q else x
            tail = x if tail is None else tail + x
        if j == 0 and extra is not None:
            tail = tail + extra
        out[pl.ds(slots + j, peers, stride=blk), :] = tail


def errors_kernel(
    arr, recv, bnd, labk_hbm, base_hbm, e_hbm, out, stg, base2, v2, stgb, labk, kr, sems, sr, esem, *ksr,
    classes, per, n,
):
    rest = classes - L
    peers, blk, _ = arr.shape
    slots = recv.shape[2]
    ntail = up(slots, per)
    tlane = lanes(ntail)
    load = pltpu.make_async_copy(labk_hbm, labk, sems.at[0])
    load.start()
    kr[:, 0:slots] = recv[0] * 2
    copies = fetch(kr, range(peers), ksr, sr)

    def unpack(p, _):
        at = p * 2 * slots
        tail = arr[p, slots : slots + ntail, :]
        for q in range(per):
            x = pltpu.roll(tail, (L - q * rest) % L, axis=1) if q else tail
            x = jnp.where(tlane < rest, x, 0.0)
            stg[pl.ds(at + 2 * q + 1, ntail, stride=2 * per), :] = x
        stg[pl.ds(at, slots, stride=2), :] = arr[p, 0:slots, :]
        return 0

    lax.fori_loop(0, peers, unpack, 0)

    for c in copies:
        c.wait()
    unroll = 2

    def spread(t, _):
        for v in range(unroll):
            k = t * unroll + v
            for p in range(peers):
                at = pl.ds(pl.multiple_of(ksr[p][0, k], 2), 2)
                base2[at, :] = pair(stg, p * slots + k)[...]
        return 0

    lax.fori_loop(0, slots // unroll, spread, 0)
    keep = pltpu.make_async_copy(base2.at[pl.ds(0, 2 * n), :], base_hbm, sems.at[1])
    keep.start()
    load.wait()

    chunk = 128
    lane = lanes(chunk)

    def error(i, _):
        row = pl.multiple_of(i * chunk, chunk)
        lab = labk[pl.ds(row, chunk), :]
        known = lab >= 0.0
        for h in range(2):
            rows = pl.ds(2 * row + h, chunk, stride=2)
            onehot = jnp.where(lab == (lane + h * L).astype(F32), 1.0, 0.0)
            v2[rows, :] = jnp.where(known, onehot - base2[rows, :], 0.0)
        piece(i).start()
        return 0

    def piece(i):
        rows = pl.ds(pl.multiple_of(2 * i * chunk, 2 * chunk), 2 * chunk)
        return pltpu.make_async_copy(v2.at[rows, :], e_hbm.at[rows, :], esem.at[i])

    v2[pl.ds(2 * n, 16), :] = jnp.zeros((16, L), F32)
    lax.fori_loop(0, n // chunk, error, 0)
    pack(bnd, v2, stgb, out, None, peers=peers, slots=bnd.shape[2], per=per, rest=rest)
    keep.wait()
    for i in range(n // chunk):
        piece(i).wait()


def tiles_kernel(tiles, cols, labels, mask, nh_hbm, nl_hbm, fh, fl, lab_hbm, cnt, nh, nl, labk, sems):
    blocks = labels.shape[0]
    halo = fh.shape[1] // L

    def body(b, _):
        rows = pl.ds(pl.multiple_of(b * L, L), L)
        for j in range(LOC_ROW):
            hi, lo = split(tiles[b * TILES_ROW + j])
            nh[rows, j * L : (j + 1) * L] = hi
            nl[rows, j * L : (j + 1) * L] = lo
        for q in range(halo):
            acc = jnp.zeros((L, L), F32)
            for j in range(LOC_ROW, TILES_ROW):
                hit = cols[b * TILES_ROW + j] == blocks + q
                acc = acc + jnp.where(hit, tiles[b * TILES_ROW + j], 0.0)
            hi, lo = split(acc)
            fh[rows, q * L : (q + 1) * L] = hi
            fl[rows, q * L : (q + 1) * L] = lo
        lab = jnp.where(mask[pl.ds(b, 1), :] > 0, labels[pl.ds(b, 1), :], -1).astype(F32)
        labk[rows, :] = jnp.broadcast_to(lab, (L, L)).T
        return 0

    lax.fori_loop(0, blocks, body, 0)
    pairs = ((nh, nh_hbm), (nl, nl_hbm), (labk, lab_hbm))
    saves = [pltpu.make_async_copy(a, b, sems.at[i]) for i, (a, b) in enumerate(pairs)]
    for c in saves:
        c.start()
    cnt[...] = jnp.zeros(cnt.shape, F32) + jnp.sum(mask[...].astype(F32))
    for c in saves:
        c.wait()


def near_kernel(v_hbm, e_hbm, nh_hbm, nl_hbm, cols, *refs, rate, classes, sums):
    if sums:
        cnt, part, tot, v2, e2, nh, nl, vh, vl, sems = refs
    else:
        part, v2, e2, nh, nl, vh, vl, sems = refs
    pairs = ((v_hbm, v2), (nh_hbm, nh), (nl_hbm, nl), (e_hbm, e2))
    loads = [pltpu.make_async_copy(a, b, sems.at[i]) for i, (a, b) in enumerate(pairs)]
    for c in loads:
        c.start()
    blocks = part.shape[0] // L
    loads[0].wait()

    def halve(b, _):
        rows = pl.ds(pl.multiple_of(b * L, L), L)
        for h in range(2):
            hi, lo = split(v2[pl.ds(b * 2 * L + h, L, stride=2), :])
            vh[rows, h * L : (h + 1) * L] = hi
            vl[rows, h * L : (h + 1) * L] = lo
        return 0

    lax.fori_loop(0, blocks, halve, 0)
    for c in loads[1:]:
        c.wait()

    def body(b, acc):
        rows = pl.ds(pl.multiple_of(b * L, L), L)
        at = [pl.ds(pl.multiple_of(cols[b * TILES_ROW + j] * L, L), L) for j in range(LOC_ROW)]
        bh = jnp.concatenate([vh[a, :] for a in at], 0)
        bl = jnp.concatenate([vl[a, :] for a in at], 0)
        a2 = dot(jnp.concatenate([nh[rows, :], nl[rows, :]], 0), bh)
        near = a2[:L] + a2[L:] + dot(nh[rows, :], bl)
        for h in range(2):
            ev = e2[pl.ds(b * 2 * L + h, L, stride=2), :]
            part[rows, h * L : (h + 1) * L] = (1.0 - rate) * ev + rate * near[:, h * L : (h + 1) * L]
            if sums:
                acc = acc + jnp.sum(jnp.abs(ev).reshape(L // 8, 8, L), 0)
        return acc

    acc = lax.fori_loop(0, blocks, body, jnp.zeros((8, L), F32))
    if sums:
        total = jnp.sum(acc) * (1.0 / classes)
        lane = lanes(8)
        tot[...] = jnp.where(lane == L - 2, total, jnp.where(lane == L - 1, cnt[...], 0.0))


def far_kernel(*refs, rate, classes, per, mode, peers, slots, n):
    rest = classes - L
    refs = list(refs)
    arr, fh, fl, part = refs[:4]
    refs = refs[4:]
    if mode != "last":
        bnd = refs.pop(0)
    if mode == "sums":
        tot = refs.pop(0)
    if mode == "turn":
        base_hbm, lab_hbm, base2, labk, sems = refs.pop(0), refs.pop(0), refs.pop(), refs.pop(), refs.pop()
        loads = [
            pltpu.make_async_copy(base_hbm, base2, sems.at[0]),
            pltpu.make_async_copy(lab_hbm, labk, sems.at[1]),
        ]
        for c in loads:
            c.start()
    if mode == "last":
        out, hm, hr = refs
    else:
        v_hbm, out, hm, hr, v2, stgb, vsem = refs
    ntail = up(slots, per)
    blk = slots + ntail
    tlane = lanes(peers)
    for k in range(slots):
        hm[pl.ds(k, peers, stride=slots), :] = arr[pl.ds(k, peers, stride=blk), :]
    for j in range(ntail):
        tail = arr[pl.ds(slots + j, peers, stride=blk), :]
        if j == 0 and mode == "turn":
            sums = jnp.sum(tail, axis=0, keepdims=True)
            sigma = sums[:, L - 2 : L - 1] / sums[:, L - 1 : L]
        for q in range(min(per, slots - j * per)):
            x = pltpu.roll(tail, (L - q * rest) % L, axis=1) if q else tail
            x = jnp.where(tlane < rest, x, 0.0)
            hr[pl.ds(j * per + q, peers, stride=slots), :] = x
    hh, hl = split(jnp.concatenate([hm[...], hr[...]], 1))
    if mode == "turn":
        for c in loads:
            c.wait()

    chunk = n // 2
    lane = lanes(chunk)
    count = n // chunk

    def piece(i):
        rows = pl.ds(pl.multiple_of(2 * i * chunk, 2 * chunk), 2 * chunk)
        return pltpu.make_async_copy(v2.at[rows, :], v_hbm.at[rows, :], vsem.at[i])

    if mode != "last":
        v2[pl.ds(2 * n, 16), :] = jnp.zeros((16, L), F32)

    def body(i, _):
        row = pl.multiple_of(i * chunk, chunk)
        rows = pl.ds(row, chunk)
        a2 = dot(jnp.concatenate([fh[rows, :], fl[rows, :]], 0), hh)
        far = a2[:chunk] + a2[chunk:] + dot(fh[rows, :], hl)
        v = part[rows, :] + rate * far
        if mode == "last":
            out[0:L, rows] = v[:, :L].T
            out[L:classes, rows] = v[:, L:].T[:rest]
            return 0
        if mode == "turn":
            mag = jnp.abs(v)
            mag = jnp.sum(mag[:, :L] + mag[:, L:], -1, keepdims=True) * (1.0 / classes) + tiny
            scale = sigma / mag
            lab = labk[rows, :]
        for h in range(2):
            x = v[:, h * L : (h + 1) * L]
            rows2 = pl.ds(2 * row + h, chunk, stride=2)
            if mode == "turn":
                onehot = jnp.where(lab == (lane + h * L).astype(F32), 1.0, 0.0)
                x = jnp.where(lab >= 0.0, onehot, base2[rows2, :] + scale * x)
            v2[rows2, :] = x
        piece(i).start()
        return 0

    lax.fori_loop(0, count, body, 0)
    if mode != "last":
        extra = tot[0:1, :] if mode == "sums" else None
        pack(bnd, v2, stgb, out, extra, peers=peers, slots=slots, per=per, rest=rest)
        for i in range(count):
            piece(i).wait()


def call(kernel, outs, ins, args, scratch=(), vmem=0, flops=0, size=0, name=None, specs=None):
    if specs:
        outs = tuple(pltpu.HBM(o.shape, o.dtype) if p is HB else o for o, p in zip(outs, specs))
    args = [pltpu.with_memory_space_constraint(a, pltpu.HBM) if p is HB else a for a, p in zip(args, ins)]
    return pl.pallas_call(
        kernel,
        out_shape=outs,
        in_specs=ins,
        out_specs=specs or jax.tree.map(lambda _: VM, outs),
        scratch_shapes=list(scratch),
        compiler_params=pltpu.CompilerParams(vmem_limit_bytes=vmem),
        cost_estimate=pl.CostEstimate(flops=flops, bytes_accessed=size, transcendentals=0),
        name=name,
    )(*args)


def swap(x):
    return lax.all_to_all(x, "dom", split_axis=0, concat_axis=0, tiled=True)


def on_device(
    peers, hidden, bases, self_weight, coef, bias, edge_src, edge_dst, edge_rel, send_rows, recv_rows, labels,
    train_mask, bnd_rows, tiles, tile_cols,
):
    n, hdim = hidden.shape
    classes = self_weight.shape[1]
    nrel, nb = coef.shape
    rest = classes - L
    per = (L - 2) // rest
    slots = send_rows.shape[2]
    bnd = bnd_rows.shape[2]
    ne = edge_src.shape[0]
    halo = peers * bnd
    sds = jax.ShapeDtypeStruct
    state = sds((n, 2 * L), F32)
    half = sds((n, 2 * L), BF16)
    blocks = n // L

    dma = lambda k: pltpu.SemaphoreType.DMA((k,))
    blk = up(slots + up(slots, per), 8) * 8
    square = lambda x: x.reshape(-1, L)
    stage = pltpu.VMEM((2 * (peers * slots + 16), L), F32)
    rows2 = pltpu.VMEM((2 * n + 16, L), F32)
    sums = pltpu.VMEM((2 * nrel * n, L), F32)
    wide = (nb + 4) * L
    erows = ne // L
    bnd_rows = 2 * bnd_rows
    sent, _ = call(
        functools.partial(scores_kernel, classes=classes, slots=slots, per=per),
        (sds((peers, blk, L), F32), sds((2 * n, L), F32)),
        [VM, VM, VM, VM, SM, VM, VM, VM, VM],
        (hidden, bases.T, self_weight.T, bias.reshape(1, -1), coef)
        + (square(edge_src), square(edge_dst), square(edge_rel), send_rows),
        [pltpu.VMEM((wide, hdim), BF16)]
        + [pltpu.VMEM((n // 2, wide), F32)]
        + [sums] * 5
        + [rows2, stage]
        + [pltpu.VMEM((erows, L), jnp.int32)] * 2
        + [pltpu.VMEM((peers, L), jnp.int32), pltpu.VMEM((2 * n, L), F32), dma(erows), dma(erows), dma(peers)]
        + [dma(1 + 4 * nrel)]
        + [pltpu.SMEM((1, L), jnp.int32)] * (2 * erows + peers),
        vmem=60 * MIB,
        name="scores",
        specs=(VM, HB),
    )
    arrived = swap(sent)
    spread = sds((2 * n, L), F32)
    flat2 = pltpu.VMEM((2 * n, L), F32)
    labv = pltpu.VMEM((n, L), F32)
    halfv = pltpu.VMEM((n, 2 * L), BF16)
    nh, nl, fh, fl, labk, cnt = call(
        tiles_kernel,
        (half, half, sds((n, halo), BF16), sds((n, halo), BF16), sds((n, L), F32), sds((8, L), F32)),
        [VM, SM, VM, VM],
        (tiles, tile_cols, square(labels), square(train_mask)),
        [halfv, halfv, labv, dma(3)],
        vmem=28 * MIB,
        flops=10**7,
        size=8 * 10**6,
        name="tiles",
        specs=(HB, HB, VM, VM, HB, VM),
    )
    lines = peers * (bnd + up(bnd, per))
    packed = sds((lines, L), F32)
    stageb = pltpu.VMEM((2 * halo, L), F32)
    base, v, out = call(
        functools.partial(errors_kernel, classes=classes, per=per, n=n),
        (spread, spread, packed),
        [VM, VM, SM, HB],
        (arrived, recv_rows, bnd_rows, labk),
        [stage, rows2, rows2, stageb, labv, pltpu.VMEM((peers, L), jnp.int32), dma(2), dma(peers), dma(n // L)]
        + [pltpu.SMEM((1, L), jnp.int32)] * peers,
        vmem=28 * MIB,
        name="errors",
        specs=(HB, HB, VM),
    )
    e = v
    hscr = [pltpu.VMEM((halo, L), F32)] * 2
    for step in range(2 * ITERS):
        rate = correct_rate if step < ITERS else smooth_rate
        halos = swap(out.reshape(peers, 1, -1)).reshape(lines, L)
        sums = step == 0
        mode = "last" if step == 2 * ITERS - 1 else "turn" if step == ITERS - 1 else "sums" if step == ITERS - 2 else "step"
        got = call(
            functools.partial(near_kernel, rate=rate, classes=classes, sums=sums),
            (state, sds((8, L), F32)) if sums else (state,),
            [HB, HB, HB, HB, SM] + [VM] * sums,
            (v, e, nh, nl, tile_cols) + ((cnt,) if sums else ()),
            [flat2, flat2, halfv, halfv, halfv, halfv, dma(4)],
            vmem=24 * MIB,
            flops=10**9,
            size=8 * 10**6,
            name="near",
        )
        part = got[0]
        if sums:
            tot = got[1]
        far = functools.partial(
            far_kernel, rate=rate, classes=classes, per=per, mode=mode, peers=peers, slots=bnd, n=n
        )
        args, ins = (halos, fh, fl, part), [VM] * 4
        if mode == "last":
            return call(far, sds((classes, n), F32), ins, args, hscr, vmem=24 * MIB, name="far_last").T
        args, ins = args + (bnd_rows,), ins + [SM]
        scratch = hscr + [rows2, stageb, dma(n // L)]
        if mode == "sums":
            args, ins = args + (tot,), ins + [VM]
        if mode == "turn":
            args, ins = args + (base, labk), ins + [HB, HB]
            scratch = scratch + [dma(2), labv, flat2]
        v, out = call(
            far, (spread, packed), ins, args, scratch, vmem=24 * MIB, name="far_" + mode, specs=(HB, VM)
        )
        if mode == "turn":
            e = v


def solution(mesh):
    row = P("dom")
    in_specs = (
        P("dom", None), P(), P(), P(), P(), row, row, row, P("dom", None, None), P("dom", None, None), row, row,
        P("dom", None, None), P("dom", None, None), row,
    )
    return jax.shard_map(
        functools.partial(on_device, mesh.shape["dom"]),
        mesh=mesh,
        in_specs=in_specs,
        out_specs=P("dom", None),
        check_vma=False,
    )
```

```python
import functools

import jax
import jax.numpy as jnp
from jax import lax
from jax.experimental import pallas as pl
from jax.experimental.pallas import tpu as pltpu
from jax.sharding import PartitionSpec as P

TILES_ROW = 4
LOC_ROW = 2
ITERS = 3
L = 128

correct_rate = 0.8
smooth_rate = 0.75
tiny = 1e-06

F32 = jnp.float32
BF16 = jnp.bfloat16
VM = pl.BlockSpec(memory_space=pltpu.VMEM)
SM = pl.BlockSpec(memory_space=pltpu.SMEM)
HB = pl.BlockSpec(memory_space=pltpu.HBM)
VO = pl.BlockSpec(memory_space=pltpu.VMEM)
MIB = 1 << 20


def up(a, b):
    return -(-a // b)


def split(x):
    hi = x.astype(BF16)
    return hi, (x - hi.astype(F32)).astype(BF16)


def dot(a, b):
    return jnp.dot(a, b, preferred_element_type=F32)


def lanes(rows):
    return lax.broadcasted_iota(jnp.int32, (rows, L), 1)


def pair(ref, row):
    return ref.at[pl.ds(pl.multiple_of(2 * row, 2), 2), :]


def gather_rows(idx, src, stg, peers, slots):
    copy, idx_ref = idx
    copy.wait()
    group = 4

    def body(g, _):
        for p in range(group):
            for k in range(slots):
                at = pl.ds(pl.multiple_of(idx_ref[g * group + p, k], 2), 2)
                pair(stg, g * (group * slots) + (p * slots + k))[...] = src[at, :]
        return 0

    lax.fori_loop(0, peers // group, body, 0)


def fetch(src, rows, refs, sems):
    copies = [pltpu.make_async_copy(src.at[pl.ds(i, 1), :], r, sems.at[i]) for i, r in zip(rows, refs)]
    for c in copies:
        c.start()
    return copies


def scores_kernel(
    hid_hbm, bt, st, bias, coef, es, ed, er, send, out, blank,
    hid, pt, p0, m2, s0, s1, s2, s3, sc2, stg, kj, kd, kp, zero, sj, sd, sp, sz, *ks, classes, slots, per,
):
    n, hdim = hid.shape
    hload = pltpu.make_async_copy(hid_hbm, hid, sz.at[1 + 4 * coef.shape[0]])
    hload.start()
    rest = classes - L
    nrel, nb = coef.shape
    peers = out.shape[0]
    erows = es.shape[0]
    acc = (s0, s1, s2, s3)
    ksj, ksd, ksp = ks[:erows], ks[erows : 2 * erows], ks[2 * erows :]
    kj[...] = (er[...] * n + es[...]) * 2
    kd[...] = (er[...] * n + ed[...]) * 2
    kp[:, 0:slots] = send[0] * 2
    copies = fetch(kj, range(erows), ksj, sj) + fetch(kd, range(erows), ksd, sd) + fetch(kp, range(peers), ksp, sp)
    zero[...] = jnp.zeros_like(zero)
    wipe = pltpu.make_async_copy(zero, blank, sz.at[0])
    wipe.start()

    base_r = nb * L
    base_s = base_r + 2 * L
    gap = 2 * L // nb
    step = 2 * L

    def arrange(i, _):
        cols = pl.ds(pl.multiple_of(i * step, step), step)
        for b in range(nb):
            x = bt[b * classes : (b + 1) * classes, cols].astype(F32)
            pt[b * L : (b + 1) * L, cols] = x[:L].astype(BF16)
            tail = jnp.concatenate([x[L:], jnp.zeros((gap - rest, step), F32)], 0)
            pt[base_r + b * gap : base_r + (b + 1) * gap, cols] = tail.astype(BF16)
        x = st[:, cols].astype(F32)
        pt[base_s : base_s + L, cols] = x[:L].astype(BF16)
        tail = jnp.concatenate([x[L:], jnp.zeros((L - rest, step), F32)], 0)
        pt[base_s + L : base_s + 2 * L, cols] = tail.astype(BF16)
        return 0

    lax.fori_loop(0, hdim // step, arrange, 0)
    wipe.wait()
    zrows = blank.shape[0]
    for c, s in enumerate(acc[:3]):
        for i in range(nrel):
            copies.append(pltpu.make_async_copy(blank, s.at[pl.ds(i * zrows, zrows), :], sz.at[1 + c * nrel + i]))
            copies[-1].start()

    chunk = p0.shape[0]
    sub = 32
    lane = lanes(sub)
    one = jnp.where(lane == rest, 1.0, 0.0)
    lane8 = lanes(8)
    gains = []
    for r in range(nrel):
        for h in range(2):
            g = jnp.zeros((8, L), F32)
            for b in range(nb // 2):
                g = jnp.where(lane8 // gap == b, coef[r, h * (nb // 2) + b], g)
            gains.append(g[0:1])
    bias0 = bias[0:1, 0:L]
    bias1 = jnp.concatenate([bias[0:1, L:classes], jnp.zeros((1, L - rest), F32)], 1)

    def project(i, _):
        row0 = pl.multiple_of(i * chunk, chunk)
        h = hid[pl.ds(row0, chunk), :]
        for j in range(0, base_s + 2 * L, 2 * L):
            p0[:, j : j + 2 * L] = lax.dot_general(
                h, pt[j : j + 2 * L, :], (((1,), (1,)), ((), ())), preferred_element_type=F32
            )

        def mix(u, _):
            rows = pl.ds(pl.multiple_of(u * sub, sub), sub)
            row = row0 + u * sub
            mains = [p0[rows, b * L : (b + 1) * L] for b in range(nb)]
            q = [p0[rows, base_r + h * L : base_r + (h + 1) * L] for h in range(2)]
            for r in range(nrel):
                x = coef[r, 0] * mains[0]
                for b in range(1, nb):
                    x = x + coef[r, b] * mains[b]
                t = gains[2 * r] * q[0] + gains[2 * r + 1] * q[1]
                turn = L // 2
                while turn >= gap:
                    t = t + pltpu.roll(t, turn, axis=1)
                    turn //= 2
                at = 2 * (r * n + row)
                m2[pl.ds(at, sub, stride=2), :] = x
                m2[pl.ds(at + 1, sub, stride=2), :] = jnp.where(lane < rest, t, one)
            at = 2 * row
            sc2[pl.ds(at, sub, stride=2), :] = p0[rows, base_s : base_s + L] + bias0
            sc2[pl.ds(at + 1, sub, stride=2), :] = p0[rows, base_s + L : base_s + 2 * L] + bias1
            return 0

        lax.fori_loop(0, chunk // sub, mix, 0)
        return 0

    sc2[pl.ds(2 * n, 16), :] = jnp.zeros((16, L), F32)
    hload.wait()
    lax.fori_loop(0, n // chunk, project, 0)

    def clear(i, _):
        s3[pl.ds(pl.multiple_of(i * 512, 512), 512), :] = jnp.zeros((512, L), F32)
        return 0

    lax.fori_loop(0, s3.shape[0] // 512, clear, 0)
    for c in copies:
        c.wait()

    def edges(t, _):
        for v in range(2):
            for e in range(erows):
                s = acc[e % 4]
                j = ksj[e][0, 2 * t + v]
                d = ksd[e][0, 2 * t + v]
                src = m2[pl.ds(pl.multiple_of(j, 2), 2), :]
                at = pl.ds(pl.multiple_of(d, 2), 2)
                s[at, :] = s[at, :] + src
        return 0

    lax.fori_loop(0, L // 2, edges, 0)

    fin = 128
    flane = lanes(fin)

    def finish(i, _):
        row = i * fin
        a0 = sc2[pl.ds(2 * row, fin, stride=2), :]
        a1 = sc2[pl.ds(2 * row + 1, fin, stride=2), :]
        for r in range(nrel):
            rows = [pl.ds(2 * (r * n + row) + h, fin, stride=2) for h in range(2)]
            m, t = [(s0[w, :] + s1[w, :]) + (s2[w, :] + s3[w, :]) for w in rows]
            inv = 1.0 / jnp.maximum(t[:, rest : rest + 1], 1.0)
            a0 = a0 + m * inv
            a1 = a1 + t * inv
        sc2[pl.ds(2 * row, fin, stride=2), :] = a0
        sc2[pl.ds(2 * row + 1, fin, stride=2), :] = jnp.where(flane < rest, a1, 0.0)
        return 0

    lax.fori_loop(0, n // fin, finish, 0)

    def collect(k, _):
        for p in range(peers):
            at = pl.ds(pl.multiple_of(ksp[p][0, k], 2), 2)
            pair(stg, p * slots + k)[...] = sc2[at, :]
        return 0

    lax.fori_loop(0, slots, collect, 0)
    ntail = up(slots, per)

    def put(p, _):
        at = p * 2 * slots
        out[p, 0:slots, :] = stg[pl.ds(at, slots, stride=2), :]
        tail = stg[pl.ds(at + 1, ntail, stride=2 * per), :]
        for q in range(1, per):
            x = stg[pl.ds(at + 2 * q + 1, ntail, stride=2 * per), :]
            tail = tail + pltpu.roll(x, q * rest, axis=1)
        out[p, slots : slots + ntail, :] = tail
        return 0

    lax.fori_loop(0, peers, put, 0)


def pack(bnd, v2, stg, out, extra, *, peers, slots, per, rest):
    gather_rows(bnd, v2, stg, peers, slots)
    ntail = up(slots, per)
    blk = slots + ntail
    for k in range(slots):
        out[pl.ds(k, peers, stride=blk), :] = stg[pl.ds(2 * k, peers, stride=2 * slots), :]
    for j in range(ntail):
        tail = None
        for q in range(min(per, slots - j * per)):
            x = stg[pl.ds(2 * (j * per + q) + 1, peers, stride=2 * slots), :]
            x = pltpu.roll(x, q * rest, axis=1) if q else x
            tail = x if tail is None else tail + x
        if j == 0 and extra is not None:
            tail = tail + extra
        out[pl.ds(slots + j, peers, stride=blk), :] = tail


def errors_kernel(
    arr, recv, bnd_hbm, labk_hbm, t_hbm, e_hbm, out, stg, base2, v2, stgb, labk, kr, bnd, sems, sr, esem, *ksr,
    classes, per, n,
):
    rest = classes - L
    peers, blk, _ = arr.shape
    slots = recv.shape[2]
    ntail = up(slots, per)
    tlane = lanes(ntail)
    load = pltpu.make_async_copy(labk_hbm, labk, sems.at[0])
    load.start()
    bcopy = pltpu.make_async_copy(bnd_hbm.at[0], bnd, sems.at[1])
    bcopy.start()
    kr[:, 0:slots] = recv[0] * 2
    copies = fetch(kr, range(peers), ksr, sr)

    def unpack(p, _):
        at = p * 2 * slots
        tail = arr[p, slots : slots + ntail, :]
        for q in range(per):
            x = pltpu.roll(tail, (L - q * rest) % L, axis=1) if q else tail
            x = jnp.where(tlane < rest, x, 0.0)
            stg[pl.ds(at + 2 * q + 1, ntail, stride=2 * per), :] = x
        stg[pl.ds(at, slots, stride=2), :] = arr[p, 0:slots, :]
        return 0

    lax.fori_loop(0, peers, unpack, 0)

    for c in copies:
        c.wait()
    unroll = 2

    def spread(t, _):
        for v in range(unroll):
            k = t * unroll + v
            for p in range(peers):
                at = pl.ds(pl.multiple_of(ksr[p][0, k], 2), 2)
                base2[at, :] = pair(stg, p * slots + k)[...]
        return 0

    lax.fori_loop(0, slots // unroll, spread, 0)
    load.wait()

    chunk = 128
    lane = lanes(chunk)

    def error(i, _):
        row = pl.multiple_of(i * chunk, chunk)
        lab = labk[pl.ds(row, chunk), :]
        known = lab >= 0.0
        for h in range(2):
            rows = pl.ds(2 * row + h, chunk, stride=2)
            onehot = jnp.where(lab == (lane + h * L).astype(F32), 1.0, 0.0)
            b = base2[rows, :]
            v2[rows, :] = jnp.where(known, onehot - b, 0.0)
            t = jnp.where(known, onehot, b)
            base2[rows, :] = jnp.where(lane == L - 1, jnp.where(known, 0.0, 1.0), t) if h else t
        piece(i, 0).start()
        piece(i, 1).start()
        return 0

    def piece(i, w):
        rows = pl.ds(pl.multiple_of(2 * i * chunk, 2 * chunk), 2 * chunk)
        a, b = ((v2, e_hbm), (base2, t_hbm))[w]
        return pltpu.make_async_copy(a.at[rows, :], b.at[rows, :], esem.at[w, i])

    v2[pl.ds(2 * n, 16), :] = jnp.zeros((16, L), F32)
    lax.fori_loop(0, n // chunk, error, 0)
    pack((bcopy, bnd), v2, stgb, out, None, peers=peers, slots=bnd.shape[1], per=per, rest=rest)
    for i in range(n // chunk):
        piece(i, 0).wait()
        piece(i, 1).wait()


def tiles_kernel(tiles, cols, labels, mask, nh_hbm, nl_hbm, fh, fl, lab_hbm, cnt, nh, nl, labk, sems):
    blocks = labels.shape[0]
    halo = fh.shape[1] // L

    def body(b, _):
        rows = pl.ds(pl.multiple_of(b * L, L), L)
        for j in range(LOC_ROW):
            hi, lo = split(tiles[b * TILES_ROW + j])
            nh[rows, j * L : (j + 1) * L] = hi
            nl[rows, j * L : (j + 1) * L] = lo
        for q in range(halo):
            acc = jnp.zeros((L, L), F32)
            for j in range(LOC_ROW, TILES_ROW):
                hit = cols[b * TILES_ROW + j] == blocks + q
                acc = acc + jnp.where(hit, tiles[b * TILES_ROW + j], 0.0)
            hi, lo = split(acc)
            fh[rows, q * L : (q + 1) * L] = hi
            fl[rows, q * L : (q + 1) * L] = lo
        lab = jnp.where(mask[pl.ds(b, 1), :] > 0, labels[pl.ds(b, 1), :], -1).astype(F32)
        labk[rows, :] = jnp.broadcast_to(lab, (L, L)).T
        return 0

    lax.fori_loop(0, blocks, body, 0)
    pairs = ((nh, nh_hbm), (nl, nl_hbm), (labk, lab_hbm))
    saves = [pltpu.make_async_copy(a, b, sems.at[i]) for i, (a, b) in enumerate(pairs)]
    for c in saves:
        c.start()
    cnt[...] = jnp.zeros(cnt.shape, F32) + jnp.sum(mask[...].astype(F32))
    for c in saves:
        c.wait()


def near_kernel(v_hbm, e_hbm, nh_hbm, nl_hbm, cols, *refs, rate, classes, sums):
    if sums:
        cnt, part, tot, v2, e2, nh, nl, vh, vl, sems = refs
    else:
        part, v2, e2, nh, nl, vh, vl, sems = refs
    pairs = ((v_hbm, v2), (nh_hbm, nh), (nl_hbm, nl), (e_hbm, e2))
    loads = [pltpu.make_async_copy(a, b, sems.at[i]) for i, (a, b) in enumerate(pairs)]
    for c in loads:
        c.start()
    blocks = part.shape[0] // L
    loads[0].wait()

    def halve(b, _):
        rows = pl.ds(pl.multiple_of(b * L, L), L)
        for h in range(2):
            hi, lo = split(v2[pl.ds(b * 2 * L + h, L, stride=2), :])
            vh[rows, h * L : (h + 1) * L] = hi
            vl[rows, h * L : (h + 1) * L] = lo
        return 0

    lax.fori_loop(0, blocks, halve, 0)
    for c in loads[1:]:
        c.wait()

    def body(b, acc):
        rows = pl.ds(pl.multiple_of(b * L, L), L)
        at = [pl.ds(pl.multiple_of(cols[b * TILES_ROW + j] * L, L), L) for j in range(LOC_ROW)]
        bh = jnp.concatenate([vh[a, :] for a in at], 0)
        bl = jnp.concatenate([vl[a, :] for a in at], 0)
        a2 = dot(jnp.concatenate([nh[rows, :], nl[rows, :]], 0), bh)
        near = a2[:L] + a2[L:] + dot(nh[rows, :], bl)
        for h in range(2):
            ev = e2[pl.ds(b * 2 * L + h, L, stride=2), :]
            part[rows, h * L : (h + 1) * L] = (1.0 - rate) * ev + rate * near[:, h * L : (h + 1) * L]
            if sums:
                acc = acc + jnp.sum(jnp.abs(ev).reshape(L // 8, 8, L), 0)
        return acc

    acc = lax.fori_loop(0, blocks, body, jnp.zeros((8, L), F32))
    if sums:
        total = jnp.sum(acc) * (1.0 / classes)
        lane = lanes(8)
        tot[...] = jnp.where(lane == L - 2, total, jnp.where(lane == L - 1, cnt[...], 0.0))


def far_kernel(*refs, rate, classes, per, mode, peers, slots, n):
    rest = classes - L
    refs = list(refs)
    arr, fh, fl, part = refs[:4]
    refs = refs[4:]
    if mode != "last":
        bnd_hbm, bnd, bsem = refs.pop(0), refs.pop(), refs.pop()
        bcopy = pltpu.make_async_copy(bnd_hbm.at[0], bnd, bsem)
        bcopy.start()
    if mode == "sums":
        tot = refs.pop(0)
    if mode == "turn":
        t_hbm, t2, sems = refs.pop(0), refs.pop(), refs.pop()
        half = t2.shape[0] // 2
        loads = [
            pltpu.make_async_copy(t_hbm.at[pl.ds(i * half, half), :], t2.at[pl.ds(i * half, half), :], sems.at[i])
            for i in range(2)
        ]
        for c in loads:
            c.start()
    if mode == "last":
        out, hm, hr = refs
    else:
        v_hbm, out, hm, hr, v2, stgb, vsem = refs
    ntail = up(slots, per)
    blk = slots + ntail
    tlane = lanes(peers)
    for k in range(slots):
        hm[pl.ds(k, peers, stride=slots), :] = arr[pl.ds(k, peers, stride=blk), :]
    for j in range(ntail):
        tail = arr[pl.ds(slots + j, peers, stride=blk), :]
        if j == 0 and mode == "turn":
            sums = jnp.sum(tail, axis=0, keepdims=True)
            sigma = sums[:, L - 2 : L - 1] / sums[:, L - 1 : L]
        for q in range(min(per, slots - j * per)):
            x = pltpu.roll(tail, (L - q * rest) % L, axis=1) if q else tail
            x = jnp.where(tlane < rest, x, 0.0)
            hr[pl.ds(j * per + q, peers, stride=slots), :] = x
    hh, hl = split(jnp.concatenate([hm[...], hr[...]], 1))

    chunk = n // 2
    lane = lanes(chunk)
    count = n // chunk

    def piece(i):
        rows = pl.ds(pl.multiple_of(2 * i * chunk, 2 * chunk), 2 * chunk)
        return pltpu.make_async_copy(v2.at[rows, :], v_hbm.at[rows, :], vsem.at[i])

    if mode != "last":
        v2[pl.ds(2 * n, 16), :] = jnp.zeros((16, L), F32)

    def body(i, _):
        row = pl.multiple_of(i * chunk, chunk)
        rows = pl.ds(row, chunk)
        a2 = dot(jnp.concatenate([fh[rows, :], fl[rows, :]], 0), hh)
        far = a2[:chunk] + a2[chunk:] + dot(fh[rows, :], hl)
        v = part[rows, :] + rate * far
        if mode == "last":
            out[0:L, rows] = v[:, :L].T
            out[L:classes, rows] = v[:, L:].T[:rest]
            return 0
        if mode == "turn":
            mag = jnp.abs(v)
            mag = jnp.sum(mag[:, :L] + mag[:, L:], -1, keepdims=True) * (1.0 / classes) + tiny
            hit = pl.ds(pl.multiple_of(i * half, half), half)
            pltpu.make_async_copy(t_hbm.at[hit, :], t2.at[hit, :], sems.at[i]).wait()
            free = t2[pl.ds(2 * row + 1, chunk, stride=2), :]
            scale = free[:, L - 1 : L] * sigma / mag
        for h in range(2):
            x = v[:, h * L : (h + 1) * L]
            rows2 = pl.ds(2 * row + h, chunk, stride=2)
            if mode == "turn":
                x = t2[rows2, :] + scale * x
                x = jnp.where(lane < rest, x, 0.0) if h else x
            v2[rows2, :] = x
        piece(i).start()
        return 0

    lax.fori_loop(0, count, body, 0)
    if mode != "last":
        extra = tot[0:1, :] if mode == "sums" else None
        pack((bcopy, bnd), v2, stgb, out, extra, peers=peers, slots=slots, per=per, rest=rest)
        for i in range(count):
            piece(i).wait()


def call(kernel, outs, ins, args, scratch=(), vmem=0, flops=0, size=0, name=None, specs=None):
    if specs:
        place = {id(HB): pltpu.HBM, id(VO): pltpu.VMEM}
        outs = tuple(place.get(id(p), jax.ShapeDtypeStruct)(o.shape, o.dtype) for o, p in zip(outs, specs))
    args = [pltpu.with_memory_space_constraint(a, pltpu.HBM) if p is HB else a for a, p in zip(args, ins)]
    return pl.pallas_call(
        kernel,
        out_shape=outs,
        in_specs=ins,
        out_specs=specs or jax.tree.map(lambda _: VM, outs),
        scratch_shapes=list(scratch),
        compiler_params=pltpu.CompilerParams(vmem_limit_bytes=vmem),
        cost_estimate=pl.CostEstimate(flops=flops, bytes_accessed=size, transcendentals=0),
        name=name,
    )(*args)


def swap(x):
    return lax.all_to_all(x, "dom", split_axis=0, concat_axis=0, tiled=True)


def on_device(
    peers, hidden, bases, self_weight, coef, bias, edge_src, edge_dst, edge_rel, send_rows, recv_rows, labels,
    train_mask, bnd_rows, tiles, tile_cols,
):
    n, hdim = hidden.shape
    classes = self_weight.shape[1]
    nrel, nb = coef.shape
    rest = classes - L
    per = (L - 2) // rest
    slots = send_rows.shape[2]
    bnd = bnd_rows.shape[2]
    ne = edge_src.shape[0]
    halo = peers * bnd
    sds = jax.ShapeDtypeStruct
    state = sds((n, 2 * L), F32)
    half = sds((n, 2 * L), BF16)
    blocks = n // L

    dma = lambda k: pltpu.SemaphoreType.DMA((k,))
    blk = up(slots + up(slots, per), 8) * 8
    square = lambda x: x.reshape(-1, L)
    stage = pltpu.VMEM((2 * (peers * slots + 16), L), F32)
    rows2 = pltpu.VMEM((2 * n + 16, L), F32)
    sums = pltpu.VMEM((2 * nrel * n, L), F32)
    wide = (nb + 4) * L
    erows = ne // L
    bnd_rows = 2 * bnd_rows
    sent, _ = call(
        functools.partial(scores_kernel, classes=classes, slots=slots, per=per),
        (sds((peers, blk, L), F32), sds((2 * n, L), F32)),
        [HB, VM, VM, VM, SM, VM, VM, VM, VM],
        (hidden, bases.T, self_weight.T, bias.reshape(1, -1), coef)
        + (square(edge_src), square(edge_dst), square(edge_rel), send_rows),
        [pltpu.VMEM((n, hdim), BF16), pltpu.VMEM((wide, hdim), BF16)]
        + [pltpu.VMEM((n // 2, wide), F32)]
        + [sums] * 5
        + [rows2, stage]
        + [pltpu.VMEM((erows, L), jnp.int32)] * 2
        + [pltpu.VMEM((peers, L), jnp.int32), pltpu.VMEM((2 * n, L), F32), dma(erows), dma(erows), dma(peers)]
        + [dma(2 + 4 * nrel)]
        + [pltpu.SMEM((1, L), jnp.int32)] * (2 * erows + peers),
        vmem=60 * MIB,
        name="scores",
        specs=(VM, HB),
    )
    arrived = swap(sent)
    spread = sds((2 * n, L), F32)
    flat2 = pltpu.VMEM((2 * n, L), F32)
    labv = pltpu.VMEM((n, L), F32)
    halfv = pltpu.VMEM((n, 2 * L), BF16)
    nh, nl, fh, fl, labk, cnt = call(
        tiles_kernel,
        (half, half, sds((n, halo), BF16), sds((n, halo), BF16), sds((n, L), F32), sds((8, L), F32)),
        [VM, SM, VM, VM],
        (tiles, tile_cols, square(labels), square(train_mask)),
        [halfv, halfv, labv, dma(3)],
        vmem=28 * MIB,
        flops=10**7,
        size=8 * 10**6,
        name="tiles",
        specs=(HB, HB, VM, VM, HB, VM),
    )
    lines = peers * (bnd + up(bnd, per))
    packed = sds((lines, L), F32)
    stageb = pltpu.VMEM((2 * halo, L), F32)
    bnds = pltpu.SMEM((peers, bnd), jnp.int32)
    base, v, out = call(
        functools.partial(errors_kernel, classes=classes, per=per, n=n),
        (spread, spread, packed),
        [VM, VM, HB, HB],
        (arrived, recv_rows, bnd_rows, labk),
        [stage, rows2, rows2, stageb, labv, pltpu.VMEM((peers, L), jnp.int32), bnds, dma(2), dma(peers)]
        + [pltpu.SemaphoreType.DMA((2, n // L))]
        + [pltpu.SMEM((1, L), jnp.int32)] * peers,
        vmem=28 * MIB,
        name="errors",
        specs=(HB, HB, VO),
    )
    e = v
    hscr = [pltpu.VMEM((halo, L), F32)] * 2
    for step in range(2 * ITERS):
        rate = correct_rate if step < ITERS else smooth_rate
        halos = swap(out.reshape(peers, 1, -1)).reshape(lines, L)
        sums = step == 0
        mode = "last" if step == 2 * ITERS - 1 else "turn" if step == ITERS - 1 else "sums" if step == ITERS - 2 else "step"
        got = call(
            functools.partial(near_kernel, rate=rate, classes=classes, sums=sums),
            (state, sds((8, L), F32)) if sums else (state,),
            [HB, HB, HB, HB, SM] + [VM] * sums,
            (v, e, nh, nl, tile_cols) + ((cnt,) if sums else ()),
            [flat2, flat2, halfv, halfv, halfv, halfv, dma(4)],
            vmem=24 * MIB,
            flops=10**9,
            size=8 * 10**6,
            name="near",
        )
        part = got[0]
        if sums:
            tot = got[1]
        far = functools.partial(
            far_kernel, rate=rate, classes=classes, per=per, mode=mode, peers=peers, slots=bnd, n=n
        )
        args, ins = (halos, fh, fl, part), [VM] * 4
        if mode == "last":
            return call(far, sds((classes, n), F32), ins, args, hscr, vmem=24 * MIB, name="far_last").T
        args, ins = args + (bnd_rows,), ins + [HB]
        scratch = hscr + [rows2, stageb, dma(n // L)]
        if mode == "sums":
            args, ins = args + (tot,), ins + [VM]
        if mode == "turn":
            args, ins = args + (base,), ins + [HB]
            scratch = scratch + [dma(2), flat2]
        scratch = scratch + [pltpu.SemaphoreType.DMA, bnds]
        v, out = call(
            far, (spread, packed), ins, args, scratch, vmem=24 * MIB, name="far_" + mode, specs=(HB, VO)
        )
        if mode == "turn":
            e = v


def solution(mesh):
    row = P("dom")
    in_specs = (
        P("dom", None), P(), P(), P(), P(), row, row, row, P("dom", None, None), P("dom", None, None), row, row,
        P("dom", None, None), P("dom", None, None), row,
    )
    return jax.shard_map(
        functools.partial(on_device, mesh.shape["dom"]),
        mesh=mesh,
        in_specs=in_specs,
        out_specs=P("dom", None),
        check_vma=False,
    )
```

```python
import functools

import jax
import jax.numpy as jnp
from jax import lax
from jax.experimental import pallas as pl
from jax.experimental.pallas import tpu as pltpu
from jax.sharding import PartitionSpec as P

TILES_ROW = 4
LOC_ROW = 2
ITERS = 3
L = 128

correct_rate = 0.8
smooth_rate = 0.75
tiny = 1e-06

F32 = jnp.float32
BF16 = jnp.bfloat16
VM = pl.BlockSpec(memory_space=pltpu.VMEM)
SM = pl.BlockSpec(memory_space=pltpu.SMEM)
HB = pl.BlockSpec(memory_space=pltpu.HBM)
VO = pl.BlockSpec(memory_space=pltpu.VMEM)
MIB = 1 << 20


def up(a, b):
    return -(-a // b)


def split(x):
    hi = x.astype(BF16)
    return hi, (x - hi.astype(F32)).astype(BF16)


def dot(a, b):
    return jnp.dot(a, b, preferred_element_type=F32)


def lanes(rows):
    return lax.broadcasted_iota(jnp.int32, (rows, L), 1)


def pair(ref, row):
    return ref.at[pl.ds(pl.multiple_of(2 * row, 2), 2), :]


def gather_rows(idx, src, stg, peers, slots):
    copy, idx_ref = idx
    copy.wait()
    group = 4

    def body(g, _):
        for p in range(group):
            for k in range(slots):
                at = pl.ds(pl.multiple_of(idx_ref[g * group + p, k], 2), 2)
                pair(stg, g * (group * slots) + (p * slots + k))[...] = src[at, :]
        return 0

    lax.fori_loop(0, peers // group, body, 0)


def fetch(src, rows, refs, sems):
    copies = [pltpu.make_async_copy(src.at[pl.ds(i, 1), :], r, sems.at[i]) for i, r in zip(rows, refs)]
    for c in copies:
        c.start()
    return copies


def scores_kernel(
    hid_hbm, bt, st, bias, coef, es, ed, er, send, out, blank,
    hid, pt, p0, m2, s0, s1, s2, s3, sc2, stg, kj, kd, kp, zero, sj, sd, sp, sz, *ks, classes, slots, per,
):
    n, hdim = hid.shape
    hload = pltpu.make_async_copy(hid_hbm, hid, sz.at[1 + 4 * coef.shape[0]])
    hload.start()
    rest = classes - L
    nrel, nb = coef.shape
    peers = out.shape[0]
    erows = es.shape[0]
    acc = (s0, s1, s2, s3)
    ksj, ksd, ksp = ks[:erows], ks[erows : 2 * erows], ks[2 * erows :]
    kj[...] = (er[...] * n + es[...]) * 2
    kd[...] = (er[...] * n + ed[...]) * 2
    kp[:, 0:slots] = send[0] * 2
    copies = fetch(kj, range(erows), ksj, sj) + fetch(kd, range(erows), ksd, sd) + fetch(kp, range(peers), ksp, sp)
    zero[...] = jnp.zeros_like(zero)
    wipe = pltpu.make_async_copy(zero, blank, sz.at[0])
    wipe.start()

    base_r = nb * L
    base_s = base_r + 2 * L
    gap = 2 * L // nb
    step = 2 * L

    def arrange(i, _):
        cols = pl.ds(pl.multiple_of(i * step, step), step)
        for b in range(nb):
            x = bt[b * classes : (b + 1) * classes, cols].astype(F32)
            pt[b * L : (b + 1) * L, cols] = x[:L].astype(BF16)
            tail = jnp.concatenate([x[L:], jnp.zeros((gap - rest, step), F32)], 0)
            pt[base_r + b * gap : base_r + (b + 1) * gap, cols] = tail.astype(BF16)
        x = st[:, cols].astype(F32)
        pt[base_s : base_s + L, cols] = x[:L].astype(BF16)
        tail = jnp.concatenate([x[L:], jnp.zeros((L - rest, step), F32)], 0)
        pt[base_s + L : base_s + 2 * L, cols] = tail.astype(BF16)
        return 0

    lax.fori_loop(0, hdim // step, arrange, 0)
    wipe.wait()
    zrows = blank.shape[0]
    for c, s in enumerate(acc[:3]):
        for i in range(nrel):
            copies.append(pltpu.make_async_copy(blank, s.at[pl.ds(i * zrows, zrows), :], sz.at[1 + c * nrel + i]))
            copies[-1].start()

    chunk = p0.shape[0]
    sub = 128
    lane = lanes(sub)
    one = jnp.where(lane == rest, 1.0, 0.0)
    lane8 = lanes(8)
    gains = []
    for r in range(nrel):
        for h in range(2):
            g = jnp.zeros((8, L), F32)
            for b in range(nb // 2):
                g = jnp.where(lane8 // gap == b, coef[r, h * (nb // 2) + b], g)
            gains.append(g[0:1])
    bias0 = bias[0:1, 0:L]
    bias1 = jnp.concatenate([bias[0:1, L:classes], jnp.zeros((1, L - rest), F32)], 1)

    def project(i, _):
        row0 = pl.multiple_of(i * chunk, chunk)
        h = hid[pl.ds(row0, chunk), :]
        for j in range(0, base_s + 2 * L, 2 * L):
            p0[:, j : j + 2 * L] = lax.dot_general(
                h, pt[j : j + 2 * L, :], (((1,), (1,)), ((), ())), preferred_element_type=F32
            )

        def mix(u, _):
            rows = pl.ds(pl.multiple_of(u * sub, sub), sub)
            row = row0 + u * sub
            mains = [p0[rows, b * L : (b + 1) * L] for b in range(nb)]
            q = [p0[rows, base_r + h * L : base_r + (h + 1) * L] for h in range(2)]
            for r in range(nrel):
                x = coef[r, 0] * mains[0]
                for b in range(1, nb):
                    x = x + coef[r, b] * mains[b]
                t = gains[2 * r] * q[0] + gains[2 * r + 1] * q[1]
                turn = L // 2
                while turn >= gap:
                    t = t + pltpu.roll(t, turn, axis=1)
                    turn //= 2
                at = 2 * (r * n + row)
                m2[pl.ds(at, sub, stride=2), :] = x
                m2[pl.ds(at + 1, sub, stride=2), :] = jnp.where(lane < rest, t, one)
            at = 2 * row
            sc2[pl.ds(at, sub, stride=2), :] = p0[rows, base_s : base_s + L] + bias0
            sc2[pl.ds(at + 1, sub, stride=2), :] = p0[rows, base_s + L : base_s + 2 * L] + bias1
            return 0

        lax.fori_loop(0, chunk // sub, mix, 0)
        return 0

    sc2[pl.ds(2 * n, 16), :] = jnp.zeros((16, L), F32)
    hload.wait()
    lax.fori_loop(0, n // chunk, project, 0)

    def clear(i, _):
        s3[pl.ds(pl.multiple_of(i * 512, 512), 512), :] = jnp.zeros((512, L), F32)
        return 0

    lax.fori_loop(0, s3.shape[0] // 512, clear, 0)
    for c in copies:
        c.wait()

    def edges(t, _):
        for v in range(2):
            for e in range(erows):
                s = acc[e % 4]
                j = ksj[e][0, 2 * t + v]
                d = ksd[e][0, 2 * t + v]
                src = m2[pl.ds(pl.multiple_of(j, 2), 2), :]
                at = pl.ds(pl.multiple_of(d, 2), 2)
                s[at, :] = s[at, :] + src
        return 0

    lax.fori_loop(0, L // 2, edges, 0)

    fin = 128
    flane = lanes(fin)

    def finish(i, _):
        row = i * fin
        a0 = sc2[pl.ds(2 * row, fin, stride=2), :]
        a1 = sc2[pl.ds(2 * row + 1, fin, stride=2), :]
        for r in range(nrel):
            rows = [pl.ds(2 * (r * n + row) + h, fin, stride=2) for h in range(2)]
            m, t = [(s0[w, :] + s1[w, :]) + (s2[w, :] + s3[w, :]) for w in rows]
            inv = 1.0 / jnp.maximum(t[:, rest : rest + 1], 1.0)
            a0 = a0 + m * inv
            a1 = a1 + t * inv
        sc2[pl.ds(2 * row, fin, stride=2), :] = a0
        sc2[pl.ds(2 * row + 1, fin, stride=2), :] = jnp.where(flane < rest, a1, 0.0)
        return 0

    lax.fori_loop(0, n // fin, finish, 0)

    def collect(k, _):
        for p in range(peers):
            at = pl.ds(pl.multiple_of(ksp[p][0, k], 2), 2)
            pair(stg, p * slots + k)[...] = sc2[at, :]
        return 0

    lax.fori_loop(0, slots, collect, 0)
    ntail = up(slots, per)

    many = 8

    def put(g, _):
        tails = []
        for v in range(many):
            p = g * many + v
            at = p * 2 * slots
            out[p, 0:slots, :] = stg[pl.ds(at, slots, stride=2), :]
            tails.append([stg[pl.ds(at + 2 * q + 1, ntail, stride=2 * per), :] for q in range(per)])
        tails = [[pltpu.roll(x, q * rest, axis=1) if q else x for q, x in enumerate(t)] for t in tails]
        for v, t in enumerate(tails):
            out[g * many + v, slots : slots + ntail, :] = sum(t[1:], t[0])
        return 0

    lax.fori_loop(0, peers // many, put, 0)


def pack(bnd, v2, stg, out, extra, *, peers, slots, per, rest):
    gather_rows(bnd, v2, stg, peers, slots)
    ntail = up(slots, per)
    blk = slots + ntail
    for k in range(slots):
        out[pl.ds(k, peers, stride=blk), :] = stg[pl.ds(2 * k, peers, stride=2 * slots), :]
    for j in range(ntail):
        tail = None
        for q in range(min(per, slots - j * per)):
            x = stg[pl.ds(2 * (j * per + q) + 1, peers, stride=2 * slots), :]
            x = pltpu.roll(x, q * rest, axis=1) if q else x
            tail = x if tail is None else tail + x
        if j == 0 and extra is not None:
            tail = tail + extra
        out[pl.ds(slots + j, peers, stride=blk), :] = tail


def errors_kernel(
    arr, recv, bnd_hbm, labk_hbm, t_hbm, e_hbm, out, stg, base2, v2, stgb, labk, kr, bnd, sems, sr, esem, *ksr,
    classes, per, n,
):
    rest = classes - L
    peers, blk, _ = arr.shape
    slots = recv.shape[2]
    ntail = up(slots, per)
    tlane = lanes(ntail)
    load = pltpu.make_async_copy(labk_hbm, labk, sems.at[0])
    load.start()
    bcopy = pltpu.make_async_copy(bnd_hbm.at[0], bnd, sems.at[1])
    bcopy.start()
    kr[:, 0:slots] = recv[0] * 2
    copies = fetch(kr, range(peers), ksr, sr)

    many = 4

    def unpack(g, _):
        tails = []
        for v in range(many):
            tail = arr[g * many + v, slots : slots + ntail, :]
            tails.append([pltpu.roll(tail, (L - q * rest) % L, axis=1) if q else tail for q in range(per)])
        for v in range(many):
            p = g * many + v
            at = p * 2 * slots
            for q, x in enumerate(tails[v]):
                stg[pl.ds(at + 2 * q + 1, ntail, stride=2 * per), :] = jnp.where(tlane < rest, x, 0.0)
            stg[pl.ds(at, slots, stride=2), :] = arr[p, 0:slots, :]
        return 0

    lax.fori_loop(0, peers // many, unpack, 0)

    for c in copies:
        c.wait()
    unroll = 2

    def spread(t, _):
        for v in range(unroll):
            k = t * unroll + v
            for p in range(peers):
                at = pl.ds(pl.multiple_of(ksr[p][0, k], 2), 2)
                base2[at, :] = pair(stg, p * slots + k)[...]
        return 0

    lax.fori_loop(0, slots // unroll, spread, 0)
    load.wait()

    chunk = 128
    lane = lanes(chunk)

    def error(i, _):
        row = pl.multiple_of(i * chunk, chunk)
        lab = labk[pl.ds(row, chunk), :]
        known = lab >= 0.0
        for h in range(2):
            rows = pl.ds(2 * row + h, chunk, stride=2)
            onehot = jnp.where(lab == (lane + h * L).astype(F32), 1.0, 0.0)
            b = base2[rows, :]
            v2[rows, :] = jnp.where(known, onehot - b, 0.0)
            t = jnp.where(known, onehot, b)
            base2[rows, :] = jnp.where(lane == L - 1, jnp.where(known, 0.0, 1.0), t) if h else t
        piece(i, 0).start()
        piece(i, 1).start()
        return 0

    def piece(i, w):
        rows = pl.ds(pl.multiple_of(2 * i * chunk, 2 * chunk), 2 * chunk)
        a, b = ((v2, e_hbm), (base2, t_hbm))[w]
        return pltpu.make_async_copy(a.at[rows, :], b.at[rows, :], esem.at[w, i])

    v2[pl.ds(2 * n, 16), :] = jnp.zeros((16, L), F32)
    lax.fori_loop(0, n // chunk, error, 0)
    pack((bcopy, bnd), v2, stgb, out, None, peers=peers, slots=bnd.shape[1], per=per, rest=rest)
    for i in range(n // chunk):
        piece(i, 0).wait()
        piece(i, 1).wait()


def tiles_kernel(tiles, cols, labels, mask, nh_hbm, nl_hbm, fh, fl, lab_hbm, cnt, nh, nl, labk, sems):
    blocks = labels.shape[0]
    halo = fh.shape[1] // L

    def body(b, _):
        rows = pl.ds(pl.multiple_of(b * L, L), L)
        for j in range(LOC_ROW):
            hi, lo = split(tiles[b * TILES_ROW + j])
            nh[rows, j * L : (j + 1) * L] = hi
            nl[rows, j * L : (j + 1) * L] = lo
        for q in range(halo):
            acc = jnp.zeros((L, L), F32)
            for j in range(LOC_ROW, TILES_ROW):
                hit = cols[b * TILES_ROW + j] == blocks + q
                acc = acc + jnp.where(hit, tiles[b * TILES_ROW + j], 0.0)
            hi, lo = split(acc)
            fh[rows, q * L : (q + 1) * L] = hi
            fl[rows, q * L : (q + 1) * L] = lo
        lab = jnp.where(mask[pl.ds(b, 1), :] > 0, labels[pl.ds(b, 1), :], -1).astype(F32)
        labk[rows, :] = jnp.broadcast_to(lab, (L, L)).T
        return 0

    lax.fori_loop(0, blocks, body, 0)
    pairs = ((nh, nh_hbm), (nl, nl_hbm), (labk, lab_hbm))
    saves = [pltpu.make_async_copy(a, b, sems.at[i]) for i, (a, b) in enumerate(pairs)]
    for c in saves:
        c.start()
    cnt[...] = jnp.zeros(cnt.shape, F32) + jnp.sum(mask[...].astype(F32))
    for c in saves:
        c.wait()


def near_kernel(v_hbm, e_hbm, nh_hbm, nl_hbm, cols, *refs, rate, classes, sums):
    if sums:
        cnt, part, tot, v2, e2, nh, nl, vh, vl, sems = refs
    else:
        part, v2, e2, nh, nl, vh, vl, sems = refs
    pairs = ((v_hbm, v2), (nh_hbm, nh), (nl_hbm, nl), (e_hbm, e2))
    loads = [pltpu.make_async_copy(a, b, sems.at[i]) for i, (a, b) in enumerate(pairs)]
    for c in loads:
        c.start()
    blocks = part.shape[0] // L
    loads[0].wait()

    def halve(b, _):
        rows = pl.ds(pl.multiple_of(b * L, L), L)
        for h in range(2):
            hi, lo = split(v2[pl.ds(b * 2 * L + h, L, stride=2), :])
            vh[rows, h * L : (h + 1) * L] = hi
            vl[rows, h * L : (h + 1) * L] = lo
        return 0

    lax.fori_loop(0, blocks, halve, 0)
    for c in loads[1:]:
        c.wait()

    def body(b, acc):
        rows = pl.ds(pl.multiple_of(b * L, L), L)
        at = [pl.ds(pl.multiple_of(cols[b * TILES_ROW + j] * L, L), L) for j in range(LOC_ROW)]
        bh = jnp.concatenate([vh[a, :] for a in at], 0)
        bl = jnp.concatenate([vl[a, :] for a in at], 0)
        a2 = dot(jnp.concatenate([nh[rows, :], nl[rows, :]], 0), bh)
        near = a2[:L] + a2[L:] + dot(nh[rows, :], bl)
        for h in range(2):
            ev = e2[pl.ds(b * 2 * L + h, L, stride=2), :]
            part[rows, h * L : (h + 1) * L] = (1.0 - rate) * ev + rate * near[:, h * L : (h + 1) * L]
            if sums:
                acc = acc + jnp.sum(jnp.abs(ev).reshape(L // 8, 8, L), 0)
        return acc

    acc = lax.fori_loop(0, blocks, body, jnp.zeros((8, L), F32))
    if sums:
        total = jnp.sum(acc) * (1.0 / classes)
        lane = lanes(8)
        tot[...] = jnp.where(lane == L - 2, total, jnp.where(lane == L - 1, cnt[...], 0.0))


def far_kernel(*refs, rate, classes, per, mode, peers, slots, n):
    rest = classes - L
    refs = list(refs)
    arr, fh, fl, part = refs[:4]
    refs = refs[4:]
    if mode != "last":
        bnd_hbm, bnd, bsem = refs.pop(0), refs.pop(), refs.pop()
        bcopy = pltpu.make_async_copy(bnd_hbm.at[0], bnd, bsem)
        bcopy.start()
    if mode == "sums":
        tot = refs.pop(0)
    if mode == "turn":
        t_hbm, t2, sems = refs.pop(0), refs.pop(), refs.pop()
        half = t2.shape[0] // 2
        loads = [
            pltpu.make_async_copy(t_hbm.at[pl.ds(i * half, half), :], t2.at[pl.ds(i * half, half), :], sems.at[i])
            for i in range(2)
        ]
        for c in loads:
            c.start()
    if mode == "last":
        out, hm, hr = refs
    else:
        v_hbm, out, hm, hr, v2, stgb, vsem = refs
    ntail = up(slots, per)
    blk = slots + ntail
    tlane = lanes(peers)
    for k in range(slots):
        hm[pl.ds(k, peers, stride=slots), :] = arr[pl.ds(k, peers, stride=blk), :]
    for j in range(ntail):
        tail = arr[pl.ds(slots + j, peers, stride=blk), :]
        if j == 0 and mode == "turn":
            sums = jnp.sum(tail, axis=0, keepdims=True)
            sigma = sums[:, L - 2 : L - 1] / sums[:, L - 1 : L]
        for q in range(min(per, slots - j * per)):
            x = pltpu.roll(tail, (L - q * rest) % L, axis=1) if q else tail
            x = jnp.where(tlane < rest, x, 0.0)
            hr[pl.ds(j * per + q, peers, stride=slots), :] = x
    hh, hl = split(jnp.concatenate([hm[...], hr[...]], 1))

    chunk = n // 2
    lane = lanes(chunk)
    count = n // chunk

    def piece(i):
        rows = pl.ds(pl.multiple_of(2 * i * chunk, 2 * chunk), 2 * chunk)
        return pltpu.make_async_copy(v2.at[rows, :], v_hbm.at[rows, :], vsem.at[i])

    if mode != "last":
        v2[pl.ds(2 * n, 16), :] = jnp.zeros((16, L), F32)

    def body(i, _):
        row = pl.multiple_of(i * chunk, chunk)
        rows = pl.ds(row, chunk)
        a2 = dot(jnp.concatenate([fh[rows, :], fl[rows, :]], 0), hh)
        far = a2[:chunk] + a2[chunk:] + dot(fh[rows, :], hl)
        v = part[rows, :] + rate * far
        if mode == "last":
            out[0:L, rows] = v[:, :L].T
            out[L:classes, rows] = v[:, L:].T[:rest]
            return 0
        if mode == "turn":
            mag = jnp.abs(v)
            mag = jnp.sum(mag[:, :L] + mag[:, L:], -1, keepdims=True) * (1.0 / classes) + tiny
            hit = pl.ds(pl.multiple_of(i * half, half), half)
            pltpu.make_async_copy(t_hbm.at[hit, :], t2.at[hit, :], sems.at[i]).wait()
            free = t2[pl.ds(2 * row + 1, chunk, stride=2), :]
            scale = free[:, L - 1 : L] * sigma / mag
        for h in range(2):
            x = v[:, h * L : (h + 1) * L]
            rows2 = pl.ds(2 * row + h, chunk, stride=2)
            if mode == "turn":
                x = t2[rows2, :] + scale * x
                x = jnp.where(lane < rest, x, 0.0) if h else x
            v2[rows2, :] = x
        piece(i).start()
        return 0

    lax.fori_loop(0, count, body, 0)
    if mode != "last":
        extra = tot[0:1, :] if mode == "sums" else None
        pack((bcopy, bnd), v2, stgb, out, extra, peers=peers, slots=slots, per=per, rest=rest)
        for i in range(count):
            piece(i).wait()


def call(kernel, outs, ins, args, scratch=(), vmem=0, flops=0, size=0, name=None, specs=None):
    if specs:
        place = {id(HB): pltpu.HBM, id(VO): pltpu.VMEM}
        outs = tuple(place.get(id(p), jax.ShapeDtypeStruct)(o.shape, o.dtype) for o, p in zip(outs, specs))
    args = [pltpu.with_memory_space_constraint(a, pltpu.HBM) if p is HB else a for a, p in zip(args, ins)]
    return pl.pallas_call(
        kernel,
        out_shape=outs,
        in_specs=ins,
        out_specs=specs or jax.tree.map(lambda _: VM, outs),
        scratch_shapes=list(scratch),
        compiler_params=pltpu.CompilerParams(vmem_limit_bytes=vmem),
        cost_estimate=pl.CostEstimate(flops=flops, bytes_accessed=size, transcendentals=0),
        name=name,
    )(*args)


def swap(x):
    return lax.all_to_all(x, "dom", split_axis=0, concat_axis=0, tiled=True)


def on_device(
    peers, hidden, bases, self_weight, coef, bias, edge_src, edge_dst, edge_rel, send_rows, recv_rows, labels,
    train_mask, bnd_rows, tiles, tile_cols,
):
    n, hdim = hidden.shape
    classes = self_weight.shape[1]
    nrel, nb = coef.shape
    rest = classes - L
    per = (L - 2) // rest
    slots = send_rows.shape[2]
    bnd = bnd_rows.shape[2]
    ne = edge_src.shape[0]
    halo = peers * bnd
    sds = jax.ShapeDtypeStruct
    state = sds((n, 2 * L), F32)
    half = sds((n, 2 * L), BF16)
    blocks = n // L

    dma = lambda k: pltpu.SemaphoreType.DMA((k,))
    blk = up(slots + up(slots, per), 8) * 8
    square = lambda x: x.reshape(-1, L)
    stage = pltpu.VMEM((2 * (peers * slots + 16), L), F32)
    rows2 = pltpu.VMEM((2 * n + 16, L), F32)
    sums = pltpu.VMEM((2 * nrel * n, L), F32)
    wide = (nb + 4) * L
    erows = ne // L
    bnd_rows = 2 * bnd_rows
    sent, _ = call(
        functools.partial(scores_kernel, classes=classes, slots=slots, per=per),
        (sds((peers, blk, L), F32), sds((2 * n, L), F32)),
        [HB, VM, VM, VM, SM, VM, VM, VM, VM],
        (hidden, bases.T, self_weight.T, bias.reshape(1, -1), coef)
        + (square(edge_src), square(edge_dst), square(edge_rel), send_rows),
        [pltpu.VMEM((n, hdim), BF16), pltpu.VMEM((wide, hdim), BF16)]
        + [pltpu.VMEM((n // 2, wide), F32)]
        + [sums] * 5
        + [rows2, stage]
        + [pltpu.VMEM((erows, L), jnp.int32)] * 2
        + [pltpu.VMEM((peers, L), jnp.int32), pltpu.VMEM((2 * n, L), F32), dma(erows), dma(erows), dma(peers)]
        + [dma(2 + 4 * nrel)]
        + [pltpu.SMEM((1, L), jnp.int32)] * (2 * erows + peers),
        vmem=60 * MIB,
        name="scores",
        specs=(VM, HB),
    )
    arrived = swap(sent)
    spread = sds((2 * n, L), F32)
    flat2 = pltpu.VMEM((2 * n, L), F32)
    labv = pltpu.VMEM((n, L), F32)
    halfv = pltpu.VMEM((n, 2 * L), BF16)
    nh, nl, fh, fl, labk, cnt = call(
        tiles_kernel,
        (half, half, sds((n, halo), BF16), sds((n, halo), BF16), sds((n, L), F32), sds((8, L), F32)),
        [VM, SM, VM, VM],
        (tiles, tile_cols, square(labels), square(train_mask)),
        [halfv, halfv, labv, dma(3)],
        vmem=28 * MIB,
        flops=10**7,
        size=8 * 10**6,
        name="tiles",
        specs=(HB, HB, VM, VM, HB, VM),
    )
    lines = peers * (bnd + up(bnd, per))
    packed = sds((lines, L), F32)
    stageb = pltpu.VMEM((2 * halo, L), F32)
    bnds = pltpu.SMEM((peers, bnd), jnp.int32)
    base, v, out = call(
        functools.partial(errors_kernel, classes=classes, per=per, n=n),
        (spread, spread, packed),
        [VM, VM, HB, HB],
        (arrived, recv_rows, bnd_rows, labk),
        [stage, rows2, rows2, stageb, labv, pltpu.VMEM((peers, L), jnp.int32), bnds, dma(2), dma(peers)]
        + [pltpu.SemaphoreType.DMA((2, n // L))]
        + [pltpu.SMEM((1, L), jnp.int32)] * peers,
        vmem=28 * MIB,
        name="errors",
        specs=(HB, HB, VO),
    )
    e = v
    hscr = [pltpu.VMEM((halo, L), F32)] * 2
    for step in range(2 * ITERS):
        rate = correct_rate if step < ITERS else smooth_rate
        halos = swap(out.reshape(peers, 1, -1)).reshape(lines, L)
        sums = step == 0
        mode = "last" if step == 2 * ITERS - 1 else "turn" if step == ITERS - 1 else "sums" if step == ITERS - 2 else "step"
        got = call(
            functools.partial(near_kernel, rate=rate, classes=classes, sums=sums),
            (state, sds((8, L), F32)) if sums else (state,),
            [HB, HB, HB, HB, SM] + [VM] * sums,
            (v, e, nh, nl, tile_cols) + ((cnt,) if sums else ()),
            [flat2, flat2, halfv, halfv, halfv, halfv, dma(4)],
            vmem=24 * MIB,
            flops=10**9,
            size=8 * 10**6,
            name="near",
        )
        part = got[0]
        if sums:
            tot = got[1]
        far = functools.partial(
            far_kernel, rate=rate, classes=classes, per=per, mode=mode, peers=peers, slots=bnd, n=n
        )
        args, ins = (halos, fh, fl, part), [VM] * 4
        if mode == "last":
            return call(far, sds((classes, n), F32), ins, args, hscr, vmem=24 * MIB, name="far_last").T
        args, ins = args + (bnd_rows,), ins + [HB]
        scratch = hscr + [rows2, stageb, dma(n // L)]
        if mode == "sums":
            args, ins = args + (tot,), ins + [VM]
        if mode == "turn":
            args, ins = args + (base,), ins + [HB]
            scratch = scratch + [dma(2), flat2]
        scratch = scratch + [pltpu.SemaphoreType.DMA, bnds]
        v, out = call(
            far, (spread, packed), ins, args, scratch, vmem=24 * MIB, name="far_" + mode, specs=(HB, VO)
        )
        if mode == "turn":
            e = v


def solution(mesh):
    row = P("dom")
    in_specs = (
        P("dom", None), P(), P(), P(), P(), row, row, row, P("dom", None, None), P("dom", None, None), row, row,
        P("dom", None, None), P("dom", None, None), row,
    )
    return jax.shard_map(
        functools.partial(on_device, mesh.shape["dom"]),
        mesh=mesh,
        in_specs=in_specs,
        out_specs=P("dom", None),
        check_vma=False,
    )
```

```python
import functools

import jax
import jax.numpy as jnp
from jax import lax
from jax.experimental import pallas as pl
from jax.experimental.pallas import tpu as pltpu
from jax.sharding import PartitionSpec as P

TILES_ROW = 4
LOC_ROW = 2
ITERS = 3
L = 128

correct_rate = 0.8
smooth_rate = 0.75
tiny = 1e-06

F32 = jnp.float32
BF16 = jnp.bfloat16
VM = pl.BlockSpec(memory_space=pltpu.VMEM)
SM = pl.BlockSpec(memory_space=pltpu.SMEM)
HB = pl.BlockSpec(memory_space=pltpu.HBM)
VO = pl.BlockSpec(memory_space=pltpu.VMEM)
MIB = 1 << 20


def up(a, b):
    return -(-a // b)


def split(x):
    hi = x.astype(BF16)
    return hi, (x - hi.astype(F32)).astype(BF16)


def dot(a, b):
    return jnp.dot(a, b, preferred_element_type=F32)


def lanes(rows):
    return lax.broadcasted_iota(jnp.int32, (rows, L), 1)


def pair(ref, row):
    return ref.at[pl.ds(pl.multiple_of(2 * row, 2), 2), :]


def gather_rows(idx, src, stg, peers, slots):
    copy, idx_ref = idx
    copy.wait()
    group = 4

    def body(g, _):
        for p in range(group):
            for k in range(slots):
                at = pl.ds(pl.multiple_of(idx_ref[g * group + p, k], 2), 2)
                pair(stg, g * (group * slots) + (p * slots + k))[...] = src[at, :]
        return 0

    lax.fori_loop(0, peers // group, body, 0)


def fetch(src, rows, refs, sems):
    copies = [pltpu.make_async_copy(src.at[pl.ds(i, 1), :], r, sems.at[i]) for i, r in zip(rows, refs)]
    for c in copies:
        c.start()
    return copies


def scores_kernel(
    hid_hbm, bt, st, bias, coef, es, ed, er, send, out, blank,
    hid, pt, p0, p1, m2, s0, s1, s2, s3, sc2, stg, kj, kd, kp, zero, sj, sd, sp, sz, *ks, classes, slots, per,
):
    n, hdim = hid.shape
    hload = pltpu.make_async_copy(hid_hbm, hid, sz.at[1 + 4 * coef.shape[0]])
    hload.start()
    rest = classes - L
    nrel, nb = coef.shape
    peers = out.shape[0]
    erows = es.shape[0]
    acc = (s0, s1, s2, s3)
    ksj, ksd, ksp = ks[:erows], ks[erows : 2 * erows], ks[2 * erows :]
    kj[...] = (er[...] * n + es[...]) * 2
    kd[...] = (er[...] * n + ed[...]) * 2
    kp[:, 0:slots] = send[0] * 2
    copies = fetch(kj, range(erows), ksj, sj) + fetch(kd, range(erows), ksd, sd) + fetch(kp, range(peers), ksp, sp)
    zero[...] = jnp.zeros_like(zero)
    wipe = pltpu.make_async_copy(zero, blank, sz.at[0])
    wipe.start()

    base_r = nb * L
    base_s = base_r + 2 * L
    gap = 2 * L // nb
    step = 2 * L

    def arrange(i, _):
        cols = pl.ds(pl.multiple_of(i * step, step), step)
        for b in range(nb):
            x = bt[b * classes : (b + 1) * classes, cols].astype(F32)
            pt[b * L : (b + 1) * L, cols] = x[:L].astype(BF16)
            tail = jnp.concatenate([x[L:], jnp.zeros((gap - rest, step), F32)], 0)
            pt[base_r + b * gap : base_r + (b + 1) * gap, cols] = tail.astype(BF16)
        x = st[:, cols].astype(F32)
        pt[base_s : base_s + L, cols] = x[:L].astype(BF16)
        tail = jnp.concatenate([x[L:], jnp.zeros((L - rest, step), F32)], 0)
        pt[base_s + L : base_s + 2 * L, cols] = tail.astype(BF16)
        return 0

    lax.fori_loop(0, hdim // step, arrange, 0)
    wipe.wait()
    zrows = blank.shape[0]
    for c, s in enumerate(acc[:3]):
        for i in range(nrel):
            copies.append(pltpu.make_async_copy(blank, s.at[pl.ds(i * zrows, zrows), :], sz.at[1 + c * nrel + i]))
            copies[-1].start()

    chunk = p0.shape[0]
    sub = 128
    lane = lanes(sub)
    one = jnp.where(lane == rest, 1.0, 0.0)
    lane8 = lanes(8)
    gains = []
    for r in range(nrel):
        for h in range(2):
            g = jnp.zeros((8, L), F32)
            for b in range(nb // 2):
                g = jnp.where(lane8 // gap == b, coef[r, h * (nb // 2) + b], g)
            gains.append(g[0:1])
    bias0 = bias[0:1, 0:L]
    bias1 = jnp.concatenate([bias[0:1, L:classes], jnp.zeros((1, L - rest), F32)], 1)

    def project(i, dst):
        h = hid[pl.ds(pl.multiple_of(i * chunk, chunk), chunk), :]
        for j in range(0, base_s + 2 * L, 2 * L):
            dst[:, j : j + 2 * L] = lax.dot_general(
                h, pt[j : j + 2 * L, :], (((1,), (1,)), ((), ())), preferred_element_type=F32
            )
            yield

    def mix(i, src):
        for u in range(0, chunk, sub):
            rows = slice(u, u + sub)
            row = i * chunk + u
            mains = [src[rows, b * L : (b + 1) * L] for b in range(nb)]
            q = [src[rows, base_r + h * L : base_r + (h + 1) * L] for h in range(2)]
            for r in range(nrel):
                x = coef[r, 0] * mains[0]
                for b in range(1, nb):
                    x = x + coef[r, b] * mains[b]
                t = gains[2 * r] * q[0] + gains[2 * r + 1] * q[1]
                turn = L // 2
                while turn >= gap:
                    t = t + pltpu.roll(t, turn, axis=1)
                    turn //= 2
                at = 2 * (r * n + row)
                m2[pl.ds(at, sub, stride=2), :] = x
                m2[pl.ds(at + 1, sub, stride=2), :] = jnp.where(lane < rest, t, one)
                yield
            at = 2 * row
            sc2[pl.ds(at, sub, stride=2), :] = src[rows, base_s : base_s + L] + bias0
            sc2[pl.ds(at + 1, sub, stride=2), :] = src[rows, base_s + L : base_s + 2 * L] + bias1

    def weave(*works):
        works = list(works)
        while works:
            for w in list(works):
                if next(w, 0) == 0:
                    works.remove(w)

    sc2[pl.ds(2 * n, 16), :] = jnp.zeros((16, L), F32)
    count = n // chunk
    hload.wait()
    weave(project(0, p0))

    def pipe(t, _):
        weave(mix(2 * t, p0), project(2 * t + 1, p1))
        weave(mix(2 * t + 1, p1), project(2 * t + 2, p0))
        return 0

    lax.fori_loop(0, count // 2 - 1, pipe, 0)
    weave(mix(count - 2, p0), project(count - 1, p1))
    weave(mix(count - 1, p1))

    def clear(i, _):
        s3[pl.ds(pl.multiple_of(i * 512, 512), 512), :] = jnp.zeros((512, L), F32)
        return 0

    lax.fori_loop(0, s3.shape[0] // 512, clear, 0)
    for c in copies:
        c.wait()

    def edges(t, _):
        for v in range(2):
            for e in range(erows):
                s = acc[e % 4]
                j = ksj[e][0, 2 * t + v]
                d = ksd[e][0, 2 * t + v]
                src = m2[pl.ds(pl.multiple_of(j, 2), 2), :]
                at = pl.ds(pl.multiple_of(d, 2), 2)
                s[at, :] = s[at, :] + src
        return 0

    lax.fori_loop(0, L // 2, edges, 0)

    fin = 128
    flane = lanes(fin)

    def finish(i, _):
        row = i * fin
        a0 = sc2[pl.ds(2 * row, fin, stride=2), :]
        a1 = sc2[pl.ds(2 * row + 1, fin, stride=2), :]
        for r in range(nrel):
            rows = [pl.ds(2 * (r * n + row) + h, fin, stride=2) for h in range(2)]
            m, t = [(s0[w, :] + s1[w, :]) + (s2[w, :] + s3[w, :]) for w in rows]
            inv = 1.0 / jnp.maximum(t[:, rest : rest + 1], 1.0)
            a0 = a0 + m * inv
            a1 = a1 + t * inv
        sc2[pl.ds(2 * row, fin, stride=2), :] = a0
        sc2[pl.ds(2 * row + 1, fin, stride=2), :] = jnp.where(flane < rest, a1, 0.0)
        return 0

    lax.fori_loop(0, n // fin, finish, 0)

    def collect(k, _):
        for p in range(peers):
            at = pl.ds(pl.multiple_of(ksp[p][0, k], 2), 2)
            pair(stg, p * slots + k)[...] = sc2[at, :]
        return 0

    lax.fori_loop(0, slots, collect, 0)
    ntail = up(slots, per)

    many = 8

    def put(g, _):
        tails = []
        for v in range(many):
            p = g * many + v
            at = p * 2 * slots
            out[p, 0:slots, :] = stg[pl.ds(at, slots, stride=2), :]
            tails.append([stg[pl.ds(at + 2 * q + 1, ntail, stride=2 * per), :] for q in range(per)])
        tails = [[pltpu.roll(x, q * rest, axis=1) if q else x for q, x in enumerate(t)] for t in tails]
        for v, t in enumerate(tails):
            out[g * many + v, slots : slots + ntail, :] = sum(t[1:], t[0])
        return 0

    lax.fori_loop(0, peers // many, put, 0)


def pack(bnd, v2, stg, out, extra, *, peers, slots, per, rest):
    gather_rows(bnd, v2, stg, peers, slots)
    ntail = up(slots, per)
    blk = slots + ntail
    for k in range(slots):
        out[pl.ds(k, peers, stride=blk), :] = stg[pl.ds(2 * k, peers, stride=2 * slots), :]
    for j in range(ntail):
        tail = None
        for q in range(min(per, slots - j * per)):
            x = stg[pl.ds(2 * (j * per + q) + 1, peers, stride=2 * slots), :]
            x = pltpu.roll(x, q * rest, axis=1) if q else x
            tail = x if tail is None else tail + x
        if j == 0 and extra is not None:
            tail = tail + extra
        out[pl.ds(slots + j, peers, stride=blk), :] = tail


def errors_kernel(
    arr, recv, bnd_hbm, labk_hbm, t_hbm, e_hbm, out, stg, base2, v2, stgb, labk, kr, bnd, sems, sr, esem, *ksr,
    classes, per, n,
):
    rest = classes - L
    peers, blk, _ = arr.shape
    slots = recv.shape[2]
    ntail = up(slots, per)
    tlane = lanes(ntail)
    load = pltpu.make_async_copy(labk_hbm, labk, sems.at[0])
    load.start()
    bcopy = pltpu.make_async_copy(bnd_hbm.at[0], bnd, sems.at[1])
    bcopy.start()
    kr[:, 0:slots] = recv[0] * 2
    copies = fetch(kr, range(peers), ksr, sr)

    many = 4

    def unpack(g, _):
        tails = []
        for v in range(many):
            tail = arr[g * many + v, slots : slots + ntail, :]
            tails.append([pltpu.roll(tail, (L - q * rest) % L, axis=1) if q else tail for q in range(per)])
        for v in range(many):
            p = g * many + v
            at = p * 2 * slots
            for q, x in enumerate(tails[v]):
                stg[pl.ds(at + 2 * q + 1, ntail, stride=2 * per), :] = jnp.where(tlane < rest, x, 0.0)
            stg[pl.ds(at, slots, stride=2), :] = arr[p, 0:slots, :]
        return 0

    lax.fori_loop(0, peers // many, unpack, 0)

    for c in copies:
        c.wait()
    unroll = 2

    def spread(t, _):
        for v in range(unroll):
            k = t * unroll + v
            for p in range(peers):
                at = pl.ds(pl.multiple_of(ksr[p][0, k], 2), 2)
                base2[at, :] = pair(stg, p * slots + k)[...]
        return 0

    lax.fori_loop(0, slots // unroll, spread, 0)
    load.wait()

    chunk = 128
    lane = lanes(chunk)

    def error(i, _):
        row = pl.multiple_of(i * chunk, chunk)
        lab = labk[pl.ds(row, chunk), :]
        known = lab >= 0.0
        for h in range(2):
            rows = pl.ds(2 * row + h, chunk, stride=2)
            onehot = jnp.where(lab == (lane + h * L).astype(F32), 1.0, 0.0)
            b = base2[rows, :]
            v2[rows, :] = jnp.where(known, onehot - b, 0.0)
            t = jnp.where(known, onehot, b)
            base2[rows, :] = jnp.where(lane == L - 1, jnp.where(known, 0.0, 1.0), t) if h else t
        piece(i, 0).start()
        piece(i, 1).start()
        return 0

    def piece(i, w):
        rows = pl.ds(pl.multiple_of(2 * i * chunk, 2 * chunk), 2 * chunk)
        a, b = ((v2, e_hbm), (base2, t_hbm))[w]
        return pltpu.make_async_copy(a.at[rows, :], b.at[rows, :], esem.at[w, i])

    v2[pl.ds(2 * n, 16), :] = jnp.zeros((16, L), F32)
    lax.fori_loop(0, n // chunk, error, 0)
    pack((bcopy, bnd), v2, stgb, out, None, peers=peers, slots=bnd.shape[1], per=per, rest=rest)
    for i in range(n // chunk):
        piece(i, 0).wait()
        piece(i, 1).wait()


def tiles_kernel(tiles, cols, labels, mask, nh_hbm, nl_hbm, fh, fl, lab_hbm, cnt, nh, nl, labk, sems):
    blocks = labels.shape[0]
    halo = fh.shape[1] // L

    def body(b, _):
        rows = pl.ds(pl.multiple_of(b * L, L), L)
        for j in range(LOC_ROW):
            hi, lo = split(tiles[b * TILES_ROW + j])
            nh[rows, j * L : (j + 1) * L] = hi
            nl[rows, j * L : (j + 1) * L] = lo
        for q in range(halo):
            acc = jnp.zeros((L, L), F32)
            for j in range(LOC_ROW, TILES_ROW):
                hit = cols[b * TILES_ROW + j] == blocks + q
                acc = acc + jnp.where(hit, tiles[b * TILES_ROW + j], 0.0)
            hi, lo = split(acc)
            fh[rows, q * L : (q + 1) * L] = hi
            fl[rows, q * L : (q + 1) * L] = lo
        lab = jnp.where(mask[pl.ds(b, 1), :] > 0, labels[pl.ds(b, 1), :], -1).astype(F32)
        labk[rows, :] = jnp.broadcast_to(lab, (L, L)).T
        return 0

    lax.fori_loop(0, blocks, body, 0)
    pairs = ((nh, nh_hbm), (nl, nl_hbm), (labk, lab_hbm))
    saves = [pltpu.make_async_copy(a, b, sems.at[i]) for i, (a, b) in enumerate(pairs)]
    for c in saves:
        c.start()
    cnt[...] = jnp.zeros(cnt.shape, F32) + jnp.sum(mask[...].astype(F32))
    for c in saves:
        c.wait()


def near_kernel(v_hbm, e_hbm, nh_hbm, nl_hbm, cols, *refs, rate, classes, sums):
    if sums:
        cnt, part, tot, v2, e2, nh, nl, vh, vl, sems = refs
    else:
        part, v2, e2, nh, nl, vh, vl, sems = refs
    pairs = ((v_hbm, v2), (nh_hbm, nh), (nl_hbm, nl), (e_hbm, e2))
    loads = [pltpu.make_async_copy(a, b, sems.at[i]) for i, (a, b) in enumerate(pairs)]
    for c in loads:
        c.start()
    blocks = part.shape[0] // L
    loads[0].wait()

    def halve(b, _):
        rows = pl.ds(pl.multiple_of(b * L, L), L)
        for h in range(2):
            hi, lo = split(v2[pl.ds(b * 2 * L + h, L, stride=2), :])
            vh[rows, h * L : (h + 1) * L] = hi
            vl[rows, h * L : (h + 1) * L] = lo
        return 0

    lax.fori_loop(0, blocks, halve, 0)
    for c in loads[1:]:
        c.wait()

    def body(b, acc):
        rows = pl.ds(pl.multiple_of(b * L, L), L)
        at = [pl.ds(pl.multiple_of(cols[b * TILES_ROW + j] * L, L), L) for j in range(LOC_ROW)]
        bh = jnp.concatenate([vh[a, :] for a in at], 0)
        bl = jnp.concatenate([vl[a, :] for a in at], 0)
        a2 = dot(jnp.concatenate([nh[rows, :], nl[rows, :]], 0), bh)
        near = a2[:L] + a2[L:] + dot(nh[rows, :], bl)
        for h in range(2):
            ev = e2[pl.ds(b * 2 * L + h, L, stride=2), :]
            part[rows, h * L : (h + 1) * L] = (1.0 - rate) * ev + rate * near[:, h * L : (h + 1) * L]
            if sums:
                acc = acc + jnp.sum(jnp.abs(ev).reshape(L // 8, 8, L), 0)
        return acc

    acc = lax.fori_loop(0, blocks, body, jnp.zeros((8, L), F32))
    if sums:
        total = jnp.sum(acc) * (1.0 / classes)
        lane = lanes(8)
        tot[...] = jnp.where(lane == L - 2, total, jnp.where(lane == L - 1, cnt[...], 0.0))


def far_kernel(*refs, rate, classes, per, mode, peers, slots, n):
    rest = classes - L
    refs = list(refs)
    arr, fh, fl, part = refs[:4]
    refs = refs[4:]
    if mode != "last":
        bnd_hbm, bnd, bsem = refs.pop(0), refs.pop(), refs.pop()
        bcopy = pltpu.make_async_copy(bnd_hbm.at[0], bnd, bsem)
        bcopy.start()
    if mode == "sums":
        tot = refs.pop(0)
    if mode == "turn":
        t_hbm, t2, sems = refs.pop(0), refs.pop(), refs.pop()
        half = t2.shape[0] // 2
        loads = [
            pltpu.make_async_copy(t_hbm.at[pl.ds(i * half, half), :], t2.at[pl.ds(i * half, half), :], sems.at[i])
            for i in range(2)
        ]
        for c in loads:
            c.start()
    if mode == "last":
        out, hm, hr = refs
    else:
        v_hbm, out, hm, hr, v2, stgb, vsem = refs
    ntail = up(slots, per)
    blk = slots + ntail
    tlane = lanes(peers)
    for k in range(slots):
        hm[pl.ds(k, peers, stride=slots), :] = arr[pl.ds(k, peers, stride=blk), :]
    for j in range(ntail):
        tail = arr[pl.ds(slots + j, peers, stride=blk), :]
        if j == 0 and mode == "turn":
            sums = jnp.sum(tail, axis=0, keepdims=True)
            sigma = sums[:, L - 2 : L - 1] / sums[:, L - 1 : L]
        for q in range(min(per, slots - j * per)):
            x = pltpu.roll(tail, (L - q * rest) % L, axis=1) if q else tail
            x = jnp.where(tlane < rest, x, 0.0)
            hr[pl.ds(j * per + q, peers, stride=slots), :] = x
    hh, hl = split(jnp.concatenate([hm[...], hr[...]], 1))

    chunk = n // 2
    lane = lanes(chunk)
    count = n // chunk

    def piece(i):
        rows = pl.ds(pl.multiple_of(2 * i * chunk, 2 * chunk), 2 * chunk)
        return pltpu.make_async_copy(v2.at[rows, :], v_hbm.at[rows, :], vsem.at[i])

    if mode != "last":
        v2[pl.ds(2 * n, 16), :] = jnp.zeros((16, L), F32)

    def body(i, _):
        row = pl.multiple_of(i * chunk, chunk)
        rows = pl.ds(row, chunk)
        a2 = dot(jnp.concatenate([fh[rows, :], fl[rows, :]], 0), hh)
        far = a2[:chunk] + a2[chunk:] + dot(fh[rows, :], hl)
        v = part[rows, :] + rate * far
        if mode == "last":
            out[0:L, rows] = v[:, :L].T
            out[L:classes, rows] = v[:, L:].T[:rest]
            return 0
        if mode == "turn":
            mag = jnp.abs(v)
            mag = jnp.sum(mag[:, :L] + mag[:, L:], -1, keepdims=True) * (1.0 / classes) + tiny
            hit = pl.ds(pl.multiple_of(i * half, half), half)
            pltpu.make_async_copy(t_hbm.at[hit, :], t2.at[hit, :], sems.at[i]).wait()
            free = t2[pl.ds(2 * row + 1, chunk, stride=2), :]
            scale = free[:, L - 1 : L] * sigma / mag
        for h in range(2):
            x = v[:, h * L : (h + 1) * L]
            rows2 = pl.ds(2 * row + h, chunk, stride=2)
            if mode == "turn":
                x = t2[rows2, :] + scale * x
                x = jnp.where(lane < rest, x, 0.0) if h else x
            v2[rows2, :] = x
        piece(i).start()
        return 0

    lax.fori_loop(0, count, body, 0)
    if mode != "last":
        extra = tot[0:1, :] if mode == "sums" else None
        pack((bcopy, bnd), v2, stgb, out, extra, peers=peers, slots=slots, per=per, rest=rest)
        for i in range(count):
            piece(i).wait()


def call(kernel, outs, ins, args, scratch=(), vmem=0, flops=0, size=0, name=None, specs=None):
    if specs:
        place = {id(HB): pltpu.HBM, id(VO): pltpu.VMEM}
        outs = tuple(place.get(id(p), jax.ShapeDtypeStruct)(o.shape, o.dtype) for o, p in zip(outs, specs))
    args = [pltpu.with_memory_space_constraint(a, pltpu.HBM) if p is HB else a for a, p in zip(args, ins)]
    return pl.pallas_call(
        kernel,
        out_shape=outs,
        in_specs=ins,
        out_specs=specs or jax.tree.map(lambda _: VM, outs),
        scratch_shapes=list(scratch),
        compiler_params=pltpu.CompilerParams(vmem_limit_bytes=vmem),
        cost_estimate=pl.CostEstimate(flops=flops, bytes_accessed=size, transcendentals=0),
        name=name,
    )(*args)


def swap(x):
    return lax.all_to_all(x, "dom", split_axis=0, concat_axis=0, tiled=True)


def on_device(
    peers, hidden, bases, self_weight, coef, bias, edge_src, edge_dst, edge_rel, send_rows, recv_rows, labels,
    train_mask, bnd_rows, tiles, tile_cols,
):
    n, hdim = hidden.shape
    classes = self_weight.shape[1]
    nrel, nb = coef.shape
    rest = classes - L
    per = (L - 2) // rest
    slots = send_rows.shape[2]
    bnd = bnd_rows.shape[2]
    ne = edge_src.shape[0]
    halo = peers * bnd
    sds = jax.ShapeDtypeStruct
    state = sds((n, 2 * L), F32)
    half = sds((n, 2 * L), BF16)
    blocks = n // L

    dma = lambda k: pltpu.SemaphoreType.DMA((k,))
    blk = up(slots + up(slots, per), 8) * 8
    square = lambda x: x.reshape(-1, L)
    stage = pltpu.VMEM((2 * (peers * slots + 16), L), F32)
    rows2 = pltpu.VMEM((2 * n + 16, L), F32)
    sums = pltpu.VMEM((2 * nrel * n, L), F32)
    wide = (nb + 4) * L
    erows = ne // L
    bnd_rows = 2 * bnd_rows
    sent, _ = call(
        functools.partial(scores_kernel, classes=classes, slots=slots, per=per),
        (sds((peers, blk, L), F32), sds((2 * n, L), F32)),
        [HB, VM, VM, VM, SM, VM, VM, VM, VM],
        (hidden, bases.T, self_weight.T, bias.reshape(1, -1), coef)
        + (square(edge_src), square(edge_dst), square(edge_rel), send_rows),
        [pltpu.VMEM((n, hdim), BF16), pltpu.VMEM((wide, hdim), BF16)]
        + [pltpu.VMEM((n // 4, wide), F32)] * 2
        + [sums] * 5
        + [rows2, stage]
        + [pltpu.VMEM((erows, L), jnp.int32)] * 2
        + [pltpu.VMEM((peers, L), jnp.int32), pltpu.VMEM((2 * n, L), F32), dma(erows), dma(erows), dma(peers)]
        + [dma(2 + 4 * nrel)]
        + [pltpu.SMEM((1, L), jnp.int32)] * (2 * erows + peers),
        vmem=60 * MIB,
        name="scores",
        specs=(VM, HB),
    )
    arrived = swap(sent)
    spread = sds((2 * n, L), F32)
    flat2 = pltpu.VMEM((2 * n, L), F32)
    labv = pltpu.VMEM((n, L), F32)
    halfv = pltpu.VMEM((n, 2 * L), BF16)
    nh, nl, fh, fl, labk, cnt = call(
        tiles_kernel,
        (half, half, sds((n, halo), BF16), sds((n, halo), BF16), sds((n, L), F32), sds((8, L), F32)),
        [VM, SM, VM, VM],
        (tiles, tile_cols, square(labels), square(train_mask)),
        [halfv, halfv, labv, dma(3)],
        vmem=28 * MIB,
        flops=10**7,
        size=8 * 10**6,
        name="tiles",
        specs=(HB, HB, VM, VM, HB, VM),
    )
    lines = peers * (bnd + up(bnd, per))
    packed = sds((lines, L), F32)
    stageb = pltpu.VMEM((2 * halo, L), F32)
    bnds = pltpu.SMEM((peers, bnd), jnp.int32)
    base, v, out = call(
        functools.partial(errors_kernel, classes=classes, per=per, n=n),
        (spread, spread, packed),
        [VM, VM, HB, HB],
        (arrived, recv_rows, bnd_rows, labk),
        [stage, rows2, rows2, stageb, labv, pltpu.VMEM((peers, L), jnp.int32), bnds, dma(2), dma(peers)]
        + [pltpu.SemaphoreType.DMA((2, n // L))]
        + [pltpu.SMEM((1, L), jnp.int32)] * peers,
        vmem=28 * MIB,
        name="errors",
        specs=(HB, HB, VO),
    )
    e = v
    hscr = [pltpu.VMEM((halo, L), F32)] * 2
    for step in range(2 * ITERS):
        rate = correct_rate if step < ITERS else smooth_rate
        halos = swap(out.reshape(peers, 1, -1)).reshape(lines, L)
        sums = step == 0
        mode = "last" if step == 2 * ITERS - 1 else "turn" if step == ITERS - 1 else "sums" if step == ITERS - 2 else "step"
        got = call(
            functools.partial(near_kernel, rate=rate, classes=classes, sums=sums),
            (state, sds((8, L), F32)) if sums else (state,),
            [HB, HB, HB, HB, SM] + [VM] * sums,
            (v, e, nh, nl, tile_cols) + ((cnt,) if sums else ()),
            [flat2, flat2, halfv, halfv, halfv, halfv, dma(4)],
            vmem=24 * MIB,
            flops=10**9,
            size=8 * 10**6,
            name="near",
        )
        part = got[0]
        if sums:
            tot = got[1]
        far = functools.partial(
            far_kernel, rate=rate, classes=classes, per=per, mode=mode, peers=peers, slots=bnd, n=n
        )
        args, ins = (halos, fh, fl, part), [VM] * 4
        if mode == "last":
            return call(far, sds((classes, n), F32), ins, args, hscr, vmem=24 * MIB, name="far_last").T
        args, ins = args + (bnd_rows,), ins + [HB]
        scratch = hscr + [rows2, stageb, dma(n // L)]
        if mode == "sums":
            args, ins = args + (tot,), ins + [VM]
        if mode == "turn":
            args, ins = args + (base,), ins + [HB]
            scratch = scratch + [dma(2), flat2]
        scratch = scratch + [pltpu.SemaphoreType.DMA, bnds]
        v, out = call(
            far, (spread, packed), ins, args, scratch, vmem=24 * MIB, name="far_" + mode, specs=(HB, VO)
        )
        if mode == "turn":
            e = v


def solution(mesh):
    row = P("dom")
    in_specs = (
        P("dom", None), P(), P(), P(), P(), row, row, row, P("dom", None, None), P("dom", None, None), row, row,
        P("dom", None, None), P("dom", None, None), row,
    )
    return jax.shard_map(
        functools.partial(on_device, mesh.shape["dom"]),
        mesh=mesh,
        in_specs=in_specs,
        out_specs=P("dom", None),
        check_vma=False,
    )
```

```python
import functools

import jax
import jax.numpy as jnp
from jax import lax
from jax.experimental import pallas as pl
from jax.experimental.pallas import tpu as pltpu
from jax.sharding import PartitionSpec as P

TILES_ROW = 4
LOC_ROW = 2
ITERS = 3
L = 128

correct_rate = 0.8
smooth_rate = 0.75
tiny = 1e-06

F32 = jnp.float32
BF16 = jnp.bfloat16
VM = pl.BlockSpec(memory_space=pltpu.VMEM)
SM = pl.BlockSpec(memory_space=pltpu.SMEM)
HB = pl.BlockSpec(memory_space=pltpu.HBM)
VO = pl.BlockSpec(memory_space=pltpu.VMEM)
MIB = 1 << 20


def up(a, b):
    return -(-a // b)


def split(x):
    hi = x.astype(BF16)
    return hi, (x - hi.astype(F32)).astype(BF16)


def dot(a, b):
    return jnp.dot(a, b, preferred_element_type=F32)


def lanes(rows):
    return lax.broadcasted_iota(jnp.int32, (rows, L), 1)


def pair(ref, row):
    return ref.at[pl.ds(pl.multiple_of(2 * row, 2), 2), :]


def gather_rows(idx, src, stg, peers, slots):
    copy, idx_ref = idx
    copy.wait()
    group = 4

    def body(g, _):
        for p in range(group):
            for k in range(slots):
                at = pl.ds(pl.multiple_of(idx_ref[g * group + p, k], 2), 2)
                pair(stg, g * (group * slots) + (p * slots + k))[...] = src[at, :]
        return 0

    lax.fori_loop(0, peers // group, body, 0)


def fetch(src, rows, refs, sems):
    copies = [pltpu.make_async_copy(src.at[pl.ds(i, 1), :], r, sems.at[i]) for i, r in zip(rows, refs)]
    for c in copies:
        c.start()
    return copies


def scores_kernel(
    hid_hbm, bt, st, bias, coef, es, ed, er, send, out, blank,
    hid, pt, p0, p1, m2, s0, s1, s2, s3, sc2, stg, kj, kd, kp, zero, sj, sd, sp, sz, *ks, classes, slots, per,
):
    n, hdim = hid.shape
    hload = pltpu.make_async_copy(hid_hbm, hid, sz.at[1 + 4 * coef.shape[0]])
    hload.start()
    rest = classes - L
    nrel, nb = coef.shape
    peers = out.shape[0]
    erows = es.shape[0]
    acc = (s0, s1, s2, s3)
    ksj, ksd, ksp = ks[:erows], ks[erows : 2 * erows], ks[2 * erows :]
    kj[...] = (er[...] * n + es[...]) * 2
    kd[...] = (er[...] * n + ed[...]) * 2
    kp[:, 0:slots] = send[0] * 2
    copies = fetch(kj, range(erows), ksj, sj) + fetch(kd, range(erows), ksd, sd) + fetch(kp, range(peers), ksp, sp)
    zero[...] = jnp.zeros_like(zero)
    wipe = pltpu.make_async_copy(zero, blank, sz.at[0])
    wipe.start()

    base_r = nb * L
    base_s = base_r + 2 * L
    gap = 2 * L // nb
    step = 2 * L

    def arrange(i, _):
        cols = pl.ds(pl.multiple_of(i * step, step), step)
        for b in range(nb):
            x = bt[b * classes : (b + 1) * classes, cols].astype(F32)
            pt[b * L : (b + 1) * L, cols] = x[:L].astype(BF16)
            tail = jnp.concatenate([x[L:], jnp.zeros((gap - rest, step), F32)], 0)
            pt[base_r + b * gap : base_r + (b + 1) * gap, cols] = tail.astype(BF16)
        x = st[:, cols].astype(F32)
        pt[base_s : base_s + L, cols] = x[:L].astype(BF16)
        tail = jnp.concatenate([x[L:], jnp.zeros((L - rest, step), F32)], 0)
        pt[base_s + L : base_s + 2 * L, cols] = tail.astype(BF16)
        return 0

    lax.fori_loop(0, hdim // step, arrange, 0)
    wipe.wait()
    zrows = blank.shape[0]
    for c, s in enumerate(acc[:3]):
        for i in range(nrel):
            copies.append(pltpu.make_async_copy(blank, s.at[pl.ds(i * zrows, zrows), :], sz.at[1 + c * nrel + i]))
            copies[-1].start()

    chunk = p0.shape[0]
    sub = 128
    lane = lanes(sub)
    one = jnp.where(lane == rest, 1.0, 0.0)
    lane8 = lanes(8)
    gains = []
    for r in range(nrel):
        for h in range(2):
            g = jnp.zeros((8, L), F32)
            for b in range(nb // 2):
                g = jnp.where(lane8 // gap == b, coef[r, h * (nb // 2) + b], g)
            gains.append(g[0:1])
    bias0 = bias[0:1, 0:L]
    bias1 = jnp.concatenate([bias[0:1, L:classes], jnp.zeros((1, L - rest), F32)], 1)

    def project(i, dst):
        h = hid[pl.ds(pl.multiple_of(i * chunk, chunk), chunk), :]
        for j in range(0, base_s + 2 * L, 2 * L):
            dst[:, j : j + 2 * L] = lax.dot_general(
                h, pt[j : j + 2 * L, :], (((1,), (1,)), ((), ())), preferred_element_type=F32
            )
            yield

    def mix(i, src):
        for u in range(0, chunk, sub):
            rows = slice(u, u + sub)
            row = i * chunk + u
            mains = [src[rows, b * L : (b + 1) * L] for b in range(nb)]
            size = 2 * sub
            q = [src[rows, base_r + h * L : base_r + (h + 1) * L] for h in range(2)]
            for r in range(nrel):
                x = coef[r, 0] * mains[0]
                for b in range(1, nb):
                    x = x + coef[r, b] * mains[b]
                t = gains[2 * r] * q[0] + gains[2 * r + 1] * q[1]
                turn = L // 2
                while turn >= gap:
                    t = t + pltpu.roll(t, turn, axis=1)
                    turn //= 2
                at = 2 * (r * n + row)
                m2[pl.ds(at, sub, stride=2), :] = x
                m2[pl.ds(at + 1, sub, stride=2), :] = jnp.where(lane < rest, t, one)
                s3[pl.ds(pl.multiple_of(2 * nrel * row + r * size, size), size), :] = jnp.zeros((size, L), F32)
                yield
            at = 2 * row
            sc2[pl.ds(at, sub, stride=2), :] = src[rows, base_s : base_s + L] + bias0
            sc2[pl.ds(at + 1, sub, stride=2), :] = src[rows, base_s + L : base_s + 2 * L] + bias1

    def weave(*works):
        works = list(works)
        while works:
            for w in list(works):
                if next(w, 0) == 0:
                    works.remove(w)

    sc2[pl.ds(2 * n, 16), :] = jnp.zeros((16, L), F32)
    count = n // chunk
    hload.wait()
    weave(project(0, p0))

    def pipe(t, _):
        weave(mix(2 * t, p0), project(2 * t + 1, p1))
        weave(mix(2 * t + 1, p1), project(2 * t + 2, p0))
        return 0

    lax.fori_loop(0, count // 2 - 1, pipe, 0)
    weave(mix(count - 2, p0), project(count - 1, p1))
    weave(mix(count - 1, p1))

    for c in copies:
        c.wait()

    def edges(t, _):
        for v in range(2):
            for e in range(erows):
                s = acc[e % 4]
                j = ksj[e][0, 2 * t + v]
                d = ksd[e][0, 2 * t + v]
                src = m2[pl.ds(pl.multiple_of(j, 2), 2), :]
                at = pl.ds(pl.multiple_of(d, 2), 2)
                s[at, :] = s[at, :] + src
        return 0

    lax.fori_loop(0, L // 2, edges, 0)

    fin = 128
    flane = lanes(fin)

    def finish(i, _):
        row = i * fin
        a0 = sc2[pl.ds(2 * row, fin, stride=2), :]
        a1 = sc2[pl.ds(2 * row + 1, fin, stride=2), :]
        for r in range(nrel):
            rows = [pl.ds(2 * (r * n + row) + h, fin, stride=2) for h in range(2)]
            m, t = [(s0[w, :] + s1[w, :]) + (s2[w, :] + s3[w, :]) for w in rows]
            inv = 1.0 / jnp.maximum(t[:, rest : rest + 1], 1.0)
            a0 = a0 + m * inv
            a1 = a1 + t * inv
        sc2[pl.ds(2 * row, fin, stride=2), :] = a0
        sc2[pl.ds(2 * row + 1, fin, stride=2), :] = jnp.where(flane < rest, a1, 0.0)
        return 0

    lax.fori_loop(0, n // fin, finish, 0)

    def collect(t, _):
        for k in (2 * t, 2 * t + 1):
            for p in range(peers):
                at = pl.ds(pl.multiple_of(ksp[p][0, k], 2), 2)
                pair(stg, p * slots + k)[...] = sc2[at, :]
        return 0

    lax.fori_loop(0, slots // 2, collect, 0)
    ntail = up(slots, per)

    many = 8

    def put(g, _):
        tails = []
        for v in range(many):
            p = g * many + v
            at = p * 2 * slots
            out[p, 0:slots, :] = stg[pl.ds(at, slots, stride=2), :]
            tails.append([stg[pl.ds(at + 2 * q + 1, ntail, stride=2 * per), :] for q in range(per)])
        tails = [[pltpu.roll(x, q * rest, axis=1) if q else x for q, x in enumerate(t)] for t in tails]
        for v, t in enumerate(tails):
            out[g * many + v, slots : slots + ntail, :] = sum(t[1:], t[0])
        return 0

    lax.fori_loop(0, peers // many, put, 0)


def pack(bnd, v2, stg, out, extra, *, peers, slots, per, rest):
    gather_rows(bnd, v2, stg, peers, slots)
    ntail = up(slots, per)
    blk = slots + ntail
    for k in range(slots):
        out[pl.ds(k, peers, stride=blk), :] = stg[pl.ds(2 * k, peers, stride=2 * slots), :]
    for j in range(ntail):
        tail = None
        for q in range(min(per, slots - j * per)):
            x = stg[pl.ds(2 * (j * per + q) + 1, peers, stride=2 * slots), :]
            x = pltpu.roll(x, q * rest, axis=1) if q else x
            tail = x if tail is None else tail + x
        if j == 0 and extra is not None:
            tail = tail + extra
        out[pl.ds(slots + j, peers, stride=blk), :] = tail


def errors_kernel(
    arr, recv, bnd_hbm, labk_hbm, t_hbm, e_hbm, out, stg, base2, v2, stgb, labk, kr, bnd, sems, sr, esem, *ksr,
    classes, per, n,
):
    rest = classes - L
    peers, blk, _ = arr.shape
    slots = recv.shape[2]
    ntail = up(slots, per)
    tlane = lanes(ntail)
    load = pltpu.make_async_copy(labk_hbm, labk, sems.at[0])
    load.start()
    bcopy = pltpu.make_async_copy(bnd_hbm.at[0], bnd, sems.at[1])
    bcopy.start()
    kr[:, 0:slots] = recv[0] * 2
    copies = fetch(kr, range(peers), ksr, sr)

    many = 8

    def unpack(g, _):
        tails = []
        for v in range(many):
            tail = arr[g * many + v, slots : slots + ntail, :]
            tails.append([pltpu.roll(tail, (L - q * rest) % L, axis=1) if q else tail for q in range(per)])
        for v in range(many):
            p = g * many + v
            at = p * 2 * slots
            for q, x in enumerate(tails[v]):
                stg[pl.ds(at + 2 * q + 1, ntail, stride=2 * per), :] = jnp.where(tlane < rest, x, 0.0)
            stg[pl.ds(at, slots, stride=2), :] = arr[p, 0:slots, :]
        return 0

    lax.fori_loop(0, peers // many, unpack, 0)

    for c in copies:
        c.wait()
    unroll = 2

    def spread(t, _):
        for v in range(unroll):
            k = t * unroll + v
            for p in range(peers):
                at = pl.ds(pl.multiple_of(ksr[p][0, k], 2), 2)
                base2[at, :] = pair(stg, p * slots + k)[...]
        return 0

    lax.fori_loop(0, slots // unroll, spread, 0)
    load.wait()

    chunk = 128
    lane = lanes(chunk)

    def error(i, _):
        row = pl.multiple_of(i * chunk, chunk)
        lab = labk[pl.ds(row, chunk), :]
        known = lab >= 0.0
        for h in range(2):
            rows = pl.ds(2 * row + h, chunk, stride=2)
            onehot = jnp.where(lab == (lane + h * L).astype(F32), 1.0, 0.0)
            b = base2[rows, :]
            v2[rows, :] = jnp.where(known, onehot - b, 0.0)
            t = jnp.where(known, onehot, b)
            base2[rows, :] = jnp.where(lane == L - 1, jnp.where(known, 0.0, 1.0), t) if h else t
        piece(i, 0).start()
        piece(i, 1).start()
        return 0

    def piece(i, w):
        rows = pl.ds(pl.multiple_of(2 * i * chunk, 2 * chunk), 2 * chunk)
        a, b = ((v2, e_hbm), (base2, t_hbm))[w]
        return pltpu.make_async_copy(a.at[rows, :], b.at[rows, :], esem.at[w, i])

    v2[pl.ds(2 * n, 16), :] = jnp.zeros((16, L), F32)
    lax.fori_loop(0, n // chunk, error, 0)
    pack((bcopy, bnd), v2, stgb, out, None, peers=peers, slots=bnd.shape[1], per=per, rest=rest)
    for i in range(n // chunk):
        piece(i, 0).wait()
        piece(i, 1).wait()


def tiles_kernel(tiles, cols, labels, mask, nh_hbm, nl_hbm, fh, fl, lab_hbm, cnt, nh, nl, labk, sems):
    blocks = labels.shape[0]
    halo = fh.shape[1] // L

    def body(b, _):
        rows = pl.ds(pl.multiple_of(b * L, L), L)
        for j in range(LOC_ROW):
            hi, lo = split(tiles[b * TILES_ROW + j])
            nh[rows, j * L : (j + 1) * L] = hi
            nl[rows, j * L : (j + 1) * L] = lo
        for q in range(halo):
            acc = jnp.zeros((L, L), F32)
            for j in range(LOC_ROW, TILES_ROW):
                hit = cols[b * TILES_ROW + j] == blocks + q
                acc = acc + jnp.where(hit, tiles[b * TILES_ROW + j], 0.0)
            hi, lo = split(acc)
            fh[rows, q * L : (q + 1) * L] = hi
            fl[rows, q * L : (q + 1) * L] = lo
        lab = jnp.where(mask[pl.ds(b, 1), :] > 0, labels[pl.ds(b, 1), :], -1).astype(F32)
        labk[rows, :] = jnp.broadcast_to(lab, (L, L)).T
        return 0

    lax.fori_loop(0, blocks, body, 0)
    pairs = ((nh, nh_hbm), (nl, nl_hbm), (labk, lab_hbm))
    saves = [pltpu.make_async_copy(a, b, sems.at[i]) for i, (a, b) in enumerate(pairs)]
    for c in saves:
        c.start()
    cnt[...] = jnp.zeros(cnt.shape, F32) + jnp.sum(mask[...].astype(F32))
    for c in saves:
        c.wait()


def near_kernel(v_hbm, e_hbm, nh_hbm, nl_hbm, cols, *refs, rate, classes, sums):
    if sums:
        cnt, part, tot, v2, e2, nh, nl, vh, vl, sems = refs
    else:
        part, v2, e2, nh, nl, vh, vl, sems = refs
    pairs = ((v_hbm, v2), (nh_hbm, nh), (nl_hbm, nl), (e_hbm, e2))
    loads = [pltpu.make_async_copy(a, b, sems.at[i]) for i, (a, b) in enumerate(pairs)]
    for c in loads:
        c.start()
    blocks = part.shape[0] // L
    loads[0].wait()

    def halve(b, _):
        rows = pl.ds(pl.multiple_of(b * L, L), L)
        for h in range(2):
            hi, lo = split(v2[pl.ds(b * 2 * L + h, L, stride=2), :])
            vh[rows, h * L : (h + 1) * L] = hi
            vl[rows, h * L : (h + 1) * L] = lo
        return 0

    lax.fori_loop(0, blocks, halve, 0)
    for c in loads[1:]:
        c.wait()

    def body(b, acc):
        rows = pl.ds(pl.multiple_of(b * L, L), L)
        at = [pl.ds(pl.multiple_of(cols[b * TILES_ROW + j] * L, L), L) for j in range(LOC_ROW)]
        bh = jnp.concatenate([vh[a, :] for a in at], 0)
        bl = jnp.concatenate([vl[a, :] for a in at], 0)
        a2 = dot(jnp.concatenate([nh[rows, :], nl[rows, :]], 0), bh)
        near = a2[:L] + a2[L:] + dot(nh[rows, :], bl)
        for h in range(2):
            ev = e2[pl.ds(b * 2 * L + h, L, stride=2), :]
            part[rows, h * L : (h + 1) * L] = (1.0 - rate) * ev + rate * near[:, h * L : (h + 1) * L]
            if sums:
                acc = acc + jnp.sum(jnp.abs(ev).reshape(L // 8, 8, L), 0)
        return acc

    acc = lax.fori_loop(0, blocks, body, jnp.zeros((8, L), F32))
    if sums:
        total = jnp.sum(acc) * (1.0 / classes)
        lane = lanes(8)
        tot[...] = jnp.where(lane == L - 2, total, jnp.where(lane == L - 1, cnt[...], 0.0))


def far_kernel(*refs, rate, classes, per, mode, peers, slots, n):
    rest = classes - L
    refs = list(refs)
    arr, fh, fl, part = refs[:4]
    refs = refs[4:]
    if mode != "last":
        bnd_hbm, bnd, bsem = refs.pop(0), refs.pop(), refs.pop()
        bcopy = pltpu.make_async_copy(bnd_hbm.at[0], bnd, bsem)
        bcopy.start()
    if mode == "sums":
        tot = refs.pop(0)
    if mode == "turn":
        t_hbm, t2, sems = refs.pop(0), refs.pop(), refs.pop()
        half = t2.shape[0] // 2
        loads = [
            pltpu.make_async_copy(t_hbm.at[pl.ds(i * half, half), :], t2.at[pl.ds(i * half, half), :], sems.at[i])
            for i in range(2)
        ]
        for c in loads:
            c.start()
    if mode == "last":
        out, hm, hr = refs
    else:
        v_hbm, out, hm, hr, v2, stgb, vsem = refs
    ntail = up(slots, per)
    blk = slots + ntail
    tlane = lanes(peers)
    for k in range(slots):
        hm[pl.ds(k, peers, stride=slots), :] = arr[pl.ds(k, peers, stride=blk), :]
    for j in range(ntail):
        tail = arr[pl.ds(slots + j, peers, stride=blk), :]
        if j == 0 and mode == "turn":
            sums = jnp.sum(tail, axis=0, keepdims=True)
            sigma = sums[:, L - 2 : L - 1] / sums[:, L - 1 : L]
        for q in range(min(per, slots - j * per)):
            x = pltpu.roll(tail, (L - q * rest) % L, axis=1) if q else tail
            x = jnp.where(tlane < rest, x, 0.0)
            hr[pl.ds(j * per + q, peers, stride=slots), :] = x
    hh, hl = split(jnp.concatenate([hm[...], hr[...]], 1))

    chunk = n // 2
    lane = lanes(chunk)
    count = n // chunk

    parts = 6
    small = chunk // parts

    def piece(i):
        rows = pl.ds(pl.multiple_of(2 * i * small, 2 * small), 2 * small)
        return pltpu.make_async_copy(v2.at[rows, :], v_hbm.at[rows, :], vsem.at[i])

    if mode != "last":
        v2[pl.ds(2 * n, 16), :] = jnp.zeros((16, L), F32)

    def body(i, _):
        row = pl.multiple_of(i * chunk, chunk)
        rows = pl.ds(row, chunk)
        a2 = dot(jnp.concatenate([fh[rows, :], fl[rows, :]], 0), hh)
        far = a2[:chunk] + a2[chunk:] + dot(fh[rows, :], hl)
        v = part[rows, :] + rate * far
        if mode == "last":
            out[0:L, rows] = v[:, :L].T
            out[L:classes, rows] = v[:, L:].T[:rest]
            return 0
        if mode == "turn":
            mag = jnp.abs(v)
            mag = jnp.sum(mag[:, :L] + mag[:, L:], -1, keepdims=True) * (1.0 / classes) + tiny
            hit = pl.ds(pl.multiple_of(i * half, half), half)
            pltpu.make_async_copy(t_hbm.at[hit, :], t2.at[hit, :], sems.at[i]).wait()
            free = t2[pl.ds(2 * row + 1, chunk, stride=2), :]
            scale = free[:, L - 1 : L] * sigma / mag
        for w in range(parts):
            own = slice(w * small, (w + 1) * small)
            for h in range(2):
                x = v[own, h * L : (h + 1) * L]
                rows2 = pl.ds(2 * (row + w * small) + h, small, stride=2)
                if mode == "turn":
                    x = t2[rows2, :] + scale[own] * x
                    x = jnp.where(lane[own] < rest, x, 0.0) if h else x
                v2[rows2, :] = x
            piece(i * parts + w).start()
        return 0

    lax.fori_loop(0, count, body, 0)
    if mode != "last":
        extra = tot[0:1, :] if mode == "sums" else None
        pack((bcopy, bnd), v2, stgb, out, extra, peers=peers, slots=slots, per=per, rest=rest)
        for i in range(count * parts):
            piece(i).wait()


def call(kernel, outs, ins, args, scratch=(), vmem=0, flops=0, size=0, name=None, specs=None):
    if specs:
        place = {id(HB): pltpu.HBM, id(VO): pltpu.VMEM}
        outs = tuple(place.get(id(p), jax.ShapeDtypeStruct)(o.shape, o.dtype) for o, p in zip(outs, specs))
    args = [pltpu.with_memory_space_constraint(a, pltpu.HBM) if p is HB else a for a, p in zip(args, ins)]
    return pl.pallas_call(
        kernel,
        out_shape=outs,
        in_specs=ins,
        out_specs=specs or jax.tree.map(lambda _: VM, outs),
        scratch_shapes=list(scratch),
        compiler_params=pltpu.CompilerParams(vmem_limit_bytes=vmem),
        cost_estimate=pl.CostEstimate(flops=flops, bytes_accessed=size, transcendentals=0),
        name=name,
    )(*args)


def swap(x):
    return lax.all_to_all(x, "dom", split_axis=0, concat_axis=0, tiled=True)


def on_device(
    peers, hidden, bases, self_weight, coef, bias, edge_src, edge_dst, edge_rel, send_rows, recv_rows, labels,
    train_mask, bnd_rows, tiles, tile_cols,
):
    n, hdim = hidden.shape
    classes = self_weight.shape[1]
    nrel, nb = coef.shape
    rest = classes - L
    per = (L - 2) // rest
    slots = send_rows.shape[2]
    bnd = bnd_rows.shape[2]
    ne = edge_src.shape[0]
    halo = peers * bnd
    sds = jax.ShapeDtypeStruct
    state = sds((n, 2 * L), F32)
    half = sds((n, 2 * L), BF16)
    blocks = n // L

    dma = lambda k: pltpu.SemaphoreType.DMA((k,))
    blk = up(slots + up(slots, per), 8) * 8
    square = lambda x: x.reshape(-1, L)
    stage = pltpu.VMEM((2 * (peers * slots + 16), L), F32)
    rows2 = pltpu.VMEM((2 * n + 16, L), F32)
    sums = pltpu.VMEM((2 * nrel * n, L), F32)
    wide = (nb + 4) * L
    erows = ne // L
    bnd_rows = 2 * bnd_rows
    sent, _ = call(
        functools.partial(scores_kernel, classes=classes, slots=slots, per=per),
        (sds((peers, blk, L), F32), sds((2 * n, L), F32)),
        [HB, VM, VM, VM, SM, VM, VM, VM, VM],
        (hidden, bases.T, self_weight.T, bias.reshape(1, -1), coef)
        + (square(edge_src), square(edge_dst), square(edge_rel), send_rows),
        [pltpu.VMEM((n, hdim), BF16), pltpu.VMEM((wide, hdim), BF16)]
        + [pltpu.VMEM((n // 4, wide), F32)] * 2
        + [sums] * 5
        + [rows2, stage]
        + [pltpu.VMEM((erows, L), jnp.int32)] * 2
        + [pltpu.VMEM((peers, L), jnp.int32), pltpu.VMEM((2 * n, L), F32), dma(erows), dma(erows), dma(peers)]
        + [dma(2 + 4 * nrel)]
        + [pltpu.SMEM((1, L), jnp.int32)] * (2 * erows + peers),
        vmem=60 * MIB,
        name="scores",
        specs=(VM, HB),
    )
    arrived = swap(sent)
    spread = sds((2 * n, L), F32)
    flat2 = pltpu.VMEM((2 * n, L), F32)
    labv = pltpu.VMEM((n, L), F32)
    halfv = pltpu.VMEM((n, 2 * L), BF16)
    nh, nl, fh, fl, labk, cnt = call(
        tiles_kernel,
        (half, half, sds((n, halo), BF16), sds((n, halo), BF16), sds((n, L), F32), sds((8, L), F32)),
        [VM, SM, VM, VM],
        (tiles, tile_cols, square(labels), square(train_mask)),
        [halfv, halfv, labv, dma(3)],
        vmem=28 * MIB,
        flops=10**7,
        size=8 * 10**6,
        name="tiles",
        specs=(HB, HB, VM, VM, HB, VM),
    )
    lines = peers * (bnd + up(bnd, per))
    packed = sds((lines, L), F32)
    stageb = pltpu.VMEM((2 * halo, L), F32)
    bnds = pltpu.SMEM((peers, bnd), jnp.int32)
    base, v, out = call(
        functools.partial(errors_kernel, classes=classes, per=per, n=n),
        (spread, spread, packed),
        [VM, VM, HB, HB],
        (arrived, recv_rows, bnd_rows, labk),
        [stage, rows2, rows2, stageb, labv, pltpu.VMEM((peers, L), jnp.int32), bnds, dma(2), dma(peers)]
        + [pltpu.SemaphoreType.DMA((2, n // L))]
        + [pltpu.SMEM((1, L), jnp.int32)] * peers,
        vmem=28 * MIB,
        name="errors",
        specs=(HB, HB, VO),
    )
    e = v
    hscr = [pltpu.VMEM((halo, L), F32)] * 2
    for step in range(2 * ITERS):
        rate = correct_rate if step < ITERS else smooth_rate
        halos = swap(out.reshape(peers, 1, -1)).reshape(lines, L)
        sums = step == 0
        mode = "last" if step == 2 * ITERS - 1 else "turn" if step == ITERS - 1 else "sums" if step == ITERS - 2 else "step"
        got = call(
            functools.partial(near_kernel, rate=rate, classes=classes, sums=sums),
            (state, sds((8, L), F32)) if sums else (state,),
            [HB, HB, HB, HB, SM] + [VM] * sums,
            (v, e, nh, nl, tile_cols) + ((cnt,) if sums else ()),
            [flat2, flat2, halfv, halfv, halfv, halfv, dma(4)],
            vmem=24 * MIB,
            flops=10**9,
            size=8 * 10**6,
            name="near",
        )
        part = got[0]
        if sums:
            tot = got[1]
        far = functools.partial(
            far_kernel, rate=rate, classes=classes, per=per, mode=mode, peers=peers, slots=bnd, n=n
        )
        args, ins = (halos, fh, fl, part), [VM] * 4
        if mode == "last":
            return call(far, sds((classes, n), F32), ins, args, hscr, vmem=24 * MIB, name="far_last").T
        args, ins = args + (bnd_rows,), ins + [HB]
        scratch = hscr + [rows2, stageb, dma(n // L)]
        if mode == "sums":
            args, ins = args + (tot,), ins + [VM]
        if mode == "turn":
            args, ins = args + (base,), ins + [HB]
            scratch = scratch + [dma(2), flat2]
        scratch = scratch + [pltpu.SemaphoreType.DMA, bnds]
        v, out = call(
            far, (spread, packed), ins, args, scratch, vmem=24 * MIB, name="far_" + mode, specs=(HB, VO)
        )
        if mode == "turn":
            e = v


def solution(mesh):
    row = P("dom")
    in_specs = (
        P("dom", None), P(), P(), P(), P(), row, row, row, P("dom", None, None), P("dom", None, None), row, row,
        P("dom", None, None), P("dom", None, None), row,
    )
    return jax.shard_map(
        functools.partial(on_device, mesh.shape["dom"]),
        mesh=mesh,
        in_specs=in_specs,
        out_specs=P("dom", None),
        check_vma=False,
    )
```

```python
import functools

import jax
import jax.numpy as jnp
from jax import lax
from jax.experimental import pallas as pl
from jax.experimental.pallas import tpu as pltpu
from jax.sharding import PartitionSpec as P

TILES_ROW = 4
LOC_ROW = 2
ITERS = 3
L = 128

correct_rate = 0.8
smooth_rate = 0.75
tiny = 1e-06

F32 = jnp.float32
BF16 = jnp.bfloat16
VM = pl.BlockSpec(memory_space=pltpu.VMEM)
SM = pl.BlockSpec(memory_space=pltpu.SMEM)
HB = pl.BlockSpec(memory_space=pltpu.HBM)
VO = pl.BlockSpec(memory_space=pltpu.VMEM)
MIB = 1 << 20


def up(a, b):
    return -(-a // b)


def split(x):
    hi = x.astype(BF16)
    return hi, (x - hi.astype(F32)).astype(BF16)


def dot(a, b):
    return jnp.dot(a, b, preferred_element_type=F32)


def lanes(rows):
    return lax.broadcasted_iota(jnp.int32, (rows, L), 1)


def pair(ref, row):
    return ref.at[pl.ds(pl.multiple_of(2 * row, 2), 2), :]


def gather_rows(idx, src, stg, peers, slots):
    copy, idx_ref = idx
    copy.wait()
    group = 4

    def body(g, _):
        for p in range(group):
            for k in range(slots):
                at = pl.ds(pl.multiple_of(idx_ref[g * group + p, k], 2), 2)
                pair(stg, g * (group * slots) + (p * slots + k))[...] = src[at, :]
        return 0

    lax.fori_loop(0, peers // group, body, 0)


def fetch(src, rows, refs, sems):
    copies = [pltpu.make_async_copy(src.at[pl.ds(i, 1), :], r, sems.at[i]) for i, r in zip(rows, refs)]
    for c in copies:
        c.start()
    return copies


def scores_kernel(
    hid_hbm, bt, st, bias, coef, es, ed, er, send, out, blank,
    hid, pt, p0, p1, m2, s0, s1, s2, s3, sc2, stg, kj, kd, kp, zero, sj, sd, sp, sz, *ks, classes, slots, per,
):
    n, hdim = hid.shape
    hload = pltpu.make_async_copy(hid_hbm, hid, sz.at[1 + 4 * coef.shape[0]])
    hload.start()
    rest = classes - L
    nrel, nb = coef.shape
    peers = out.shape[0]
    erows = es.shape[0]
    acc = (s0, s1, s2, s3)
    ksj, ksd, ksp = ks[:erows], ks[erows : 2 * erows], ks[2 * erows :]
    kj[...] = (er[...] * n + es[...]) * 2
    kd[...] = (er[...] * n + ed[...]) * 2
    kp[:, 0:slots] = send[0] * 2
    copies = fetch(kj, range(erows), ksj, sj) + fetch(kd, range(erows), ksd, sd) + fetch(kp, range(peers), ksp, sp)
    zero[...] = jnp.zeros_like(zero)
    wipe = pltpu.make_async_copy(zero, blank, sz.at[0])
    wipe.start()

    base_r = nb * L
    base_s = base_r + 2 * L
    gap = 2 * L // nb
    step = 2 * L

    def arrange(i, _):
        cols = pl.ds(pl.multiple_of(i * step, step), step)
        for b in range(nb):
            x = bt[b * classes : (b + 1) * classes, cols].astype(F32)
            pt[b * L : (b + 1) * L, cols] = x[:L].astype(BF16)
            tail = jnp.concatenate([x[L:], jnp.zeros((gap - rest, step), F32)], 0)
            pt[base_r + b * gap : base_r + (b + 1) * gap, cols] = tail.astype(BF16)
        x = st[:, cols].astype(F32)
        pt[base_s : base_s + L, cols] = x[:L].astype(BF16)
        tail = jnp.concatenate([x[L:], jnp.zeros((L - rest, step), F32)], 0)
        pt[base_s + L : base_s + 2 * L, cols] = tail.astype(BF16)
        return 0

    lax.fori_loop(0, hdim // step, arrange, 0)
    wipe.wait()
    zrows = blank.shape[0]
    for c, s in enumerate(acc[:3]):
        for i in range(nrel):
            copies.append(pltpu.make_async_copy(blank, s.at[pl.ds(i * zrows, zrows), :], sz.at[1 + c * nrel + i]))
            copies[-1].start()

    chunk = p0.shape[0]
    sub = 128
    lane = lanes(sub)
    one = jnp.where(lane == rest, 1.0, 0.0)
    lane8 = lanes(8)
    gains = []
    for r in range(nrel):
        for h in range(2):
            g = jnp.zeros((8, L), F32)
            for b in range(nb // 2):
                g = jnp.where(lane8 // gap == b, coef[r, h * (nb // 2) + b], g)
            gains.append(g[0:1])
    bias0 = bias[0:1, 0:L]
    bias1 = jnp.concatenate([bias[0:1, L:classes], jnp.zeros((1, L - rest), F32)], 1)

    def project(i, dst):
        h = hid[pl.ds(pl.multiple_of(i * chunk, chunk), chunk), :]
        for j in range(0, base_s + 2 * L, 2 * L):
            dst[:, j : j + 2 * L] = lax.dot_general(
                h, pt[j : j + 2 * L, :], (((1,), (1,)), ((), ())), preferred_element_type=F32
            )
            yield

    def mix(i, src):
        for u in range(0, chunk, sub):
            rows = slice(u, u + sub)
            row = i * chunk + u
            mains = [src[rows, b * L : (b + 1) * L] for b in range(nb)]
            size = 2 * sub
            q = [src[rows, base_r + h * L : base_r + (h + 1) * L] for h in range(2)]
            for r in range(nrel):
                x = coef[r, 0] * mains[0]
                for b in range(1, nb):
                    x = x + coef[r, b] * mains[b]
                t = gains[2 * r] * q[0] + gains[2 * r + 1] * q[1]
                turn = L // 2
                while turn >= gap:
                    t = t + pltpu.roll(t, turn, axis=1)
                    turn //= 2
                at = 2 * (r * n + row)
                m2[pl.ds(at, sub, stride=2), :] = x
                m2[pl.ds(at + 1, sub, stride=2), :] = jnp.where(lane < rest, t, one)
                s3[pl.ds(pl.multiple_of(2 * nrel * row + r * size, size), size), :] = jnp.zeros((size, L), F32)
                yield
            at = 2 * row
            sc2[pl.ds(at, sub, stride=2), :] = src[rows, base_s : base_s + L] + bias0
            sc2[pl.ds(at + 1, sub, stride=2), :] = src[rows, base_s + L : base_s + 2 * L] + bias1

    def weave(*works):
        works = list(works)
        while works:
            for w in list(works):
                if next(w, 0) == 0:
                    works.remove(w)

    sc2[pl.ds(2 * n, 16), :] = jnp.zeros((16, L), F32)
    count = n // chunk
    hload.wait()
    weave(project(0, p0))

    def pipe(t, _):
        weave(mix(2 * t, p0), project(2 * t + 1, p1))
        weave(mix(2 * t + 1, p1), project(2 * t + 2, p0))
        return 0

    lax.fori_loop(0, count // 2 - 1, pipe, 0)
    weave(mix(count - 2, p0), project(count - 1, p1))
    weave(mix(count - 1, p1))

    for c in copies:
        c.wait()

    def edges(t, _):
        for v in range(2):
            for e in range(erows):
                s = acc[e % 4]
                j = ksj[e][0, 2 * t + v]
                d = ksd[e][0, 2 * t + v]
                src = m2[pl.ds(pl.multiple_of(j, 2), 2), :]
                at = pl.ds(pl.multiple_of(d, 2), 2)
                s[at, :] = s[at, :] + src
        return 0

    lax.fori_loop(0, L // 2, edges, 0)

    fin = 128
    flane = lanes(fin)

    def finish(i, _):
        row = i * fin
        a0 = sc2[pl.ds(2 * row, fin, stride=2), :]
        a1 = sc2[pl.ds(2 * row + 1, fin, stride=2), :]
        for r in range(nrel):
            rows = [pl.ds(2 * (r * n + row) + h, fin, stride=2) for h in range(2)]
            m, t = [(s0[w, :] + s1[w, :]) + (s2[w, :] + s3[w, :]) for w in rows]
            inv = 1.0 / jnp.maximum(t[:, rest : rest + 1], 1.0)
            a0 = a0 + m * inv
            a1 = a1 + t * inv
        sc2[pl.ds(2 * row, fin, stride=2), :] = a0
        sc2[pl.ds(2 * row + 1, fin, stride=2), :] = jnp.where(flane < rest, a1, 0.0)
        return 0

    lax.fori_loop(0, n // fin, finish, 0)

    def collect(t, _):
        for k in (2 * t, 2 * t + 1):
            for p in range(peers):
                at = pl.ds(pl.multiple_of(ksp[p][0, k], 2), 2)
                pair(stg, p * slots + k)[...] = sc2[at, :]
        return 0

    lax.fori_loop(0, slots // 2, collect, 0)
    ntail = up(slots, per)

    many = 8

    def put(g, _):
        tails = []
        for v in range(many):
            p = g * many + v
            at = p * 2 * slots
            out[p, 0:slots, :] = stg[pl.ds(at, slots, stride=2), :]
            tails.append([stg[pl.ds(at + 2 * q + 1, ntail, stride=2 * per), :] for q in range(per)])
        tails = [[pltpu.roll(x, q * rest, axis=1) if q else x for q, x in enumerate(t)] for t in tails]
        for v, t in enumerate(tails):
            out[g * many + v, slots : slots + ntail, :] = sum(t[1:], t[0])
        return 0

    lax.fori_loop(0, peers // many, put, 0)


def pack(bnd, v2, stg, out, extra, *, peers, slots, per, rest):
    gather_rows(bnd, v2, stg, peers, slots)
    ntail = up(slots, per)
    blk = slots + ntail
    for k in range(slots):
        out[pl.ds(k, peers, stride=blk), :] = stg[pl.ds(2 * k, peers, stride=2 * slots), :]
    for j in range(ntail):
        tail = None
        for q in range(min(per, slots - j * per)):
            x = stg[pl.ds(2 * (j * per + q) + 1, peers, stride=2 * slots), :]
            x = pltpu.roll(x, q * rest, axis=1) if q else x
            tail = x if tail is None else tail + x
        if j == 0 and extra is not None:
            tail = tail + extra
        out[pl.ds(slots + j, peers, stride=blk), :] = tail


def errors_kernel(
    arr, recv, bnd_hbm, labk_hbm, t_hbm, e_hbm, out, stg, base2, v2, stgb, labk, kr, bnd, sems, sr, esem, *ksr,
    classes, per, n,
):
    rest = classes - L
    peers, blk, _ = arr.shape
    slots = recv.shape[2]
    ntail = up(slots, per)
    tlane = lanes(ntail)
    load = pltpu.make_async_copy(labk_hbm, labk, sems.at[0])
    load.start()
    bcopy = pltpu.make_async_copy(bnd_hbm.at[0], bnd, sems.at[1])
    bcopy.start()
    kr[:, 0:slots] = recv[0] * 2
    copies = fetch(kr, range(peers), ksr, sr)

    many = 8

    def unpack(g, _):
        tails = []
        for v in range(many):
            tail = arr[g * many + v, slots : slots + ntail, :]
            tails.append([pltpu.roll(tail, (L - q * rest) % L, axis=1) if q else tail for q in range(per)])
        for v in range(many):
            p = g * many + v
            at = p * 2 * slots
            for q, x in enumerate(tails[v]):
                stg[pl.ds(at + 2 * q + 1, ntail, stride=2 * per), :] = jnp.where(tlane < rest, x, 0.0)
            stg[pl.ds(at, slots, stride=2), :] = arr[p, 0:slots, :]
        return 0

    lax.fori_loop(0, peers // many, unpack, 0)

    for c in copies:
        c.wait()
    unroll = 2

    def spread(t, _):
        for v in range(unroll):
            k = t * unroll + v
            for p in range(peers):
                at = pl.ds(pl.multiple_of(ksr[p][0, k], 2), 2)
                base2[at, :] = pair(stg, p * slots + k)[...]
        return 0

    lax.fori_loop(0, slots // unroll, spread, 0)
    load.wait()

    chunk = 128
    lane = lanes(chunk)

    def error(i, _):
        row = pl.multiple_of(i * chunk, chunk)
        lab = labk[pl.ds(row, chunk), :]
        known = lab >= 0.0
        for h in range(2):
            rows = pl.ds(2 * row + h, chunk, stride=2)
            onehot = jnp.where(lab == (lane + h * L).astype(F32), 1.0, 0.0)
            b = base2[rows, :]
            v2[rows, :] = jnp.where(known, onehot - b, 0.0)
            t = jnp.where(known, onehot, b)
            base2[rows, :] = jnp.where(lane == L - 1, jnp.where(known, 0.0, 1.0), t) if h else t
        piece(i, 0).start()
        piece(i, 1).start()
        return 0

    def piece(i, w):
        rows = pl.ds(pl.multiple_of(2 * i * chunk, 2 * chunk), 2 * chunk)
        a, b = ((v2, e_hbm), (base2, t_hbm))[w]
        return pltpu.make_async_copy(a.at[rows, :], b.at[rows, :], esem.at[w, i])

    v2[pl.ds(2 * n, 16), :] = jnp.zeros((16, L), F32)
    lax.fori_loop(0, n // chunk, error, 0)
    pack((bcopy, bnd), v2, stgb, out, None, peers=peers, slots=bnd.shape[1], per=per, rest=rest)
    for i in range(n // chunk):
        piece(i, 0).wait()
        piece(i, 1).wait()


def tiles_kernel(tiles, cols, labels, mask, nh_hbm, nl_hbm, fh, fl, lab_hbm, cnt, nh, nl, labk, sems):
    blocks = labels.shape[0]
    halo = fh.shape[1] // L

    def body(b, _):
        rows = pl.ds(pl.multiple_of(b * L, L), L)
        for j in range(LOC_ROW):
            hi, lo = split(tiles[b * TILES_ROW + j])
            nh[rows, j * L : (j + 1) * L] = hi
            nl[rows, j * L : (j + 1) * L] = lo
        for q in range(halo):
            acc = jnp.zeros((L, L), F32)
            for j in range(LOC_ROW, TILES_ROW):
                hit = cols[b * TILES_ROW + j] == blocks + q
                acc = acc + jnp.where(hit, tiles[b * TILES_ROW + j], 0.0)
            hi, lo = split(acc)
            fh[rows, q * L : (q + 1) * L] = hi
            fl[rows, q * L : (q + 1) * L] = lo
        lab = jnp.where(mask[pl.ds(b, 1), :] > 0, labels[pl.ds(b, 1), :], -1).astype(F32)
        labk[rows, :] = jnp.broadcast_to(lab, (L, L)).T
        return 0

    lax.fori_loop(0, blocks, body, 0)
    pairs = ((nh, nh_hbm), (nl, nl_hbm), (labk, lab_hbm))
    saves = [pltpu.make_async_copy(a, b, sems.at[i]) for i, (a, b) in enumerate(pairs)]
    for c in saves:
        c.start()
    cnt[...] = jnp.zeros(cnt.shape, F32) + jnp.sum(mask[...].astype(F32))
    for c in saves:
        c.wait()


def near_kernel(v_hbm, e_hbm, nh_hbm, nl_hbm, cols, *refs, rate, classes, sums):
    if sums:
        cnt, part, tot, v2, e2, nh, nl, vh, vl, sems = refs
    else:
        part, v2, e2, nh, nl, vh, vl, sems = refs
    pairs = ((v_hbm, v2), (nh_hbm, nh), (nl_hbm, nl), (e_hbm, e2))
    loads = [pltpu.make_async_copy(a, b, sems.at[i]) for i, (a, b) in enumerate(pairs)]
    for c in loads:
        c.start()
    blocks = part.shape[0] // L
    loads[0].wait()

    def halve(b, _):
        rows = pl.ds(pl.multiple_of(b * L, L), L)
        for h in range(2):
            hi, lo = split(v2[pl.ds(b * 2 * L + h, L, stride=2), :])
            vh[rows, h * L : (h + 1) * L] = hi
            vl[rows, h * L : (h + 1) * L] = lo
        return 0

    lax.fori_loop(0, blocks, halve, 0)
    for c in loads[1:]:
        c.wait()

    def body(b, acc):
        rows = pl.ds(pl.multiple_of(b * L, L), L)
        at = [pl.ds(pl.multiple_of(cols[b * TILES_ROW + j] * L, L), L) for j in range(LOC_ROW)]
        bh = jnp.concatenate([vh[a, :] for a in at], 0)
        bl = jnp.concatenate([vl[a, :] for a in at], 0)
        a2 = dot(jnp.concatenate([nh[rows, :], nl[rows, :]], 0), bh)
        near = a2[:L] + a2[L:] + dot(nh[rows, :], bl)
        for h in range(2):
            ev = e2[pl.ds(b * 2 * L + h, L, stride=2), :]
            part[rows, h * L : (h + 1) * L] = (1.0 - rate) * ev + rate * near[:, h * L : (h + 1) * L]
            if sums:
                acc = acc + jnp.sum(jnp.abs(ev).reshape(L // 8, 8, L), 0)
        return acc

    acc = lax.fori_loop(0, blocks, body, jnp.zeros((8, L), F32))
    if sums:
        total = jnp.sum(acc) * (1.0 / classes)
        lane = lanes(8)
        tot[...] = jnp.where(lane == L - 2, total, jnp.where(lane == L - 1, cnt[...], 0.0))


def far_kernel(*refs, rate, classes, per, mode, peers, slots, n):
    rest = classes - L
    refs = list(refs)
    arr, fh, fl, part = refs[:4]
    refs = refs[4:]
    if mode != "last":
        bnd_hbm, bnd, bsem = refs.pop(0), refs.pop(), refs.pop()
        bcopy = pltpu.make_async_copy(bnd_hbm.at[0], bnd, bsem)
        bcopy.start()
    if mode == "sums":
        tot = refs.pop(0)
    if mode == "turn":
        t_hbm, t2, sems = refs.pop(0), refs.pop(), refs.pop()
        half = t2.shape[0] // 2
        loads = [
            pltpu.make_async_copy(t_hbm.at[pl.ds(i * half, half), :], t2.at[pl.ds(i * half, half), :], sems.at[i])
            for i in range(2)
        ]
        for c in loads:
            c.start()
    if mode == "last":
        out_hbm, hm, hr, out, osem = refs
    else:
        v_hbm, out, hm, hr, v2, stgb, vsem = refs
    ntail = up(slots, per)
    blk = slots + ntail
    tlane = lanes(peers)
    for k in range(slots):
        hm[pl.ds(k, peers, stride=slots), :] = arr[pl.ds(k, peers, stride=blk), :]
    for j in range(ntail):
        tail = arr[pl.ds(slots + j, peers, stride=blk), :]
        if j == 0 and mode == "turn":
            sums = jnp.sum(tail, axis=0, keepdims=True)
            sigma = sums[:, L - 2 : L - 1] / sums[:, L - 1 : L]
        for q in range(min(per, slots - j * per)):
            x = pltpu.roll(tail, (L - q * rest) % L, axis=1) if q else tail
            x = jnp.where(tlane < rest, x, 0.0)
            hr[pl.ds(j * per + q, peers, stride=slots), :] = x
    hh, hl = split(jnp.concatenate([hm[...], hr[...]], 1))

    chunk = n // (4 if mode == "last" else 2)
    lane = lanes(chunk)
    count = n // chunk

    def ship(i):
        cols = pl.ds(pl.multiple_of(i * chunk, chunk), chunk)
        return pltpu.make_async_copy(out.at[:, cols], out_hbm.at[:, cols], osem.at[i])

    parts = 6
    small = chunk // parts

    def piece(i):
        rows = pl.ds(pl.multiple_of(2 * i * small, 2 * small), 2 * small)
        return pltpu.make_async_copy(v2.at[rows, :], v_hbm.at[rows, :], vsem.at[i])

    if mode != "last":
        v2[pl.ds(2 * n, 16), :] = jnp.zeros((16, L), F32)

    def body(i, _):
        row = pl.multiple_of(i * chunk, chunk)
        rows = pl.ds(row, chunk)
        a2 = dot(jnp.concatenate([fh[rows, :], fl[rows, :]], 0), hh)
        far = a2[:chunk] + a2[chunk:] + dot(fh[rows, :], hl)
        v = part[rows, :] + rate * far
        if mode == "last":
            out[0:L, rows] = v[:, :L].T
            out[L:classes, rows] = v[:, L:].T[:rest]
            ship(i).start()
            return 0
        if mode == "turn":
            mag = jnp.abs(v)
            mag = jnp.sum(mag[:, :L] + mag[:, L:], -1, keepdims=True) * (1.0 / classes) + tiny
            hit = pl.ds(pl.multiple_of(i * half, half), half)
            pltpu.make_async_copy(t_hbm.at[hit, :], t2.at[hit, :], sems.at[i]).wait()
            free = t2[pl.ds(2 * row + 1, chunk, stride=2), :]
            scale = free[:, L - 1 : L] * sigma / mag
        for w in range(parts):
            own = slice(w * small, (w + 1) * small)
            for h in range(2):
                x = v[own, h * L : (h + 1) * L]
                rows2 = pl.ds(2 * (row + w * small) + h, small, stride=2)
                if mode == "turn":
                    x = t2[rows2, :] + scale[own] * x
                    x = jnp.where(lane[own] < rest, x, 0.0) if h else x
                v2[rows2, :] = x
            piece(i * parts + w).start()
        return 0

    lax.fori_loop(0, count, body, 0)
    if mode == "last":
        for i in range(count):
            ship(i).wait()
    else:
        extra = tot[0:1, :] if mode == "sums" else None
        pack((bcopy, bnd), v2, stgb, out, extra, peers=peers, slots=slots, per=per, rest=rest)
        for i in range(count * parts):
            piece(i).wait()


def call(kernel, outs, ins, args, scratch=(), vmem=0, flops=0, size=0, name=None, specs=None):
    if specs:
        place = {id(HB): pltpu.HBM, id(VO): pltpu.VMEM}
        outs = tuple(place.get(id(p), jax.ShapeDtypeStruct)(o.shape, o.dtype) for o, p in zip(outs, specs))
    args = [pltpu.with_memory_space_constraint(a, pltpu.HBM) if p is HB else a for a, p in zip(args, ins)]
    return pl.pallas_call(
        kernel,
        out_shape=outs,
        in_specs=ins,
        out_specs=specs or jax.tree.map(lambda _: VM, outs),
        scratch_shapes=list(scratch),
        compiler_params=pltpu.CompilerParams(vmem_limit_bytes=vmem),
        cost_estimate=pl.CostEstimate(flops=flops, bytes_accessed=size, transcendentals=0),
        name=name,
    )(*args)


def swap(x):
    return lax.all_to_all(x, "dom", split_axis=0, concat_axis=0, tiled=True)


def on_device(
    peers, hidden, bases, self_weight, coef, bias, edge_src, edge_dst, edge_rel, send_rows, recv_rows, labels,
    train_mask, bnd_rows, tiles, tile_cols,
):
    n, hdim = hidden.shape
    classes = self_weight.shape[1]
    nrel, nb = coef.shape
    rest = classes - L
    per = (L - 2) // rest
    slots = send_rows.shape[2]
    bnd = bnd_rows.shape[2]
    ne = edge_src.shape[0]
    halo = peers * bnd
    sds = jax.ShapeDtypeStruct
    state = sds((n, 2 * L), F32)
    half = sds((n, 2 * L), BF16)
    blocks = n // L

    dma = lambda k: pltpu.SemaphoreType.DMA((k,))
    blk = up(slots + up(slots, per), 8) * 8
    square = lambda x: x.reshape(-1, L)
    stage = pltpu.VMEM((2 * (peers * slots + 16), L), F32)
    rows2 = pltpu.VMEM((2 * n + 16, L), F32)
    sums = pltpu.VMEM((2 * nrel * n, L), F32)
    wide = (nb + 4) * L
    erows = ne // L
    bnd_rows = 2 * bnd_rows
    sent, _ = call(
        functools.partial(scores_kernel, classes=classes, slots=slots, per=per),
        (sds((peers, blk, L), F32), sds((2 * n, L), F32)),
        [HB, VM, VM, VM, SM, VM, VM, VM, VM],
        (hidden, bases.T, self_weight.T, bias.reshape(1, -1), coef)
        + (square(edge_src), square(edge_dst), square(edge_rel), send_rows),
        [pltpu.VMEM((n, hdim), BF16), pltpu.VMEM((wide, hdim), BF16)]
        + [pltpu.VMEM((n // 4, wide), F32)] * 2
        + [sums] * 5
        + [rows2, stage]
        + [pltpu.VMEM((erows, L), jnp.int32)] * 2
        + [pltpu.VMEM((peers, L), jnp.int32), pltpu.VMEM((2 * n, L), F32), dma(erows), dma(erows), dma(peers)]
        + [dma(2 + 4 * nrel)]
        + [pltpu.SMEM((1, L), jnp.int32)] * (2 * erows + peers),
        vmem=60 * MIB,
        name="scores",
        specs=(VM, HB),
    )
    arrived = swap(sent)
    spread = sds((2 * n, L), F32)
    flat2 = pltpu.VMEM((2 * n, L), F32)
    labv = pltpu.VMEM((n, L), F32)
    halfv = pltpu.VMEM((n, 2 * L), BF16)
    nh, nl, fh, fl, labk, cnt = call(
        tiles_kernel,
        (half, half, sds((n, halo), BF16), sds((n, halo), BF16), sds((n, L), F32), sds((8, L), F32)),
        [VM, SM, VM, VM],
        (tiles, tile_cols, square(labels), square(train_mask)),
        [halfv, halfv, labv, dma(3)],
        vmem=28 * MIB,
        flops=10**7,
        size=8 * 10**6,
        name="tiles",
        specs=(HB, HB, VM, VM, HB, VM),
    )
    lines = peers * (bnd + up(bnd, per))
    packed = sds((lines, L), F32)
    stageb = pltpu.VMEM((2 * halo, L), F32)
    bnds = pltpu.SMEM((peers, bnd), jnp.int32)
    base, v, out = call(
        functools.partial(errors_kernel, classes=classes, per=per, n=n),
        (spread, spread, packed),
        [VM, VM, HB, HB],
        (arrived, recv_rows, bnd_rows, labk),
        [stage, rows2, rows2, stageb, labv, pltpu.VMEM((peers, L), jnp.int32), bnds, dma(2), dma(peers)]
        + [pltpu.SemaphoreType.DMA((2, n // L))]
        + [pltpu.SMEM((1, L), jnp.int32)] * peers,
        vmem=28 * MIB,
        name="errors",
        specs=(HB, HB, VO),
    )
    e = v
    hscr = [pltpu.VMEM((halo, L), F32)] * 2
    for step in range(2 * ITERS):
        rate = correct_rate if step < ITERS else smooth_rate
        halos = swap(out.reshape(peers, 1, -1)).reshape(lines, L)
        sums = step == 0
        mode = "last" if step == 2 * ITERS - 1 else "turn" if step == ITERS - 1 else "sums" if step == ITERS - 2 else "step"
        got = call(
            functools.partial(near_kernel, rate=rate, classes=classes, sums=sums),
            (state, sds((8, L), F32)) if sums else (state,),
            [HB, HB, HB, HB, SM] + [VM] * sums,
            (v, e, nh, nl, tile_cols) + ((cnt,) if sums else ()),
            [flat2, flat2, halfv, halfv, halfv, halfv, dma(4)],
            vmem=24 * MIB,
            flops=10**9,
            size=8 * 10**6,
            name="near",
        )
        part = got[0]
        if sums:
            tot = got[1]
        far = functools.partial(
            far_kernel, rate=rate, classes=classes, per=per, mode=mode, peers=peers, slots=bnd, n=n
        )
        args, ins = (halos, fh, fl, part), [VM] * 4
        if mode == "last":
            scratch = hscr + [pltpu.VMEM((classes, n), F32), dma(4)]
            got = call(
                far, (sds((classes, n), F32),), ins, args, scratch, vmem=24 * MIB, name="far_last", specs=(HB,)
            )
            return got[0].T
        args, ins = args + (bnd_rows,), ins + [HB]
        scratch = hscr + [rows2, stageb, dma(n // L)]
        if mode == "sums":
            args, ins = args + (tot,), ins + [VM]
        if mode == "turn":
            args, ins = args + (base,), ins + [HB]
            scratch = scratch + [dma(2), flat2]
        scratch = scratch + [pltpu.SemaphoreType.DMA, bnds]
        v, out = call(
            far, (spread, packed), ins, args, scratch, vmem=24 * MIB, name="far_" + mode, specs=(HB, VO)
        )
        if mode == "turn":
            e = v


def solution(mesh):
    row = P("dom")
    in_specs = (
        P("dom", None), P(), P(), P(), P(), row, row, row, P("dom", None, None), P("dom", None, None), row, row,
        P("dom", None, None), P("dom", None, None), row,
    )
    return jax.shard_map(
        functools.partial(on_device, mesh.shape["dom"]),
        mesh=mesh,
        in_specs=in_specs,
        out_specs=P("dom", None),
        check_vma=False,
    )
```
